32 devices in a mesh: gx: 2 (over x), gy: 4 (over z), gz: 4 (over y, core).
Axes of the slice: x: 2, y: 2, z: 4, core: 2. Of those that a mesh axis runs over, the one named last changes fastest.
Arguments:
- source: float32 [32, 256, 512], P('gx', 'gy', 'gz'), may hold values from -5 to 5
- first_guess: float32 [32, 256, 512], P('gx', 'gy', 'gz'), may hold values from -5 to 5
- cell_classes: int32 [32, 256, 512], P('gx', 'gy', 'gz'), may hold values from 0 to 7
- class_table: float32 [8], replicated, may hold values from 0.2 to 5
Outputs:
- solution: float32 [32, 256, 512], P('gx', 'gy', 'gz')
- residual: float32 [32, 256, 512], P('gx', 'gy', 'gz')
The draws below stay inside these ranges and needn't reach their ends.
All inputs are finite; a program needn't handle non-finite values.
Results may differ from the reference program's by a relative error of at most 0.0003.
Values sent between devices are 32-bit elements; how exact they have to be, the bound alone decides.
No kernel may reach another device: no remote copies, remote signals or barrier semaphores. Data moves between devices by JAX's collectives and lax.ppermute only.
A program may use at most 192 MiB of HBM per device.

```python
import math
import jax
import jax.numpy as jnp
from jax import lax

LEVELS = 3
SWEEPS = 4
COARSE = 16
CLASSES = 8
NX = 32
NY = 256
NZ = 512


def draw_source(key, part):
    rough = jax.random.normal(key, (NX, NY, NZ), jnp.float32)
    return jnp.clip(rough, -5.0, 5.0)


def place_ends(entries, own_key, low, largest):
    place = [jax.random.randint(jax.random.fold_in(own_key, axis), (), 0, length) for axis, length in enumerate(entries.shape)]
    longest = entries.shape.index(max(entries.shape))
    neighbour = place[:longest] + [(place[longest] + 1) % entries.shape[longest]] + place[longest + 1:]
    return entries.at[tuple(place)].set(low).at[tuple(neighbour)].set(largest)


def shard_levels(own_key, extent, cuts, smallest, high):
    gain, own = 1.0, jax.random.fold_in(own_key, 6)
    for dim, parts in cuts:
        draws = jnp.exp(jax.random.uniform(jax.random.fold_in(own, dim), (parts,), jnp.float32, smallest / len(cuts), high / len(cuts)))
        gain = gain * jnp.repeat(draws, extent[dim] // parts).reshape([-1 if axis == dim else 1 for axis in range(len(extent))])
    return gain


def gaussian(rng, dims, scale, most, cuts=(), kind=jnp.bfloat16):
    array = jax.random.normal(rng, dims, jnp.float32) * scale
    if len(cuts) > 0:
        array = shard_levels(rng, dims, cuts, -0.22, 0.18) * array
    return jnp.clip(array, min=-most, max=most).astype(kind)


def setup_inputs(seed: int = 0) -> dict:
    keys = jax.random.split(jax.random.key(seed), 5)
    source = draw_source(jax.random.fold_in(keys[4], 71), 0)
    first_guess = gaussian(keys[1], (NX, NY, NZ), 1.0, 5.0, ((0, 2), (1, 4), (2, 4)), jnp.float32)
    cell_classes = place_ends(jax.random.randint(keys[2], (NX, NY, NZ), 0, CLASSES), jax.random.fold_in(keys[2], 1), 0, CLASSES - 1).astype(jnp.int32)
    class_table = jnp.clip(jnp.exp(jax.random.uniform(keys[3], (CLASSES,), jnp.float32, math.log(0.2), math.log(5.0))), 0.2, 5.0)
    return dict(source=source, first_guess=first_guess, cell_classes=cell_classes, class_table=class_table)


relax_weight = 0.85


def neighbor(padded, axis_dim, offset):
    window = [slice(1, -1), slice(1, -1), slice(1, -1)]
    window[axis_dim] = slice(1 + offset, padded.shape[axis_dim] - 1 + offset)
    return padded[tuple(window)]


def apply_padded(padded_u, padded_c, level_scale):
    center_u = padded_u[1:-1, 1:-1, 1:-1]
    center_c = padded_c[1:-1, 1:-1, 1:-1]
    stencil_sum = jnp.zeros_like(center_u)
    diagonal = jnp.zeros_like(center_u)
    for axis_dim in range(3):
        for offset in (-1, 1):
            face = 0.5 * (center_c + neighbor(padded_c, axis_dim, offset))
            stencil_sum = stencil_sum + face * (center_u - neighbor(padded_u, axis_dim, offset))
            diagonal = diagonal + face
    return level_scale * stencil_sum, level_scale * diagonal


def restrict(field):
    size_x, size_y, size_z = field.shape
    return field.reshape(size_x // 2, 2, size_y // 2, 2, size_z // 2, 2).mean(axis=(1, 3, 5))


def prolong(field):
    size_x, size_y, size_z = field.shape
    spread = jnp.broadcast_to(field[:, None, :, None, :, None], (size_x, 2, size_y, 2, size_z, 2))
    return spread.reshape(2 * size_x, 2 * size_y, 2 * size_z)


def sweep(values, rhs_field, coef_padded, level_scale):
    stencil_sum, diagonal = apply_padded(jnp.pad(values, 1), coef_padded, level_scale)
    return values + relax_weight * (rhs_field - stencil_sum) / diagonal


def residual_of(values, rhs_field, coef_padded, level_scale):
    stencil_sum, diagonal = apply_padded(jnp.pad(values, 1), coef_padded, level_scale)
    return rhs_field - stencil_sum


def reference(source, first_guess, cell_classes, class_table):
    coef_list = [class_table[cell_classes]]
    for level_id in range(LEVELS):
        coef_list.append(restrict(coef_list[-1]))
    padded_list = [jnp.pad(coef_value, 1) for coef_value in coef_list]
    rhs_list = [source]
    iterate_list = []
    values = first_guess
    for level_id in range(LEVELS):
        level_scale = 0.25 ** level_id
        if level_id > 0:
            values = jnp.zeros_like(rhs_list[level_id])
        for sweep_id in range(SWEEPS):
            values = sweep(values, rhs_list[level_id], padded_list[level_id], level_scale)
        iterate_list.append(values)
        rhs_list.append(restrict(residual_of(values, rhs_list[level_id], padded_list[level_id], level_scale)))
    coarse_scale = 0.25 ** LEVELS
    coarse_rhs = rhs_list[LEVELS]
    coarse_pad = padded_list[LEVELS]

    def coarse_step(sweep_id, values):
        return sweep(values, coarse_rhs, coarse_pad, coarse_scale)

    correction = lax.fori_loop(0, COARSE, coarse_step, jnp.zeros_like(coarse_rhs))
    for level_id in reversed(range(LEVELS)):
        level_scale = 0.25 ** level_id
        values = iterate_list[level_id] + prolong(correction)
        for sweep_id in range(SWEEPS):
            values = sweep(values, rhs_list[level_id], padded_list[level_id], level_scale)
        correction = values
    final = residual_of(correction, source, padded_list[0], 1.0)
    return correction, final
```

```python
import functools

import jax
import jax.numpy as jnp
from jax import lax
from jax.experimental import pallas as pl
from jax.experimental.pallas import tpu as pltpu
from jax.sharding import PartitionSpec as P

LEVELS = 3
SWEEPS = 4
COARSE = 16
CLASSES = 8
W = 0.85
HX = 5
F32 = jnp.float32
HI = lax.Precision.HIGHEST


def pairs_even(n):
    return [(i, i ^ 1) for i in range(n)]


def pairs_odd(n):
    out = []
    for i in range(1, n - 1, 2):
        out += [(i, i + 1), (i + 1, i)]
    return out


def swap_even(x, axis):
    return lax.ppermute(x, axis, pairs_even(lax.axis_size(axis)))


def swap_odd(x, axis):
    return lax.ppermute(x, axis, pairs_odd(lax.axis_size(axis)))


def swap_xor(x, axis, m):
    return lax.ppermute(x, axis, [(i, i ^ m) for i in range(lax.axis_size(axis))])


def even(axis):
    return lax.rem(lax.axis_index(axis), 2) == 0


def call(body, outs, *args, scratch=(), smem=()):
    specs = [
        pl.BlockSpec(memory_space=pltpu.SMEM if i in smem else pltpu.VMEM) for i in range(len(args))
    ]
    shapes = [jax.ShapeDtypeStruct(s, F32) for s in outs]
    return pl.pallas_call(
        body,
        out_shape=shapes,
        in_specs=specs,
        out_specs=[pl.BlockSpec(memory_space=pltpu.VMEM) for _ in outs],
        scratch_shapes=[pltpu.VMEM(s, F32) for s in scratch],
        name=getattr(body, "__name__", None) or body.func.__name__,
    )(*args)


def lanes(rows=8):
    return lax.broadcasted_iota(jnp.int32, (rows, 128), 1)


def rot(x, shift):
    if isinstance(shift, int):
        shift = shift % 128
        if shift == 0:
            return x
    else:
        shift = lax.rem(shift + 1024, 128)
    return pltpu.roll(x, shift, 1)


def face_start(axis, total, width, want_even):
    hi = even(axis) if want_even else jnp.logical_not(even(axis))
    return jnp.where(hi, total - width, 0)


def start_kernel(nsx, src, guess, cls, table, c_out, y_a, y_b, *x_out):
    nx, ny, _ = src.shape

    def plane(x, _):
        k = cls[x]
        acc = jnp.full(k.shape, table[0], F32)
        for i in range(1, CLASSES):
            acc = jnp.where(k == i, table[i], acc)
        c_out[x] = acc
        return 0

    lax.fori_loop(0, nx, plane, 0)
    for s in range(nsx):
        p5 = face_start("gx", nx, HX, s == 0)
        p4 = face_start("gx", nx, HX - 1, s == 0)
        for f in range(HX):
            x_out[s][f] = c_out[p5 + f]
            x_out[s][HX + f] = guess[p5 + f]
        for f in range(HX - 1):
            x_out[s][2 * HX + f] = src[p4 + f]
    for ref, flag in ((y_a, True), (y_b, False)):
        r = pl.multiple_of(face_start("gy", ny, 8, flag), 8)
        for k, a in enumerate((c_out, guess, src)):
            ref[k * nx : (k + 1) * nx] = a[:, pl.ds(r, 8), :]


def zpack_kernel(na, *refs):
    arrs = refs[:na]
    r_a, r_b, z_a, z_b = refs[na:]
    nx, ny, _ = arrs[0].shape
    ey, ez = even("gy"), even("gz")
    group = lanes() // 8
    for k in range(na):
        for t in range(ny // 8 + 2):
            right = jnp.zeros((8, 128), F32)
            left = jnp.zeros((8, 128), F32)
            for x in range(nx):
                if t == 0:
                    v = jnp.where(ey, r_b[k * nx + x], r_a[k * nx + x])
                elif t == ny // 8 + 1:
                    v = jnp.where(ey, r_a[k * nx + x], r_b[k * nx + x])
                else:
                    v = arrs[k][x, (t - 1) * 8 : t * 8]
                right = jnp.where(group == x, rot(v, 8 * x + 8), right)
                left = jnp.where(group == x, rot(v, 8 * x), left)
            z_a[k, t * 8 : t * 8 + 8] = jnp.where(ez, right, left)
            z_b[k, t * 8 : t * 8 + 8] = jnp.where(ez, left, right)


def face_list(na):
    widths = (HX, HX, HX - 1)
    return [(k, f, widths[k]) for k in range(na) for f in range(widths[k])]


def xframe_kernel(na, nx, nsx, r_a, r_b, z_a, z_b, *x_out):
    ey, ez = even("gy"), even("gz")
    rows = z_a.shape[1]
    lane = lanes()
    planes = face_list(na)
    for s in range(nsx):
        for j, (k, f, w) in enumerate(planes):
            p = face_start("gx", nx, w, s == 0) + f
            va, vb = r_a[k * nx + p], r_b[k * nx + p]
            x_out[s][j * 16 : j * 16 + 8] = jnp.where(ey, vb, va)
            x_out[s][j * 16 + 8 : j * 16 + 16] = jnp.where(ey, va, vb)
        base = len(planes) * 16
        for strip in range(-(-len(planes) // 8)):
            for t in range(rows // 8):
                acc = jnp.zeros((8, 128), F32)
                for j in range(strip * 8, min(strip * 8 + 8, len(planes))):
                    k, f, w = planes[j]
                    g = j % 8
                    p = face_start("gx", nx, w, s == 0) + f
                    za, zb = z_a[k, t * 8 : t * 8 + 8], z_b[k, t * 8 : t * 8 + 8]
                    right = jnp.where(ez, za, zb)
                    left = jnp.where(ez, zb, za)
                    acc = jnp.where(lane // 8 == 2 * g, rot(left, 16 * g - 8 * p), acc)
                    acc = jnp.where(lane // 8 == 2 * g + 1, rot(right, 16 * g + 8 - 8 * p), acc)
                r0 = base + strip * rows + t * 8
                x_out[s][r0 : r0 + 8] = acc


def own_offset(nsx):
    return HX * lax.axis_index("gx") if nsx == 1 else HX


def assemble(nsx, k, planes, m, h, own, r_a, r_b, z_a, z_b, x1, x2):
    nx, ny, _ = own.shape
    off = 1 + own_offset(nsx)
    ey, ez = even("gy"), even("gz")
    lane = lanes()
    kk = planes[0]
    tiles = ny // 8 + 2
    is_left, is_right = lane >= 120, lane < 8

    for x in range(nx):
        va, vb = r_a[kk * nx + x], r_b[kk * nx + x]
        m[off + x, 8:16] = jnp.where(ey, vb, va)
        m[off + x, 16 : 16 + ny] = own[x]
        m[off + x, 16 + ny : 24 + ny] = jnp.where(ey, va, vb)
    for t in range(tiles):
        za, zb = z_a[kk, t * 8 : t * 8 + 8], z_b[kk, t * 8 : t * 8 + 8]
        right = jnp.where(ez, za, zb)
        left = jnp.where(ez, zb, za)
        for x in range(nx):
            v = jnp.where(is_right, rot(right, -8 * x), 0.0)
            h[off + x, 8 + t * 8 : 16 + t * 8] = jnp.where(is_left, rot(left, 120 - 8 * x), v)
    for s in range(nsx):
        hi = even("gx") if s == 0 else jnp.logical_not(even("gx"))
        for j, k_, f, w, base in planes[1]:
            p = off + jnp.where(hi, nx, -w) + f
            m[p, 8:16] = x2[s][j * 16 : j * 16 + 8]
            m[p, 16 : 16 + ny] = x1[s][j]
            m[p, 16 + ny : 24 + ny] = x2[s][j * 16 + 8 : j * 16 + 16]
            for t in range(tiles):
                r0 = base + (j // 8) * tiles * 8 + t * 8
                v = x2[s][r0 : r0 + 8]
                g = j % 8
                a = jnp.where(is_left, rot(v, 120 - 16 * g), 0.0)
                h[p, 8 + t * 8 : 16 + t * 8] = jnp.where(is_right, rot(v, -16 * g - 8), a)


def plane_map(na, k):
    ps = face_list(na)
    base = len(ps) * 16
    return (k, [(j, kk, f, w, base) for j, (kk, f, w) in enumerate(ps) if kk == k])


def zshift(vals, wrap=True):
    lo = lanes(vals[0].shape[0])
    down = [rot(v, 1) for v in vals]
    up = [rot(v, -1) for v in vals]
    if len(vals) == 2:
        first, last = lo == 0, lo == 127
        down = [jnp.where(first, down[1 - t], down[t]) for t in (0, 1)]
        up = [jnp.where(last, up[1 - t], up[t]) for t in (0, 1)]
    return down, up


def neighbours(refs, x, r, n):
    vals = [ref[x, pl.ds(8 + r, n)] for ref in refs]
    down, up = zshift(vals)
    out = []
    for t, ref in enumerate(refs):
        out.append(
            (
                ref[x - 1, pl.ds(8 + r, n)],
                ref[x + 1, pl.ds(8 + r, n)],
                ref[x, pl.ds(7 + r, n)],
                ref[x, pl.ds(9 + r, n)],
                down[t],
                up[t],
            )
        )
    return vals, out


def zero(*refs):
    for ref in refs:

        def one(x, _):
            ref[x] = jnp.zeros(ref.shape[1:], F32)
            return 0

        lax.fori_loop(0, ref.shape[0], one, 0)


def chunks(rows, n=8):
    return range(0, rows, n)


def build_coef(c, b, a, q, d, scale, full_lanes):
    nx, rows = c[0].shape[0] - 2, c[0].shape[1] - 16

    def plane(x, _):
        for r in chunks(rows):
            vals, nb = neighbours(c, x, r, 8)
            lane = lanes()
            for t in range(len(c)):
                six = list(nb[t])
                if full_lanes:
                    six[4] = jnp.where(lane == 0, 0.0, six[4])
                    six[5] = jnp.where(lane == 127, 0.0, six[5])
                total = 6.0 * vals[t] + (((six[0] + six[1]) + (six[2] + six[3])) + (six[4] + six[5]))
                inside = vals[t] > 0.0
                g = jnp.where(inside, W / jnp.where(inside, total, 1.0), 0.0)
                rw = pl.ds(r, 8)
                for j in range(6):
                    face = g * (vals[t] + six[j])
                    if full_lanes and j == 4:
                        face = jnp.where(lane == 0, 0.0, face)
                    if full_lanes and j == 5:
                        face = jnp.where(lane == 127, 0.0, face)
                    a[j][t][x - 1, rw] = face
                q[t][x - 1, rw] = g * ((2.0 / scale) * b[t][x, pl.ds(8 + r, 8)])
                if d is not None:
                    d[t][x - 1, rw] = total * (0.5 * scale / W)
        return 0

    lax.fori_loop(1, nx + 1, plane, 0)


def weighted(a, vals, nb, t, x, rw):
    s = a[0][t][x - 1, rw] * nb[t][0] + a[1][t][x - 1, rw] * nb[t][1]
    u = a[2][t][x - 1, rw] * nb[t][2] + a[3][t][x - 1, rw] * nb[t][3]
    w = a[4][t][x - 1, rw] * nb[t][4] + a[5][t][x - 1, rw] * nb[t][5]
    return (s + u) + w


def sweep(src, dst, a, q, unroll=False):
    nx, rows = src[0].shape[0] - 2, src[0].shape[1] - 16

    def plane(x, _):
        for r in chunks(rows):
            vals, nb = neighbours(src, x, r, 8)
            rw = pl.ds(r, 8)
            for t in range(len(src)):
                dst[t][x, pl.ds(8 + r, 8)] = ((1.0 - W) * vals[t] + q[t][x - 1, rw]) + weighted(
                    a, vals, nb, t, x, rw
                )
        return 0

    if unroll:
        for x in range(1, nx + 1):
            plane(x, 0)
    else:
        lax.fori_loop(1, nx + 1, plane, 0)


def copy_q(dst, q):
    def plane(x, _):
        for t in range(len(q)):
            dst[t][x + 1, 8 : 8 + q[t].shape[1]] = q[t][x]
        return 0

    lax.fori_loop(0, q[0].shape[0], plane, 0)


def residual_rows(v, b, a, d, x, r, n=8):
    vals, nb = neighbours(v, x, r, n)
    rw = pl.ds(r, n)
    return b - d[0][x - 1, rw] * (W * vals[0] - weighted(a, vals, nb, 0, x, rw))


def pick(shift_out, cols, limit):
    i = lax.broadcasted_iota(jnp.int32, (128, 128), 0)
    o = lax.broadcasted_iota(jnp.int32, (128, 128), 1)
    return jnp.where((i // 2 == o - shift_out) & (i < limit), 0.125, 0.0).astype(F32)


def dot(a, b):
    return lax.dot_general(a, b, (((1,), (0,)), ((), ())), precision=HI, preferred_element_type=F32)


def half_rows(ref, r0, n):
    return ref[pl.ds(r0, n // 2, stride=2)] + ref[pl.ds(r0 + 1, n // 2, stride=2)]


def fine_arrays(xp, rows):
    pad, bare = (xp + 2, rows + 16, 128), (xp, rows, 128)
    return [pad] * 8 + [bare] * 16


def split_fine(s):
    two = lambda i: (s[i], s[i + 1])
    return two(0), two(2), two(4), two(6), [two(8 + 2 * j) for j in range(6)], two(20), two(22)


def load_fine(nsx, na, which, refs_own, r, target):
    for k, own, (m, h) in zip(which, refs_own, target):
        assemble(nsx, k, plane_map(na, k), m, h, own, r[0], r[1], r[2], r[3], r[4], r[5])


def fine_down_kernel(nsx, *refs):
    c_own, guess, src, r_a, r_b, z_a, z_b = refs[:7]
    x1, x2 = refs[7 : 7 + nsx], refs[7 + nsx : 7 + 2 * nsx]
    n = 7 + 2 * nsx
    v_out, bc, y_a, y_b = refs[n : n + 4]
    xf = refs[n + 4 : n + 4 + nsx]
    s = refs[n + 4 + nsx :]
    c, b, v, v2, a, q, d = split_fine(s[:24])
    pair = s[24]
    nx, ny, _ = src.shape
    off = 1 + own_offset(nsx)
    zero(*c, *b, *v, *v2)
    load_fine(nsx, 3, (0, 1, 2), (c_own, guess, src), (r_a, r_b, z_a, z_b, x1, x2), (c, v, b))
    build_coef(c, b, a, q, d, 1.0, False)

    def two(_, carry):
        sweep(v, v2, a, q)
        sweep(v2, v, a, q)
        return carry

    lax.fori_loop(0, SWEEPS // 2, two, 0)
    pb, pc = pick(0, 64, 128), pick(64, 64, 128)

    def coarse(i, _):
        x = off + 2 * i
        for r in chunks(ny):
            r0 = residual_rows(v, src[2 * i, pl.ds(r, 8)], a, d, x, 8 + r)
            r1 = residual_rows(v, src[2 * i + 1, pl.ds(r, 8)], a, d, x + 1, 8 + r)
            pair[0, pl.ds(r, 8)] = r0 + r1
            pair[1, pl.ds(r, 8)] = c_own[2 * i, pl.ds(r, 8)] + c_own[2 * i + 1, pl.ds(r, 8)]
            v_out[2 * i, pl.ds(r, 8)] = v[0][x, pl.ds(16 + r, 8)]
            v_out[2 * i + 1, pl.ds(r, 8)] = v[0][x + 1, pl.ds(16 + r, 8)]
        bc[i] = dot(half_rows(pair.at[0], 0, ny), pb) + dot(half_rows(pair.at[1], 0, ny), pc)
        return 0

    lax.fori_loop(0, nx // 2, coarse, 0)
    for k in range(nsx):
        p5 = face_start("gx", nx, HX, k == 0)
        for f in range(HX):
            xf[k][f] = v_out[p5 + f]
    for ref, flag in ((y_a, True), (y_b, False)):
        r = pl.multiple_of(face_start("gy", ny, 8, flag), 8)
        ref[...] = v_out[:, pl.ds(r, 8), :]


def mid_y_kernel(gathered, *refs):
    if gathered:
        full_in, full, y_a, y_b = refs
        full[...] = full_in[...]
    else:
        own, other, full, y_a, y_b = refs
        n = own.shape[0]
        ix = lax.axis_index("gx")
        full[pl.ds(n * ix, n)] = own[...]
        full[pl.ds(n - n * ix, n)] = other[...]
    ny = full.shape[1]
    for ref, flag in ((y_a, True), (y_b, False)):
        r = pl.multiple_of(face_start("gy", ny, 16, flag), 8)
        ref[...] = full[:, pl.ds(r, 16), :]


def mid_rows(full, r_a, r_b, x, t, ny):
    ey = even("gy")
    if t < 2:
        return jnp.where(ey, r_b[x, t * 8 : t * 8 + 8], r_a[x, t * 8 : t * 8 + 8])
    if t >= ny // 8 + 2:
        u = t - ny // 8 - 2
        return jnp.where(ey, r_a[x, u * 8 : u * 8 + 8], r_b[x, u * 8 : u * 8 + 8])
    return full[x, (t - 2) * 8 : (t - 1) * 8]


def mid_z_kernel(full, r_a, r_b, z_a, z_b):
    nx, ny, _ = full.shape
    ez = even("gz")
    slot = lax.rem(lanes(), 64) // 16
    for t in range(ny // 8 + 4):

        def group(s, _):
            right = jnp.zeros((8, 128), F32)
            left = jnp.zeros((8, 128), F32)
            for g in range(4):
                v = mid_rows(full, r_a, r_b, 4 * s + g, t, ny)
                right = jnp.where(slot == g, rot(v, 16 * g - 48), right)
                left = jnp.where(slot == g, rot(v, 16 * g), left)
            z_a[s, t * 8 : t * 8 + 8] = jnp.where(ez, right, left)
            z_b[s, t * 8 : t * 8 + 8] = jnp.where(ez, left, right)
            return 0

        lax.fori_loop(0, nx // 4, group, 0)


def mid_down_kernel(full, r_a, r_b, z_a, z_b, v_out, b_out, c_out, bc, *s):
    c, b, v, v2 = [(s[i],) for i in range(4)]
    a = [(s[4 + j],) for j in range(6)]
    q, d = (s[10],), (s[11],)
    pair = s[12]
    nx, ny, _ = full.shape
    ez = even("gz")
    lane = lanes()
    own, right_l, left_l = lane < 64, (lane >= 64) & (lane < 80), lane >= 112
    zero(c[0], b[0], v[0], v2[0])
    for t in range(ny // 8 + 4):

        def group(s_, _):
            za, zb = z_a[s_, t * 8 : t * 8 + 8], z_b[s_, t * 8 : t * 8 + 8]
            right = jnp.where(ez, za, zb)
            left = jnp.where(ez, zb, za)
            for g in range(4):
                x = 4 * s_ + g
                m = mid_rows(full, r_a, r_b, x, t, ny)
                for ref, o in ((b[0], 0), (c[0], 64)):
                    e = jnp.where(own, rot(m, -o), 0.0)
                    e = jnp.where(right_l, rot(right, 64 - o - 16 * g), e)
                    e = jnp.where(left_l, rot(left, 112 - o - 16 * g), e)
                    ref[x + 1, 8 + t * 8 : 16 + t * 8] = e
            return 0

        lax.fori_loop(0, nx // 4, group, 0)
    build_coef(c, b, a, q, d, 0.25, False)
    copy_q(v, q)
    sweep(v, v2, a, q)
    sweep(v2, v, a, q)
    sweep(v, v2, a, q)
    v = v2
    half = nx // 4
    mats = [(pick(o, 32, 64), pick(o + 32, 32, 64)) for o in (0, 64)]

    def coarse(i, _):
        acc = jnp.zeros((ny // 2, 128), F32)
        for side in (0, 1):
            x = 1 + 2 * (i + side * half)
            for r in chunks(ny):
                rp = pl.ds(24 + r, 8)
                r0 = residual_rows(v, b[0][x, rp], a, d, x, 16 + r)
                r1 = residual_rows(v, b[0][x + 1, rp], a, d, x + 1, 16 + r)
                pair[0, pl.ds(r, 8)] = r0 + r1
                pair[1, pl.ds(r, 8)] = c[0][x, rp] + c[0][x + 1, rp]
            acc = acc + dot(half_rows(pair.at[0], 0, ny), mats[side][0])
            acc = acc + dot(half_rows(pair.at[1], 0, ny), mats[side][1])
        bc[i] = acc
        return 0

    lax.fori_loop(0, half, coarse, 0)
    v_out[...] = v[0][...]
    b_out[...] = b[0][...]
    c_out[...] = c[0][...]


def spread(src, dst, mats, c, x_src, x_dst, r_src, n, r_dst, tmp, sets=False):
    for t, mat in enumerate(mats):
        p = dot(src, mat)
        tmp[t, pl.ds(0, n, stride=2)] = p
        tmp[t, pl.ds(1, n, stride=2)] = p
    for xd in x_dst:
        for t in range(len(mats)):
            for r in chunks(2 * n):
                rr = pl.ds(r_dst + r, 8)
                dst[t][xd, rr] = dst[t][xd, rr] + jnp.where(
                    c[t][xd, rr] > 0.0, tmp[t, pl.ds(r, 8)], 0.0
                )


def select_mat(fn):
    i = lax.broadcasted_iota(jnp.int32, (128, 128), 0)
    o = lax.broadcasted_iota(jnp.int32, (128, 128), 1)
    return jnp.where(i == fn(o), 1.0, 0.0).astype(F32)


def coarse_kernel(gy, gz, blocks, v1_in, b1, c1, v1_out, *s):
    c2, b2, v2, w2 = [(s[i],) for i in range(4)]
    a2 = [(s[4 + j],) for j in range(6)]
    q2, d2 = (s[10],), (s[11],)
    c3, b3, v3, w3 = [(s[12 + i],) for i in range(4)]
    a3 = [(s[16 + j],) for j in range(6)]
    q3 = (s[22],)
    v1, w1 = (s[23],), (s[24],)
    a1 = [(s[25 + j],) for j in range(6)]
    q1 = (s[31],)
    pair, tmp = s[32], s[33]
    iy, iz = lax.axis_index("gy"), lax.axis_index("gz")
    half, yb, _ = blocks.shape[1:]
    lane = lanes(yb)
    zero(c2[0], b2[0], v2[0], w2[0], c3[0], b3[0], v3[0], w3[0], w1[0])
    nx2 = 2 * half
    for jy in range(gy):
        ky = lax.bitwise_xor(jnp.int32(jy), iy)

        def plane(i, _):
            for o in (0, 64):
                for ref, oo in ((b2[0], o), (c2[0], o + 32)):
                    acc = jnp.zeros((yb, 128), F32)
                    for jz in range(gz):
                        kz = lax.bitwise_xor(jnp.int32(jz), iz)
                        idx = ((kz % 2) * (gz // 2) + kz // 2) * gy + ky
                        acc = jnp.where(lane // 32 == jz, rot(blocks[idx, i], 32 * jz - oo), acc)
                    ref[1 + i + (half if o else 0), 8 + yb * jy : 8 + yb * (jy + 1)] = acc
            return 0

        lax.fori_loop(0, half, plane, 0)
    build_coef(c2, b2, a2, q2, d2, 0.0625, True)
    copy_q(v2, q2)
    sweep(v2, w2, a2, q2)
    sweep(w2, v2, a2, q2)
    sweep(v2, w2, a2, q2)
    ny = yb * gy
    mat = pick(0, 64, 128)

    def coarse(i, _):
        x = 1 + 2 * i
        for r in chunks(ny):
            rp = pl.ds(8 + r, 8)
            r0 = residual_rows(w2, b2[0][x, rp], a2, d2, x, r)
            r1 = residual_rows(w2, b2[0][x + 1, rp], a2, d2, x + 1, r)
            pair[0, pl.ds(r, 8)] = r0 + r1
            pair[1, pl.ds(r, 8)] = c2[0][x, rp] + c2[0][x + 1, rp]
        b3[0][1 + i, 8 : 8 + ny // 2] = dot(half_rows(pair.at[0], 0, ny), mat)
        c3[0][1 + i, 8 : 8 + ny // 2] = dot(half_rows(pair.at[1], 0, ny), mat)
        return 0

    lax.fori_loop(0, nx2 // 2, coarse, 0)
    small = nx2 <= 8
    build_coef(c3, b3, a3, q3, None, 0.015625, False)
    copy_q(v3, q3)
    sweep(v3, w3, a3, q3, small)

    def two(_, carry):
        sweep(w3, v3, a3, q3, small)
        sweep(v3, w3, a3, q3, small)
        return carry

    lax.fori_loop(0, (COARSE - 2) // 2, two, 0)
    up = select_mat(lambda o: o // 2)

    def up2(i, _):
        spread(w3[0][1 + i, 8 : 8 + ny // 2], w2, [up], c2, None, (1 + 2 * i, 2 + 2 * i), None, ny // 2, 8, tmp)
        return 0

    lax.fori_loop(0, nx2 // 2, up2, 0)

    def two2(_, carry):
        sweep(w2, v2, a2, q2)
        sweep(v2, w2, a2, q2)
        return carry

    lax.fori_loop(0, SWEEPS // 2, two2, 0)
    build_coef((c1,), (b1,), a1, q1, None, 0.25, False)
    v1[0][...] = v1_in[...]
    rows1 = v1[0].shape[1] - 16
    up = select_mat(lambda o: jnp.where(o < 80, o // 2, jnp.where(o >= 112, (o + 128) // 2, -1)))
    start = pl.multiple_of(yb * iy, 8)

    def up1(i, _):
        par = rot(w2[0][1 + i, pl.ds(start, rows1 // 2)], -32 * iz)
        spread(par, v1, [up], (c1,), None, (1 + 2 * i, 2 + 2 * i), None, rows1 // 2, 8, tmp)
        return 0

    lax.fori_loop(0, nx2, up1, 0)

    def two1(_, carry):
        sweep(v1, w1, a1, q1)
        sweep(w1, v1, a1, q1)
        return carry

    lax.fori_loop(0, SWEEPS // 2, two1, 0)
    v1_out[...] = v1[0][...]


def fine_up_kernel(nsx, *refs):
    c_own, v_own, src, r_a, r_b, z_a, z_b = refs[:7]
    x1, x2 = refs[7 : 7 + nsx], refs[7 + nsx : 7 + 2 * nsx]
    n = 7 + 2 * nsx
    vr_a, vr_b, vz_a, vz_b = refs[n : n + 4]
    vx1, vx2 = refs[n + 4 : n + 4 + nsx], refs[n + 4 + nsx : n + 4 + 2 * nsx]
    n = n + 4 + 2 * nsx
    v1 = refs[n]
    sol, res = refs[n + 1 : n + 3]
    s = refs[n + 3 :]
    c, b, v, v2, a, q, d = split_fine(s[:24])
    tmp = s[24]
    nx, ny, _ = src.shape
    off = 1 + own_offset(nsx)
    zero(*c, *b, *v, *v2)
    load_fine(nsx, 3, (0, 2), (c_own, src), (r_a, r_b, z_a, z_b, x1, x2), (c, b))
    load_fine(nsx, 1, (0,), (v_own,), (vr_a, vr_b, vz_a, vz_b, vx1, vx2), (v,))
    build_coef(c, b, a, q, d, 1.0, False)
    up_m = select_mat(lambda o: o // 2)
    up_h = select_mat(
        lambda o: jnp.where(o < 8, 64 + o // 2, jnp.where(o >= 120, (o + 128) // 2, -1))
    )
    nc = v1.shape[0] - 2
    ix = lax.axis_index("gx")
    xp = v[0].shape[0] - 2
    rows = ny + 16

    def up(p, _):
        x = jnp.clip(lax.shift_right_arithmetic(nx * ix + p - off, 1), 0, nc - 1)
        par = v1[1 + x, 20 : 20 + rows // 2]
        spread(par, v, [up_m, up_h], c, None, (p,), None, rows // 2, 8, tmp)
        return 0

    lax.fori_loop(1, xp + 1, up, 0)

    def two(_, carry):
        sweep(v, v2, a, q)
        sweep(v2, v, a, q)
        return carry

    lax.fori_loop(0, SWEEPS // 2, two, 0)

    def out(x, _):
        for r in chunks(ny):
            res[x, pl.ds(r, 8)] = residual_rows(v, src[x, pl.ds(r, 8)], a, d, off + x, 8 + r)
            sol[x, pl.ds(r, 8)] = v[0][off + x, pl.ds(16 + r, 8)]
        return 0

    lax.fori_loop(0, nx, out, 0)


def named(fn, *args):
    out = functools.partial(fn, *args)
    out.__name__ = fn.__name__
    return out


def exchange_rest(na, arrs, y_a, y_b, nsx):
    nx, ny, _ = arrs[0].shape
    rows = ny + 16
    r_a, r_b = swap_even(y_a, "gy"), swap_odd(y_b, "gy")
    z_a, z_b = call(named(zpack_kernel, na), [(na, rows, 128)] * 2, *arrs, r_a, r_b)
    z_a, z_b = swap_even(z_a, "gz"), swap_odd(z_b, "gz")
    count = len(face_list(na))
    size = count * 16 + -(-count // 8) * rows
    xs = call(named(xframe_kernel, na, nx, nsx), [(size, 128)] * nsx, r_a, r_b, z_a, z_b)
    x2 = swap_x(xs)
    return (r_a, r_b, z_a, z_b), x2


def swap_x(xs):
    out = [swap_even(xs[0], "gx")]
    if len(xs) > 1:
        out.append(swap_odd(xs[1], "gx"))
    return out


def body(source, first_guess, cell_classes, class_table):
    nx, ny, _ = source.shape
    gx, gy, gz = (lax.axis_size(n) for n in ("gx", "gy", "gz"))
    nsx = 1 if gx == 2 else 2
    xp = nx + nsx * HX
    rows = ny + 16
    full = (nx, ny, 128)

    out = call(
        named(start_kernel, nsx),
        [full, (3 * nx, 8, 128), (3 * nx, 8, 128)] + [(3 * HX - 1, ny, 128)] * nsx,
        source, first_guess, cell_classes, class_table,
        smem=(3,),
    )
    c_own, y_a, y_b, xs = out[0], out[1], out[2], out[3:]
    x1 = swap_x(xs)
    rec, x2 = exchange_rest(3, (c_own, first_guess, source), y_a, y_b, nsx)
    out = call(
        named(fine_down_kernel, nsx),
        [full, (nx // 2, ny // 2, 128), (nx, 8, 128), (nx, 8, 128)] + [(HX, ny, 128)] * nsx,
        c_own, first_guess, source, *rec, *x1, *x2,
        scratch=fine_arrays(xp, rows) + [(2, ny, 128)],
    )
    v0, bc1, vy_a, vy_b, vxs = out[0], out[1], out[2], out[3], out[4:]

    n1 = gx * nx // 2
    ny1 = ny // 2
    outs = [(n1, ny1, 128), (n1, 16, 128), (n1, 16, 128)]
    if gx == 2:
        f1, y_a, y_b = call(named(mid_y_kernel, False), outs, bc1, swap_even(bc1, "gx"))
    else:
        f1, y_a, y_b = call(
            named(mid_y_kernel, True), outs, lax.all_gather(bc1, "gx", axis=0, tiled=True)
        )
    r_a, r_b = swap_even(y_a, "gy"), swap_odd(y_b, "gy")
    rows1 = ny1 + 32
    z_a, z_b = call(mid_z_kernel, [(n1 // 4, rows1, 128)] * 2, f1, r_a, r_b)
    z_a, z_b = swap_even(z_a, "gz"), swap_odd(z_b, "gz")
    pad1, bare1 = (n1 + 2, rows1 + 16, 128), (n1, rows1, 128)
    v1, b1, c1, bc2 = call(
        mid_down_kernel,
        [pad1] * 3 + [(n1 // 4, ny1 // 2, 128)],
        f1, r_a, r_b, z_a, z_b,
        scratch=[pad1] * 4 + [bare1] * 8 + [(2, ny1, 128)],
    )

    got = jnp.stack([bc2] + [swap_xor(bc2, "gy", m) for m in range(1, gy)])
    bit = gz // 2
    while bit:
        got = jnp.concatenate([got, swap_xor(got, "gz", bit)])
        bit //= 2

    vx1 = swap_x(vxs)
    vrec, vx2 = exchange_rest(1, (v0,), vy_a, vy_b, nsx)

    n2, ny2 = n1 // 2, gy * ny1 // 2
    n3, ny3 = n2 // 2, ny2 // 2
    pad2, bare2 = (n2 + 2, ny2 + 16, 128), (n2, ny2, 128)
    pad3, bare3 = (n3 + 2, ny3 + 16, 128), (n3, ny3, 128)
    (v1,) = call(
        named(coarse_kernel, gy, gz),
        [pad1],
        got, v1, b1, c1,
        scratch=[pad2] * 4 + [bare2] * 8 + [pad3] * 4 + [bare3] * 7 + [pad1] * 2 + [bare1] * 7
        + [(2, ny2, 128), (1, max(rows1, ny2), 128)],
    )
    sol, res = call(
        named(fine_up_kernel, nsx),
        [full, full],
        c_own, v0, source, *rec, *x1, *x2, *vrec, *vx1, *vx2, v1,
        scratch=fine_arrays(xp, rows) + [(2, rows, 128)],
    )
    return sol, res


def solution(mesh):
    spec = P("gx", "gy", "gz")
    return jax.shard_map(
        body,
        mesh=mesh,
        in_specs=(spec, spec, spec, P()),
        out_specs=(spec, spec),
        check_vma=False,
    )
```

```python
import functools

import math
import jax
import jax.numpy as jnp
from jax import lax
from jax.experimental import pallas as pl
from jax.experimental.pallas import tpu as pltpu
from jax.sharding import PartitionSpec as P

LEVELS = 3
SWEEPS = 4
COARSE = 16
CLASSES = 8
W = 0.85
HX = 5
F32 = jnp.float32
HI = lax.Precision.HIGHEST


def pairs_even(n):
    return [(i, i ^ 1) for i in range(n)]


def pairs_odd(n):
    out = []
    for i in range(1, n - 1, 2):
        out += [(i, i + 1), (i + 1, i)]
    return out


def swap_even(x, axis):
    return lax.ppermute(x, axis, pairs_even(lax.axis_size(axis)))


def swap_odd(x, axis):
    return lax.ppermute(x, axis, pairs_odd(lax.axis_size(axis)))


def swap_xor(x, axis, m):
    return lax.ppermute(x, axis, [(i, i ^ m) for i in range(lax.axis_size(axis))])


def even(axis):
    return lax.rem(lax.axis_index(axis), 2) == 0


def call(body, outs, *args, scratch=(), smem=()):
    specs = [
        pl.BlockSpec(memory_space=pltpu.SMEM if i in smem else pltpu.VMEM) for i in range(len(args))
    ]
    shapes = [pltpu.VMEM(s, F32) for s in outs]
    args = [pltpu.with_memory_space_constraint(a, pltpu.VMEM) if (i not in smem and a.dtype == F32) else a for i, a in enumerate(args)]
    limit = 4 * sum(math.prod(s) for s in scratch) + 6 * 2**20
    return pl.pallas_call(
        body,
        out_shape=shapes,
        in_specs=specs,
        out_specs=[pl.BlockSpec(memory_space=pltpu.VMEM) for _ in outs],
        scratch_shapes=[pltpu.VMEM(s, F32) for s in scratch],
        name=getattr(body, "__name__", None) or body.func.__name__,
        compiler_params=pltpu.CompilerParams(vmem_limit_bytes=limit),
    )(*args)


def lanes(rows=8):
    return lax.broadcasted_iota(jnp.int32, (rows, 128), 1)


def rot(x, shift):
    if isinstance(shift, int):
        shift = shift % 128
        if shift == 0:
            return x
    else:
        shift = lax.rem(shift + 1024, 128)
    return pltpu.roll(x, shift, 1)


def face_start(axis, total, width, want_even):
    hi = even(axis) if want_even else jnp.logical_not(even(axis))
    return jnp.where(hi, total - width, 0)


def start_kernel(nsx, src, guess, cls, table, c_out, y_a, y_b, *x_out):
    nx, ny, _ = src.shape

    def plane(x, _):
        k = cls[x]
        acc = jnp.full(k.shape, table[0], F32)
        for i in range(1, CLASSES):
            acc = jnp.where(k == i, table[i], acc)
        c_out[x] = acc
        return 0

    lax.fori_loop(0, nx, plane, 0)
    for s in range(nsx):
        p5 = face_start("gx", nx, HX, s == 0)
        p4 = face_start("gx", nx, HX - 1, s == 0)
        for f in range(HX):
            x_out[s][f] = c_out[p5 + f]
            x_out[s][HX + f] = guess[p5 + f]
        for f in range(HX - 1):
            x_out[s][2 * HX + f] = src[p4 + f]
    for ref, flag in ((y_a, True), (y_b, False)):
        r = pl.multiple_of(face_start("gy", ny, 8, flag), 8)
        for k, a in enumerate((c_out, guess, src)):
            ref[k * nx : (k + 1) * nx] = a[:, pl.ds(r, 8), :]


def zpack_kernel(na, *refs):
    arrs = refs[:na]
    r_a, r_b, z_a, z_b = refs[na:]
    nx, ny, _ = arrs[0].shape
    ey, ez = even("gy"), even("gz")
    group = lanes() // 8
    for k in range(na):
        for t in range(ny // 8 + 2):
            right = jnp.zeros((8, 128), F32)
            left = jnp.zeros((8, 128), F32)
            for x in range(nx):
                if t == 0:
                    v = jnp.where(ey, r_b[k * nx + x], r_a[k * nx + x])
                elif t == ny // 8 + 1:
                    v = jnp.where(ey, r_a[k * nx + x], r_b[k * nx + x])
                else:
                    v = arrs[k][x, (t - 1) * 8 : t * 8]
                right = jnp.where(group == x, rot(v, 8 * x + 8), right)
                left = jnp.where(group == x, rot(v, 8 * x), left)
            z_a[k, t * 8 : t * 8 + 8] = jnp.where(ez, right, left)
            z_b[k, t * 8 : t * 8 + 8] = jnp.where(ez, left, right)


def face_list(na):
    widths = (HX, HX, HX - 1)
    return [(k, f, widths[k]) for k in range(na) for f in range(widths[k])]


def xframe_kernel(na, nx, nsx, r_a, r_b, z_a, z_b, *x_out):
    ey, ez = even("gy"), even("gz")
    rows = z_a.shape[1]
    lane = lanes()
    planes = face_list(na)
    for s in range(nsx):
        for j, (k, f, w) in enumerate(planes):
            p = face_start("gx", nx, w, s == 0) + f
            va, vb = r_a[k * nx + p], r_b[k * nx + p]
            x_out[s][j * 16 : j * 16 + 8] = jnp.where(ey, vb, va)
            x_out[s][j * 16 + 8 : j * 16 + 16] = jnp.where(ey, va, vb)
        base = len(planes) * 16
        for strip in range(-(-len(planes) // 8)):
            for t in range(rows // 8):
                acc = jnp.zeros((8, 128), F32)
                for j in range(strip * 8, min(strip * 8 + 8, len(planes))):
                    k, f, w = planes[j]
                    g = j % 8
                    p = face_start("gx", nx, w, s == 0) + f
                    za, zb = z_a[k, t * 8 : t * 8 + 8], z_b[k, t * 8 : t * 8 + 8]
                    right = jnp.where(ez, za, zb)
                    left = jnp.where(ez, zb, za)
                    acc = jnp.where(lane // 8 == 2 * g, rot(left, 16 * g - 8 * p), acc)
                    acc = jnp.where(lane // 8 == 2 * g + 1, rot(right, 16 * g + 8 - 8 * p), acc)
                r0 = base + strip * rows + t * 8
                x_out[s][r0 : r0 + 8] = acc


def own_offset(nsx):
    return HX * lax.axis_index("gx") if nsx == 1 else HX


def assemble(nsx, k, planes, m, h, own, r_a, r_b, z_a, z_b, x1, x2):
    nx, ny, _ = own.shape
    off = 1 + own_offset(nsx)
    ey, ez = even("gy"), even("gz")
    lane = lanes()
    kk = planes[0]
    tiles = ny // 8 + 2
    is_left, is_right = lane >= 120, lane < 8

    for x in range(nx):
        va, vb = r_a[kk * nx + x], r_b[kk * nx + x]
        m[off + x, 8:16] = jnp.where(ey, vb, va)
        m[off + x, 16 : 16 + ny] = own[x]
        m[off + x, 16 + ny : 24 + ny] = jnp.where(ey, va, vb)
    for t in range(tiles):
        za, zb = z_a[kk, t * 8 : t * 8 + 8], z_b[kk, t * 8 : t * 8 + 8]
        right = jnp.where(ez, za, zb)
        left = jnp.where(ez, zb, za)
        for x in range(nx):
            v = jnp.where(is_right, rot(right, -8 * x), 0.0)
            h[off + x, 8 + t * 8 : 16 + t * 8] = jnp.where(is_left, rot(left, 120 - 8 * x), v)
    for s in range(nsx):
        hi = even("gx") if s == 0 else jnp.logical_not(even("gx"))
        for j, k_, f, w, base in planes[1]:
            p = off + jnp.where(hi, nx, -w) + f
            m[p, 8:16] = x2[s][j * 16 : j * 16 + 8]
            m[p, 16 : 16 + ny] = x1[s][j]
            m[p, 16 + ny : 24 + ny] = x2[s][j * 16 + 8 : j * 16 + 16]
            for t in range(tiles):
                r0 = base + (j // 8) * tiles * 8 + t * 8
                v = x2[s][r0 : r0 + 8]
                g = j % 8
                a = jnp.where(is_left, rot(v, 120 - 16 * g), 0.0)
                h[p, 8 + t * 8 : 16 + t * 8] = jnp.where(is_right, rot(v, -16 * g - 8), a)


def plane_map(na, k):
    ps = face_list(na)
    base = len(ps) * 16
    return (k, [(j, kk, f, w, base) for j, (kk, f, w) in enumerate(ps) if kk == k])


def zshift(vals, wrap=True):
    lo = lanes(vals[0].shape[0])
    down = [rot(v, 1) for v in vals]
    up = [rot(v, -1) for v in vals]
    if len(vals) == 2:
        first, last = lo == 0, lo == 127
        down = [jnp.where(first, down[1 - t], down[t]) for t in (0, 1)]
        up = [jnp.where(last, up[1 - t], up[t]) for t in (0, 1)]
    return down, up


def neighbours(refs, x, r, n):
    vals = [ref[x, pl.ds(8 + r, n)] for ref in refs]
    down, up = zshift(vals)
    out = []
    for t, ref in enumerate(refs):
        out.append(
            (
                ref[x - 1, pl.ds(8 + r, n)],
                ref[x + 1, pl.ds(8 + r, n)],
                ref[x, pl.ds(7 + r, n)],
                ref[x, pl.ds(9 + r, n)],
                down[t],
                up[t],
            )
        )
    return vals, out


def zero(*refs):
    for ref in refs:

        def one(x, _):
            ref[x] = jnp.zeros(ref.shape[1:], F32)
            return 0

        lax.fori_loop(0, ref.shape[0], one, 0)


def chunks(rows, n=8):
    return range(0, rows, n)


def build_coef(c, b, a, q, d, scale, full_lanes):
    nx, rows = c[0].shape[0] - 2, c[0].shape[1] - 16

    def plane(x, _):
        for r in chunks(rows):
            vals, nb = neighbours(c, x, r, 8)
            lane = lanes()
            for t in range(len(c)):
                six = list(nb[t])
                if full_lanes:
                    six[4] = jnp.where(lane == 0, 0.0, six[4])
                    six[5] = jnp.where(lane == 127, 0.0, six[5])
                total = 6.0 * vals[t] + (((six[0] + six[1]) + (six[2] + six[3])) + (six[4] + six[5]))
                inside = vals[t] > 0.0
                g = jnp.where(inside, W / jnp.where(inside, total, 1.0), 0.0)
                rw = pl.ds(r, 8)
                for j in range(6):
                    face = g * (vals[t] + six[j])
                    if full_lanes and j == 4:
                        face = jnp.where(lane == 0, 0.0, face)
                    if full_lanes and j == 5:
                        face = jnp.where(lane == 127, 0.0, face)
                    a[j][t][x - 1, rw] = face
                q[t][x - 1, rw] = g * ((2.0 / scale) * b[t][x, pl.ds(8 + r, 8)])
                if d is not None:
                    d[t][x - 1, rw] = total * (0.5 * scale / W)
        return 0

    lax.fori_loop(1, nx + 1, plane, 0)


def weighted(a, vals, nb, t, x, rw):
    s = a[0][t][x - 1, rw] * nb[t][0] + a[1][t][x - 1, rw] * nb[t][1]
    u = a[2][t][x - 1, rw] * nb[t][2] + a[3][t][x - 1, rw] * nb[t][3]
    w = a[4][t][x - 1, rw] * nb[t][4] + a[5][t][x - 1, rw] * nb[t][5]
    return (s + u) + w


def sweep(src, dst, a, q, unroll=False):
    nx, rows = src[0].shape[0] - 2, src[0].shape[1] - 16

    def plane(x, _):
        for r in chunks(rows):
            vals, nb = neighbours(src, x, r, 8)
            rw = pl.ds(r, 8)
            for t in range(len(src)):
                dst[t][x, pl.ds(8 + r, 8)] = ((1.0 - W) * vals[t] + q[t][x - 1, rw]) + weighted(
                    a, vals, nb, t, x, rw
                )
        return 0

    if unroll:
        for x in range(1, nx + 1):
            plane(x, 0)
    else:
        lax.fori_loop(1, nx + 1, plane, 0)


def copy_q(dst, q):
    def plane(x, _):
        for t in range(len(q)):
            dst[t][x + 1, 8 : 8 + q[t].shape[1]] = q[t][x]
        return 0

    lax.fori_loop(0, q[0].shape[0], plane, 0)


def residual_rows(v, b, a, d, x, r, n=8):
    vals, nb = neighbours(v, x, r, n)
    rw = pl.ds(r, n)
    return b - d[0][x - 1, rw] * (W * vals[0] - weighted(a, vals, nb, 0, x, rw))


def pick(shift_out, cols, limit):
    i = lax.broadcasted_iota(jnp.int32, (128, 128), 0)
    o = lax.broadcasted_iota(jnp.int32, (128, 128), 1)
    return jnp.where((i // 2 == o - shift_out) & (i < limit), 0.125, 0.0).astype(F32)


def dot(a, b):
    return lax.dot_general(a, b, (((1,), (0,)), ((), ())), precision=HI, preferred_element_type=F32)


def half_rows(ref, r0, n):
    return ref[pl.ds(r0, n // 2, stride=2)] + ref[pl.ds(r0 + 1, n // 2, stride=2)]


def fine_arrays(xp, rows):
    pad, bare = (xp + 2, rows + 16, 128), (xp, rows, 128)
    return [pad] * 8 + [bare] * 16


def split_fine(s):
    two = lambda i: (s[i], s[i + 1])
    return two(0), two(2), two(4), two(6), [two(8 + 2 * j) for j in range(6)], two(20), two(22)


def load_fine(nsx, na, which, refs_own, r, target):
    for k, own, (m, h) in zip(which, refs_own, target):
        assemble(nsx, k, plane_map(na, k), m, h, own, r[0], r[1], r[2], r[3], r[4], r[5])


def fine_down_kernel(nsx, *refs):
    c_own, guess, src, r_a, r_b, z_a, z_b = refs[:7]
    x1, x2 = refs[7 : 7 + nsx], refs[7 + nsx : 7 + 2 * nsx]
    n = 7 + 2 * nsx
    v_out, bc, y_a, y_b = refs[n : n + 4]
    xf = refs[n + 4 : n + 4 + nsx]
    s = refs[n + 4 + nsx :]
    c, b, v, v2, a, q, d = split_fine(s[:24])
    pair = s[24]
    nx, ny, _ = src.shape
    off = 1 + own_offset(nsx)
    zero(*c, *b, *v, *v2)
    load_fine(nsx, 3, (0, 1, 2), (c_own, guess, src), (r_a, r_b, z_a, z_b, x1, x2), (c, v, b))
    build_coef(c, b, a, q, d, 1.0, False)

    def two(_, carry):
        sweep(v, v2, a, q)
        sweep(v2, v, a, q)
        return carry

    lax.fori_loop(0, SWEEPS // 2, two, 0)
    pb, pc = pick(0, 64, 128), pick(64, 64, 128)

    def coarse(i, _):
        x = off + 2 * i
        for r in chunks(ny):
            r0 = residual_rows(v, src[2 * i, pl.ds(r, 8)], a, d, x, 8 + r)
            r1 = residual_rows(v, src[2 * i + 1, pl.ds(r, 8)], a, d, x + 1, 8 + r)
            pair[0, pl.ds(r, 8)] = r0 + r1
            pair[1, pl.ds(r, 8)] = c_own[2 * i, pl.ds(r, 8)] + c_own[2 * i + 1, pl.ds(r, 8)]
            v_out[2 * i, pl.ds(r, 8)] = v[0][x, pl.ds(16 + r, 8)]
            v_out[2 * i + 1, pl.ds(r, 8)] = v[0][x + 1, pl.ds(16 + r, 8)]
        bc[i] = dot(half_rows(pair.at[0], 0, ny), pb) + dot(half_rows(pair.at[1], 0, ny), pc)
        return 0

    lax.fori_loop(0, nx // 2, coarse, 0)
    for k in range(nsx):
        p5 = face_start("gx", nx, HX, k == 0)
        for f in range(HX):
            xf[k][f] = v_out[p5 + f]
    for ref, flag in ((y_a, True), (y_b, False)):
        r = pl.multiple_of(face_start("gy", ny, 8, flag), 8)
        ref[...] = v_out[:, pl.ds(r, 8), :]


def mid_y_kernel(gathered, *refs):
    if gathered:
        full_in, full, y_a, y_b = refs
        full[...] = full_in[...]
    else:
        own, other, full, y_a, y_b = refs
        n = own.shape[0]
        ix = lax.axis_index("gx")
        full[pl.ds(n * ix, n)] = own[...]
        full[pl.ds(n - n * ix, n)] = other[...]
    ny = full.shape[1]
    for ref, flag in ((y_a, True), (y_b, False)):
        r = pl.multiple_of(face_start("gy", ny, 16, flag), 8)
        ref[...] = full[:, pl.ds(r, 16), :]


def mid_rows(full, r_a, r_b, x, t, ny):
    ey = even("gy")
    if t < 2:
        return jnp.where(ey, r_b[x, t * 8 : t * 8 + 8], r_a[x, t * 8 : t * 8 + 8])
    if t >= ny // 8 + 2:
        u = t - ny // 8 - 2
        return jnp.where(ey, r_a[x, u * 8 : u * 8 + 8], r_b[x, u * 8 : u * 8 + 8])
    return full[x, (t - 2) * 8 : (t - 1) * 8]


def mid_z_kernel(full, r_a, r_b, z_a, z_b):
    nx, ny, _ = full.shape
    ez = even("gz")
    slot = lax.rem(lanes(), 64) // 16
    for t in range(ny // 8 + 4):

        def group(s, _):
            right = jnp.zeros((8, 128), F32)
            left = jnp.zeros((8, 128), F32)
            for g in range(4):
                v = mid_rows(full, r_a, r_b, 4 * s + g, t, ny)
                right = jnp.where(slot == g, rot(v, 16 * g - 48), right)
                left = jnp.where(slot == g, rot(v, 16 * g), left)
            z_a[s, t * 8 : t * 8 + 8] = jnp.where(ez, right, left)
            z_b[s, t * 8 : t * 8 + 8] = jnp.where(ez, left, right)
            return 0

        lax.fori_loop(0, nx // 4, group, 0)


def mid_down_kernel(full, r_a, r_b, z_a, z_b, v_out, b_out, c_out, bc, *s):
    c, b, v, v2 = [(s[i],) for i in range(4)]
    a = [(s[4 + j],) for j in range(6)]
    q, d = (s[10],), (s[11],)
    pair = s[12]
    nx, ny, _ = full.shape
    ez = even("gz")
    lane = lanes()
    own, right_l, left_l = lane < 64, (lane >= 64) & (lane < 80), lane >= 112
    zero(c[0], b[0], v[0], v2[0])
    for t in range(ny // 8 + 4):

        def group(s_, _):
            za, zb = z_a[s_, t * 8 : t * 8 + 8], z_b[s_, t * 8 : t * 8 + 8]
            right = jnp.where(ez, za, zb)
            left = jnp.where(ez, zb, za)
            for g in range(4):
                x = 4 * s_ + g
                m = mid_rows(full, r_a, r_b, x, t, ny)
                for ref, o in ((b[0], 0), (c[0], 64)):
                    e = jnp.where(own, rot(m, -o), 0.0)
                    e = jnp.where(right_l, rot(right, 64 - o - 16 * g), e)
                    e = jnp.where(left_l, rot(left, 112 - o - 16 * g), e)
                    ref[x + 1, 8 + t * 8 : 16 + t * 8] = e
            return 0

        lax.fori_loop(0, nx // 4, group, 0)
    build_coef(c, b, a, q, d, 0.25, False)
    copy_q(v, q)
    sweep(v, v2, a, q)
    sweep(v2, v, a, q)
    sweep(v, v2, a, q)
    v = v2
    half = nx // 4
    mats = [(pick(o, 32, 64), pick(o + 32, 32, 64)) for o in (0, 64)]

    def coarse(i, _):
        acc = jnp.zeros((ny // 2, 128), F32)
        for side in (0, 1):
            x = 1 + 2 * (i + side * half)
            for r in chunks(ny):
                rp = pl.ds(24 + r, 8)
                r0 = residual_rows(v, b[0][x, rp], a, d, x, 16 + r)
                r1 = residual_rows(v, b[0][x + 1, rp], a, d, x + 1, 16 + r)
                pair[0, pl.ds(r, 8)] = r0 + r1
                pair[1, pl.ds(r, 8)] = c[0][x, rp] + c[0][x + 1, rp]
            acc = acc + dot(half_rows(pair.at[0], 0, ny), mats[side][0])
            acc = acc + dot(half_rows(pair.at[1], 0, ny), mats[side][1])
        bc[i] = acc
        return 0

    lax.fori_loop(0, half, coarse, 0)
    v_out[...] = v[0][...]
    b_out[...] = b[0][...]
    c_out[...] = c[0][...]


def spread(src, dst, mats, c, x_src, x_dst, r_src, n, r_dst, tmp, sets=False):
    for t, mat in enumerate(mats):
        p = dot(src, mat)
        tmp[t, pl.ds(0, n, stride=2)] = p
        tmp[t, pl.ds(1, n, stride=2)] = p
    for xd in x_dst:
        for t in range(len(mats)):
            for r in chunks(2 * n):
                rr = pl.ds(r_dst + r, 8)
                dst[t][xd, rr] = dst[t][xd, rr] + jnp.where(
                    c[t][xd, rr] > 0.0, tmp[t, pl.ds(r, 8)], 0.0
                )


def select_mat(fn):
    i = lax.broadcasted_iota(jnp.int32, (128, 128), 0)
    o = lax.broadcasted_iota(jnp.int32, (128, 128), 1)
    return jnp.where(i == fn(o), 1.0, 0.0).astype(F32)


def coarse_kernel(gy, gz, blocks, v1_in, b1, c1, v1_out, *s):
    c2, b2, v2, w2 = [(s[i],) for i in range(4)]
    a2 = [(s[4 + j],) for j in range(6)]
    q2, d2 = (s[10],), (s[11],)
    c3, b3, v3, w3 = [(s[12 + i],) for i in range(4)]
    a3 = [(s[16 + j],) for j in range(6)]
    q3 = (s[22],)
    v1, w1 = (s[23],), (s[24],)
    a1 = [(s[25 + j],) for j in range(6)]
    q1 = (s[31],)
    pair, tmp = s[32], s[33]
    iy, iz = lax.axis_index("gy"), lax.axis_index("gz")
    half, yb, _ = blocks.shape[1:]
    lane = lanes(yb)
    zero(c2[0], b2[0], v2[0], w2[0], c3[0], b3[0], v3[0], w3[0], w1[0])
    nx2 = 2 * half
    for jy in range(gy):
        ky = lax.bitwise_xor(jnp.int32(jy), iy)

        def plane(i, _):
            for o in (0, 64):
                for ref, oo in ((b2[0], o), (c2[0], o + 32)):
                    acc = jnp.zeros((yb, 128), F32)
                    for jz in range(gz):
                        kz = lax.bitwise_xor(jnp.int32(jz), iz)
                        idx = ((kz % 2) * (gz // 2) + kz // 2) * gy + ky
                        acc = jnp.where(lane // 32 == jz, rot(blocks[idx, i], 32 * jz - oo), acc)
                    ref[1 + i + (half if o else 0), 8 + yb * jy : 8 + yb * (jy + 1)] = acc
            return 0

        lax.fori_loop(0, half, plane, 0)
    build_coef(c2, b2, a2, q2, d2, 0.0625, True)
    copy_q(v2, q2)
    sweep(v2, w2, a2, q2)
    sweep(w2, v2, a2, q2)
    sweep(v2, w2, a2, q2)
    ny = yb * gy
    mat = pick(0, 64, 128)

    def coarse(i, _):
        x = 1 + 2 * i
        for r in chunks(ny):
            rp = pl.ds(8 + r, 8)
            r0 = residual_rows(w2, b2[0][x, rp], a2, d2, x, r)
            r1 = residual_rows(w2, b2[0][x + 1, rp], a2, d2, x + 1, r)
            pair[0, pl.ds(r, 8)] = r0 + r1
            pair[1, pl.ds(r, 8)] = c2[0][x, rp] + c2[0][x + 1, rp]
        b3[0][1 + i, 8 : 8 + ny // 2] = dot(half_rows(pair.at[0], 0, ny), mat)
        c3[0][1 + i, 8 : 8 + ny // 2] = dot(half_rows(pair.at[1], 0, ny), mat)
        return 0

    lax.fori_loop(0, nx2 // 2, coarse, 0)
    small = nx2 <= 8
    build_coef(c3, b3, a3, q3, None, 0.015625, False)
    copy_q(v3, q3)
    sweep(v3, w3, a3, q3, small)

    def two(_, carry):
        sweep(w3, v3, a3, q3, small)
        sweep(v3, w3, a3, q3, small)
        return carry

    lax.fori_loop(0, (COARSE - 2) // 2, two, 0)
    up = select_mat(lambda o: o // 2)

    def up2(i, _):
        spread(w3[0][1 + i, 8 : 8 + ny // 2], w2, [up], c2, None, (1 + 2 * i, 2 + 2 * i), None, ny // 2, 8, tmp)
        return 0

    lax.fori_loop(0, nx2 // 2, up2, 0)

    def two2(_, carry):
        sweep(w2, v2, a2, q2)
        sweep(v2, w2, a2, q2)
        return carry

    lax.fori_loop(0, SWEEPS // 2, two2, 0)
    build_coef((c1,), (b1,), a1, q1, None, 0.25, False)
    v1[0][...] = v1_in[...]
    rows1 = v1[0].shape[1] - 16
    up = select_mat(lambda o: jnp.where(o < 80, o // 2, jnp.where(o >= 112, (o + 128) // 2, -1)))
    start = pl.multiple_of(yb * iy, 8)

    def up1(i, _):
        par = rot(w2[0][1 + i, pl.ds(start, rows1 // 2)], -32 * iz)
        spread(par, v1, [up], (c1,), None, (1 + 2 * i, 2 + 2 * i), None, rows1 // 2, 8, tmp)
        return 0

    lax.fori_loop(0, nx2, up1, 0)

    def two1(_, carry):
        sweep(v1, w1, a1, q1)
        sweep(w1, v1, a1, q1)
        return carry

    lax.fori_loop(0, SWEEPS // 2, two1, 0)
    v1_out[...] = v1[0][...]


def fine_up_kernel(nsx, *refs):
    c_own, v_own, src, r_a, r_b, z_a, z_b = refs[:7]
    x1, x2 = refs[7 : 7 + nsx], refs[7 + nsx : 7 + 2 * nsx]
    n = 7 + 2 * nsx
    vr_a, vr_b, vz_a, vz_b = refs[n : n + 4]
    vx1, vx2 = refs[n + 4 : n + 4 + nsx], refs[n + 4 + nsx : n + 4 + 2 * nsx]
    n = n + 4 + 2 * nsx
    v1 = refs[n]
    sol, res = refs[n + 1 : n + 3]
    s = refs[n + 3 :]
    c, b, v, v2, a, q, d = split_fine(s[:24])
    tmp = s[24]
    nx, ny, _ = src.shape
    off = 1 + own_offset(nsx)
    zero(*c, *b, *v, *v2)
    load_fine(nsx, 3, (0, 2), (c_own, src), (r_a, r_b, z_a, z_b, x1, x2), (c, b))
    load_fine(nsx, 1, (0,), (v_own,), (vr_a, vr_b, vz_a, vz_b, vx1, vx2), (v,))
    build_coef(c, b, a, q, d, 1.0, False)
    up_m = select_mat(lambda o: o // 2)
    up_h = select_mat(
        lambda o: jnp.where(o < 8, 64 + o // 2, jnp.where(o >= 120, (o + 128) // 2, -1))
    )
    nc = v1.shape[0] - 2
    ix = lax.axis_index("gx")
    xp = v[0].shape[0] - 2
    rows = ny + 16

    def up(p, _):
        x = jnp.clip(lax.shift_right_arithmetic(nx * ix + p - off, 1), 0, nc - 1)
        par = v1[1 + x, 20 : 20 + rows // 2]
        spread(par, v, [up_m, up_h], c, None, (p,), None, rows // 2, 8, tmp)
        return 0

    lax.fori_loop(1, xp + 1, up, 0)

    def two(_, carry):
        sweep(v, v2, a, q)
        sweep(v2, v, a, q)
        return carry

    lax.fori_loop(0, SWEEPS // 2, two, 0)

    def out(x, _):
        for r in chunks(ny):
            res[x, pl.ds(r, 8)] = residual_rows(v, src[x, pl.ds(r, 8)], a, d, off + x, 8 + r)
            sol[x, pl.ds(r, 8)] = v[0][off + x, pl.ds(16 + r, 8)]
        return 0

    lax.fori_loop(0, nx, out, 0)


def named(fn, *args):
    out = functools.partial(fn, *args)
    out.__name__ = fn.__name__
    return out


def exchange_rest(na, arrs, y_a, y_b, nsx):
    nx, ny, _ = arrs[0].shape
    rows = ny + 16
    r_a, r_b = swap_even(y_a, "gy"), swap_odd(y_b, "gy")
    z_a, z_b = call(named(zpack_kernel, na), [(na, rows, 128)] * 2, *arrs, r_a, r_b)
    z_a, z_b = swap_even(z_a, "gz"), swap_odd(z_b, "gz")
    count = len(face_list(na))
    size = count * 16 + -(-count // 8) * rows
    xs = call(named(xframe_kernel, na, nx, nsx), [(size, 128)] * nsx, r_a, r_b, z_a, z_b)
    x2 = swap_x(xs)
    return (r_a, r_b, z_a, z_b), x2


def swap_x(xs):
    out = [swap_even(xs[0], "gx")]
    if len(xs) > 1:
        out.append(swap_odd(xs[1], "gx"))
    return out


def body(source, first_guess, cell_classes, class_table):
    nx, ny, _ = source.shape
    gx, gy, gz = (lax.axis_size(n) for n in ("gx", "gy", "gz"))
    nsx = 1 if gx == 2 else 2
    xp = nx + nsx * HX
    rows = ny + 16
    full = (nx, ny, 128)

    out = call(
        named(start_kernel, nsx),
        [full, (3 * nx, 8, 128), (3 * nx, 8, 128)] + [(3 * HX - 1, ny, 128)] * nsx,
        source, first_guess, cell_classes, class_table,
        smem=(3,),
    )
    c_own, y_a, y_b, xs = out[0], out[1], out[2], out[3:]
    x1 = swap_x(xs)
    rec, x2 = exchange_rest(3, (c_own, first_guess, source), y_a, y_b, nsx)
    out = call(
        named(fine_down_kernel, nsx),
        [full, (nx // 2, ny // 2, 128), (nx, 8, 128), (nx, 8, 128)] + [(HX, ny, 128)] * nsx,
        c_own, first_guess, source, *rec, *x1, *x2,
        scratch=fine_arrays(xp, rows) + [(2, ny, 128)],
    )
    v0, bc1, vy_a, vy_b, vxs = out[0], out[1], out[2], out[3], out[4:]

    n1 = gx * nx // 2
    ny1 = ny // 2
    outs = [(n1, ny1, 128), (n1, 16, 128), (n1, 16, 128)]
    if gx == 2:
        f1, y_a, y_b = call(named(mid_y_kernel, False), outs, bc1, swap_even(bc1, "gx"))
    else:
        f1, y_a, y_b = call(
            named(mid_y_kernel, True), outs, lax.all_gather(bc1, "gx", axis=0, tiled=True)
        )
    r_a, r_b = swap_even(y_a, "gy"), swap_odd(y_b, "gy")
    rows1 = ny1 + 32
    z_a, z_b = call(mid_z_kernel, [(n1 // 4, rows1, 128)] * 2, f1, r_a, r_b)
    z_a, z_b = swap_even(z_a, "gz"), swap_odd(z_b, "gz")
    pad1, bare1 = (n1 + 2, rows1 + 16, 128), (n1, rows1, 128)
    v1, b1, c1, bc2 = call(
        mid_down_kernel,
        [pad1] * 3 + [(n1 // 4, ny1 // 2, 128)],
        f1, r_a, r_b, z_a, z_b,
        scratch=[pad1] * 4 + [bare1] * 8 + [(2, ny1, 128)],
    )

    got = jnp.stack([bc2] + [swap_xor(bc2, "gy", m) for m in range(1, gy)])
    bit = gz // 2
    while bit:
        got = jnp.concatenate([got, swap_xor(got, "gz", bit)])
        bit //= 2

    vx1 = swap_x(vxs)
    vrec, vx2 = exchange_rest(1, (v0,), vy_a, vy_b, nsx)

    n2, ny2 = n1 // 2, gy * ny1 // 2
    n3, ny3 = n2 // 2, ny2 // 2
    pad2, bare2 = (n2 + 2, ny2 + 16, 128), (n2, ny2, 128)
    pad3, bare3 = (n3 + 2, ny3 + 16, 128), (n3, ny3, 128)
    (v1,) = call(
        named(coarse_kernel, gy, gz),
        [pad1],
        got, v1, b1, c1,
        scratch=[pad2] * 4 + [bare2] * 8 + [pad3] * 4 + [bare3] * 7 + [pad1] * 2 + [bare1] * 7
        + [(2, ny2, 128), (1, max(rows1, ny2), 128)],
    )
    sol, res = call(
        named(fine_up_kernel, nsx),
        [full, full],
        c_own, v0, source, *rec, *x1, *x2, *vrec, *vx1, *vx2, v1,
        scratch=fine_arrays(xp, rows) + [(2, rows, 128)],
    )
    return sol, res


def solution(mesh):
    spec = P("gx", "gy", "gz")
    return jax.shard_map(
        body,
        mesh=mesh,
        in_specs=(spec, spec, spec, P()),
        out_specs=(spec, spec),
        check_vma=False,
    )
```

```python
import functools

import math
import jax
import jax.numpy as jnp
from jax import lax
from jax.experimental import pallas as pl
from jax.experimental.pallas import tpu as pltpu
from jax.sharding import PartitionSpec as P

LEVELS = 3
SWEEPS = 4
COARSE = 16
CLASSES = 8
W = 0.85
HX = 5
HL = 6
GW = 2 * HL
UNROLL = 4
F32 = jnp.float32


def pairs_even(n):
    return [(i, i ^ 1) for i in range(n)]


def pairs_odd(n):
    out = []
    for i in range(1, n - 1, 2):
        out += [(i, i + 1), (i + 1, i)]
    return out


def swap_even(x, axis):
    return lax.ppermute(x, axis, pairs_even(lax.axis_size(axis)))


def swap_odd(x, axis):
    return lax.ppermute(x, axis, pairs_odd(lax.axis_size(axis)))


def swap_xor(x, axis, m):
    return lax.ppermute(x, axis, [(i, i ^ m) for i in range(lax.axis_size(axis))])


def even(axis):
    return lax.rem(lax.axis_index(axis), 2) == 0


def call(body, outs, *args, scratch=(), smem=(), hbm_out=False, more=()):
    specs = [
        pl.BlockSpec(memory_space=pltpu.SMEM if i in smem else pltpu.VMEM) for i in range(len(args))
    ]
    shapes = [jax.ShapeDtypeStruct(s, F32) if hbm_out else pltpu.VMEM(s, F32) for s in outs]
    space = pl.ANY if hbm_out else pltpu.VMEM
    args = [pltpu.with_memory_space_constraint(a, pltpu.VMEM) if (i not in smem and a.dtype == F32) else a for i, a in enumerate(args)]
    limit = 4 * sum(math.prod(s) for s in scratch) + 6 * 2**20
    return pl.pallas_call(
        body,
        out_shape=shapes,
        in_specs=specs,
        out_specs=[pl.BlockSpec(memory_space=space) for _ in outs],
        scratch_shapes=[pltpu.VMEM(s, F32) for s in scratch] + list(more),
        name=getattr(body, "__name__", None) or body.func.__name__,
        compiler_params=pltpu.CompilerParams(vmem_limit_bytes=limit),
    )(*args)


def lanes(rows=8):
    return lax.broadcasted_iota(jnp.int32, (rows, 128), 1)


def rot(x, shift):
    if isinstance(shift, int):
        shift = shift % 128
        if shift == 0:
            return x
    else:
        shift = lax.rem(shift + 1024, 128)
    return pltpu.roll(x, shift, 1)


def face_start(axis, total, width, want_even):
    hi = even(axis) if want_even else jnp.logical_not(even(axis))
    return jnp.where(hi, total - width, 0)


def start_kernel(nsx, src, guess, cls, table, c_out, y_a, y_b, *x_out):
    nx, ny, _ = src.shape

    def plane(x, _):
        k = cls[x]
        acc = jnp.full(k.shape, table[0], F32)
        for i in range(1, CLASSES):
            acc = jnp.where(k == i, table[i], acc)
        c_out[x] = acc
        return 0

    lax.fori_loop(0, nx, plane, 0)
    for s in range(nsx):
        p5 = face_start("gx", nx, HX, s == 0)
        p4 = face_start("gx", nx, HX - 1, s == 0)
        for f in range(HX):
            x_out[s][f] = c_out[p5 + f]
            x_out[s][HX + f] = guess[p5 + f]
        for f in range(HX - 1):
            x_out[s][2 * HX + f] = src[p4 + f]
    for ref, flag in ((y_a, True), (y_b, False)):
        r = pl.multiple_of(face_start("gy", ny, 8, flag), 8)
        for k, a in enumerate((c_out, guess, src)):
            ref[k * nx : (k + 1) * nx] = a[:, pl.ds(r, 8), :]


def zpack_kernel(na, *refs):
    arrs = refs[:na]
    r_a, r_b, z, work = refs[na:]
    nx, ny, _ = arrs[0].shape
    tiles = ny // 8 + 2
    ey = even("gy")
    lane = lanes()
    for k in range(na):
        for x in range(nx):
            acc = jnp.zeros((8, 128), F32)
            va, vb = r_a[k * nx + x], r_b[k * nx + x]
            for t in range(tiles):
                if t == 0:
                    v = jnp.where(ey, vb, va)
                elif t == tiles - 1:
                    v = jnp.where(ey, va, vb)
                else:
                    v = arrs[k][x, (t - 1) * 8 : t * 8]
                g = GW * t
                acc = jnp.where((lane >= g) & (lane < g + GW), rot(v, g + HL), acc)
            work[(k * nx + x) * 8 : (k * nx + x) * 8 + 8] = acc
    mirror = select_mat(lambda o: o + (GW - 1) - 2 * lax.rem(o, GW))
    out = dot(work[...], mirror)
    for j in range(na * nx):
        z[j] = out[8 * j : 8 * j + 8]


def halo_of(z_a, z_b, i):
    ez = even("gz")
    a, b = z_a[i], z_b[i]
    within = lax.rem(lanes(), GW)
    return jnp.where(within < HL, jnp.where(ez, a, b), jnp.where(ez, b, a))


def face_list(na):
    widths = (HX, HX, HX - 1)
    return [(k, f, widths[k]) for k in range(na) for f in range(widths[k])]


def xframe_kernel(na, nx, nsx, r_a, r_b, z_a, z_b, *x_out):
    ey = even("gy")
    planes = face_list(na)
    base = len(planes) * 16
    for s in range(nsx):
        for j, (k, f, w) in enumerate(planes):
            p = k * nx + face_start("gx", nx, w, s == 0) + f
            va, vb = r_a[p], r_b[p]
            x_out[s][j * 16 : j * 16 + 8] = jnp.where(ey, vb, va)
            x_out[s][j * 16 + 8 : j * 16 + 16] = jnp.where(ey, va, vb)
            x_out[s][base + j * 8 : base + j * 8 + 8] = halo_of(z_a, z_b, p)


def own_offset(nsx):
    return HX * lax.axis_index("gx") if nsx == 1 else HX


def assemble(nsx, planes, m, h, own, r_a, r_b, z_a, z_b, x1, x2):
    nx, ny, _ = own.shape
    off = 1 + own_offset(nsx)
    ey = even("gy")
    kk = planes[0]

    def one(x, _):
        va, vb = r_a[kk * nx + x], r_b[kk * nx + x]
        m[off + x, 8:16] = jnp.where(ey, vb, va)
        m[off + x, 16 : 16 + ny] = own[x]
        m[off + x, 16 + ny : 24 + ny] = jnp.where(ey, va, vb)
        h[off + x] = halo_of(z_a, z_b, kk * nx + x)
        return 0

    lax.fori_loop(0, nx, one, 0)
    for s in range(nsx):
        hi = even("gx") if s == 0 else jnp.logical_not(even("gx"))
        for j, _, f, w, base in planes[1]:
            p = off + jnp.where(hi, nx, -w) + f
            m[p, 8:16] = x2[s][j * 16 : j * 16 + 8]
            m[p, 16 : 16 + ny] = x1[s][j]
            m[p, 16 + ny : 24 + ny] = x2[s][j * 16 + 8 : j * 16 + 16]
            h[p] = x2[s][base + j * 8 : base + j * 8 + 8]


def plane_map(na, k):
    ps = face_list(na)
    base = len(ps) * 16
    return (k, [(j, kk, f, w, base) for j, (kk, f, w) in enumerate(ps) if kk == k])


def zshift(vals, wrap=True):
    lo = lanes(vals[0].shape[0])
    down = [rot(v, 1) for v in vals]
    up = [rot(v, -1) for v in vals]
    if len(vals) == 2:
        first, last = lo == 0, lo == 127
        down = [jnp.where(first, down[1 - t], down[t]) for t in (0, 1)]
        up = [jnp.where(last, up[1 - t], up[t]) for t in (0, 1)]
    return down, up


def neighbours(refs, x, r, n):
    vals = [ref[x, pl.ds(8 + r, n)] for ref in refs]
    down, up = zshift(vals)
    out = []
    for t, ref in enumerate(refs):
        out.append(
            (
                ref[x - 1, pl.ds(8 + r, n)],
                ref[x + 1, pl.ds(8 + r, n)],
                ref[x, pl.ds(7 + r, n)],
                ref[x, pl.ds(9 + r, n)],
                down[t],
                up[t],
            )
        )
    return vals, out


def zero(*refs):
    for ref in refs:

        def one(x, _):
            ref[x] = jnp.zeros(ref.shape[1:], F32)
            return 0

        lax.fori_loop(0, ref.shape[0], one, 0)


def chunks(rows, n=8):
    return range(0, rows, n)


def build_coef(c, b, a, q, d, scale, full_lanes):
    nx, rows = c[0].shape[0] - 2, c[0].shape[1] - 16

    def plane(x, _):
        for r in chunks(rows):
            vals, nb = neighbours(c, x, r, 8)
            lane = lanes()
            for t in range(len(c)):
                six = list(nb[t])
                if full_lanes:
                    six[4] = jnp.where(lane == 0, 0.0, six[4])
                    six[5] = jnp.where(lane == 127, 0.0, six[5])
                total = 6.0 * vals[t] + (((six[0] + six[1]) + (six[2] + six[3])) + (six[4] + six[5]))
                inside = vals[t] > 0.0
                g = jnp.where(inside, W / jnp.where(inside, total, 1.0), 0.0)
                rw = pl.ds(r, 8)
                for j in range(6):
                    face = g * (vals[t] + six[j])
                    if full_lanes and j == 4:
                        face = jnp.where(lane == 0, 0.0, face)
                    if full_lanes and j == 5:
                        face = jnp.where(lane == 127, 0.0, face)
                    a[j][t][x - 1, rw] = face
                q[t][x - 1, rw] = g * ((2.0 / scale) * b[t][x, pl.ds(8 + r, 8)])
                if d is not None:
                    d[t][x - 1, rw] = total * (0.5 * scale / W)

    fine_loop(1, nx, plane, 2)


def weighted(a, vals, nb, t, x, rw):
    s = a[0][t][x - 1, rw] * nb[t][0] + a[1][t][x - 1, rw] * nb[t][1]
    u = a[2][t][x - 1, rw] * nb[t][2] + a[3][t][x - 1, rw] * nb[t][3]
    w = a[4][t][x - 1, rw] * nb[t][4] + a[5][t][x - 1, rw] * nb[t][5]
    return (s + u) + w


def sweep(src, dst, a, q, unroll=False):
    nx, rows = src[0].shape[0] - 2, src[0].shape[1] - 16

    def plane(x, _):
        for r in chunks(rows):
            vals, nb = neighbours(src, x, r, 8)
            rw = pl.ds(r, 8)
            for t in range(len(src)):
                dst[t][x, pl.ds(8 + r, 8)] = ((1.0 - W) * vals[t] + q[t][x - 1, rw]) + weighted(
                    a, vals, nb, t, x, rw
                )

    if unroll:
        for x in range(1, nx + 1):
            plane(x, 0)
    else:
        fine_loop(1, nx, plane, UNROLL)


def copy_q(dst, q):
    def plane(x, _):
        for t in range(len(q)):
            dst[t][x + 1, 8 : 8 + q[t].shape[1]] = q[t][x]
        return 0

    lax.fori_loop(0, q[0].shape[0], plane, 0)


def residual_rows(v, b, a, d, x, r, n=8):
    vals, nb = neighbours(v, x, r, n)
    rw = pl.ds(r, n)
    return b - d[0][x - 1, rw] * (W * vals[0] - weighted(a, vals, nb, 0, x, rw))


def pick(shift_out, cols, limit):
    i = lax.broadcasted_iota(jnp.int32, (128, 128), 0)
    o = lax.broadcasted_iota(jnp.int32, (128, 128), 1)
    return jnp.where((i // 2 == o - shift_out) & (i < limit), 0.125, 0.0).astype(F32)


def dot(a, b):
    bf = jnp.bfloat16
    b = b.astype(bf)
    hi = a.astype(bf)
    rest = a - hi.astype(F32)
    mid = rest.astype(bf)
    lo = (rest - mid.astype(F32)).astype(bf)
    one = lambda p: lax.dot_general(p, b, (((1,), (0,)), ((), ())), preferred_element_type=F32)
    return one(hi) + (one(mid) + one(lo))


def half_rows(ref, r0, n):
    return ref[pl.ds(r0, n // 2, stride=2)] + ref[pl.ds(r0 + 1, n // 2, stride=2)]


def fine_loop(lo, count, plane, unroll):
    while count % unroll:
        unroll -= 1

    def group(i, _):
        for u in range(unroll):
            plane(lo + i * unroll + u, 0)
        return 0

    lax.fori_loop(0, count // unroll, group, 0)


def fine_each(m, h, x, tiles, with_h, emit):
    lane = lanes()
    hv = h[x]
    edge = hv
    for t in tiles:
        g = GW * t
        v = m[x, 8 + 8 * t : 16 + 8 * t]
        beside = rot(hv, -(g + HL))
        down = jnp.where(lane == 0, beside, rot(v, 1))
        up = jnp.where(lane == 127, beside, rot(v, -1))
        six = (
            m[x - 1, 8 + 8 * t : 16 + 8 * t],
            m[x + 1, 8 + 8 * t : 16 + 8 * t],
            m[x, 7 + 8 * t : 15 + 8 * t],
            m[x, 9 + 8 * t : 17 + 8 * t],
            down,
            up,
        )
        emit(0, t, v, six)
        if with_h:
            edge = jnp.where((lane >= g) & (lane < g + GW), rot(v, g + HL), edge)
    if with_h:
        row = lax.broadcasted_iota(jnp.int32, (8, 128), 0)
        within = lax.rem(lane, GW)
        above, below = pltpu.roll(hv, 1, 0), pltpu.roll(hv, 7, 0)
        six = (
            h[x - 1],
            h[x + 1],
            jnp.where(row == 0, rot(above, GW), above),
            jnp.where(row == 7, rot(below, -GW), below),
            jnp.where(within == HL - 1, edge, rot(hv, -1)),
            jnp.where(within == HL, edge, rot(hv, 1)),
        )
        emit(1, 0, hv, six)


def cut(part, ref, x, t, pad):
    if part == 1:
        return (x, slice(0, 8))
    r = 8 * t + (8 if pad else 0)
    return (x, slice(r, r + 8))


def fine_coef(c, b, a, q, d, lo, count):
    tiles = range((c[0].shape[1] - 16) // 8)

    def plane(x, _):
        def emit(part, t, v, six):
            total = 6.0 * v + (((six[0] + six[1]) + (six[2] + six[3])) + (six[4] + six[5]))
            inside = v > 0.0
            g = jnp.where(inside, W / jnp.where(inside, total, 1.0), 0.0)
            at = cut(part, None, x - 1, t, False)
            for j in range(6):
                a[j][part][at] = g * (v + six[j])
            q[part][at] = g * (2.0 * b[part][cut(part, None, x, t, True)])
            if part == 0:
                d[at] = total * (0.5 / W)

        fine_each(c[0], c[1], x, tiles, True, emit)

    fine_loop(lo, count, plane, UNROLL)


def gather_sum(a, part, at, six):
    s = a[0][part][at] * six[0] + a[1][part][at] * six[1]
    u = a[2][part][at] * six[2] + a[3][part][at] * six[3]
    w = a[4][part][at] * six[4] + a[5][part][at] * six[5]
    return (s + u) + w


def fine_sweep(src, dst, a, q, lo, count):
    tiles = range((src[0].shape[1] - 16) // 8)

    def plane(x, _):
        def emit(part, t, v, six):
            at = cut(part, None, x - 1, t, False)
            dst[part][cut(part, None, x, t, True)] = (
                (1.0 - W) * v + q[part][at]
            ) + gather_sum(a, part, at, six)

        fine_each(src[0], src[1], x, tiles, True, emit)

    fine_loop(lo, count, plane, UNROLL)


def fine_residual(v, a, d, x, b_tile, put):
    def emit(part, t, val, six):
        at = cut(part, None, x - 1, t, False)
        put(t - 1, b_tile(t - 1) - d[at] * (W * val - gather_sum(a, part, at, six)))

    fine_each(v[0], v[1], x, range(1, (v[0].shape[1] - 16) // 8 - 1), False, emit)


def fine_range(nsx, nx, extra):
    off = own_offset(nsx)
    xp = nx + nsx * HX
    lo = jnp.maximum(off - extra, 0) + 1
    return lo, nx + nsx * extra


def fine_kept(xp, rows):
    m, h = (xp, rows, 128), (xp, 8, 128)
    return [(xp + 2, rows + 16, 128), (xp + 2, 8, 128)] + [m, h] * 7 + [m]


def fine_work(xp, rows):
    return [(xp + 2, rows + 16, 128), (xp + 2, 8, 128)] * 3


def split_kept(s):
    two = lambda i: (s[i], s[i + 1])
    return two(0), [two(2 + 2 * j) for j in range(6)], two(14), s[16]


def clear_rim(*pairs):
    for m, h in pairs:
        n, rows, _ = m.shape
        for x in (0, n - 1):
            m[x] = jnp.zeros(m.shape[1:], F32)
            h[x] = jnp.zeros(h.shape[1:], F32)

        def one(x, _):
            m[x, 0:8] = jnp.zeros((8, 128), F32)
            m[x, rows - 8 : rows] = jnp.zeros((8, 128), F32)
            return 0

        lax.fori_loop(0, n, one, 0)


def load_fine(nsx, na, which, refs_own, r, target):
    for k, own, (m, h) in zip(which, refs_own, target):
        assemble(nsx, plane_map(na, k), m, h, own, *r)


def set_up_fine(nsx, c_own, src, r, c, b, a, q, d):
    nx = src.shape[0]
    clear_rim(c)
    load_fine(nsx, 3, (0, 2), (c_own, src), r, (c, b))
    lo, count = fine_range(nsx, nx, HX - 1)
    fine_coef(c, b, a, q, d, lo, count)


def fine_sweeps(nsx, nx, v, w, a, q):
    for _ in range(SWEEPS):
        lo, count = fine_range(nsx, nx, HX - 1)
        fine_sweep(v, w, a, q, lo, count)
        v, w = w, v
    return v


def fine_down_kernel(nsx, keep, *refs):
    c_own, guess, src = refs[:3]
    n = 7 + 2 * nsx
    r = refs[3:7] + (refs[7 : 7 + nsx], refs[7 + nsx : n])
    v_out, bc, y_a, y_b = refs[n : n + 4]
    xf = refs[n + 4 : n + 4 + nsx]
    s = refs[n + 4 + nsx :]
    c, a, q, d = split_kept(s[:17])
    b, v, v2 = (s[17], s[18]), (s[19], s[20]), (s[21], s[22])
    pair = s[23]
    nx, ny, _ = src.shape
    off = 1 + own_offset(nsx)
    set_up_fine(nsx, c_own, src, r, c, b, a, q, d)
    clear_rim(v, v2)
    load_fine(nsx, 3, (1,), (guess,), r, (v,))
    v = fine_sweeps(nsx, nx, v, v2, a, q)
    pb, pc = pick(0, 64, 128), pick(64, 64, 128)

    def coarse(i, _):
        x = off + 2 * i
        rs = [None] * (ny // 8)

        def first(t, val):
            rs[t] = val

        def second(t, val):
            pair[0, 8 * t : 8 * t + 8] = rs[t] + val

        for o, put in ((0, first), (1, second)):
            fine_residual(
                v, a, d, x + o, lambda t: src[2 * i + o, 8 * t : 8 * t + 8], put
            )
        for t in range(ny // 8):
            w8 = slice(8 * t, 8 * t + 8)
            pair[1, w8] = c_own[2 * i, w8] + c_own[2 * i + 1, w8]
            v_out[2 * i, w8] = v[0][x, 16 + 8 * t : 24 + 8 * t]
            v_out[2 * i + 1, w8] = v[0][x + 1, 16 + 8 * t : 24 + 8 * t]
        bc[i] = dot(half_rows(pair.at[0], 0, ny), pb) + dot(half_rows(pair.at[1], 0, ny), pc)
        return 0

    lax.fori_loop(0, nx // 2, coarse, 0)
    for k in range(nsx):
        p5 = face_start("gx", nx, HX, k == 0)
        for f in range(HX):
            xf[k][f] = v_out[p5 + f]
    for ref, flag in ((y_a, True), (y_b, False)):
        r = pl.multiple_of(face_start("gy", ny, 8, flag), 8)
        ref[...] = v_out[:, pl.ds(r, 8), :]


def mid_y_kernel(gathered, *refs):
    if gathered:
        full_in, full, y_a, y_b = refs
        full[...] = full_in[...]
    else:
        own, other, full, y_a, y_b = refs
        n = own.shape[0]
        ix = lax.axis_index("gx")
        full[pl.ds(n * ix, n)] = own[...]
        full[pl.ds(n - n * ix, n)] = other[...]
    ny = full.shape[1]
    for ref, flag in ((y_a, True), (y_b, False)):
        r = pl.multiple_of(face_start("gy", ny, 16, flag), 8)
        ref[...] = full[:, pl.ds(r, 16), :]


def mid_rows(full, r_a, r_b, x, t, ny):
    ey = even("gy")
    if t < 2:
        return jnp.where(ey, r_b[x, t * 8 : t * 8 + 8], r_a[x, t * 8 : t * 8 + 8])
    if t >= ny // 8 + 2:
        u = t - ny // 8 - 2
        return jnp.where(ey, r_a[x, u * 8 : u * 8 + 8], r_b[x, u * 8 : u * 8 + 8])
    return full[x, (t - 2) * 8 : (t - 1) * 8]


def mid_z_kernel(full, r_a, r_b, z_a, z_b):
    nx, ny, _ = full.shape
    ez = even("gz")
    slot = lax.rem(lanes(), 64) // 16
    for t in range(ny // 8 + 4):

        def group(s, _):
            right = jnp.zeros((8, 128), F32)
            left = jnp.zeros((8, 128), F32)
            for g in range(4):
                v = mid_rows(full, r_a, r_b, 4 * s + g, t, ny)
                right = jnp.where(slot == g, rot(v, 16 * g - 48), right)
                left = jnp.where(slot == g, rot(v, 16 * g), left)
            z_a[s, t * 8 : t * 8 + 8] = jnp.where(ez, right, left)
            z_b[s, t * 8 : t * 8 + 8] = jnp.where(ez, left, right)
            return 0

        lax.fori_loop(0, nx // 4, group, 0)


def mid_down_kernel(keep, full, r_a, r_b, z_a, z_b, v_out, bc, *s):
    c, b = (s[0],), (s[1],)
    a = [(s[2 + j],) for j in range(6)]
    q, d, v, v2, pair = (s[8],), (s[9],), (s[10],), (s[11],), s[12]
    nx, ny, _ = full.shape
    ez = even("gz")
    lane = lanes()
    own, right_l, left_l = lane < 64, (lane >= 64) & (lane < 80), lane >= 112
    zero(c[0], b[0], v[0], v2[0])
    for t in range(ny // 8 + 4):

        def group(s_, _):
            za, zb = z_a[s_, t * 8 : t * 8 + 8], z_b[s_, t * 8 : t * 8 + 8]
            right = jnp.where(ez, za, zb)
            left = jnp.where(ez, zb, za)
            for g in range(4):
                x = 4 * s_ + g
                m = mid_rows(full, r_a, r_b, x, t, ny)
                for ref, o in ((b[0], 0), (c[0], 64)):
                    e = jnp.where(own, rot(m, -o), 0.0)
                    e = jnp.where(right_l, rot(right, 64 - o - 16 * g), e)
                    e = jnp.where(left_l, rot(left, 112 - o - 16 * g), e)
                    ref[x + 1, 8 + t * 8 : 16 + t * 8] = e
            return 0

        lax.fori_loop(0, nx // 4, group, 0)
    build_coef(c, b, a, q, d, 0.25, False)
    copy_q(v, q)
    sweep(v, v2, a, q)
    sweep(v2, v, a, q)
    sweep(v, v2, a, q)
    v = v2
    half = nx // 4
    mats = [(pick(o, 32, 64), pick(o + 32, 32, 64)) for o in (0, 64)]

    def coarse(i, _):
        acc = jnp.zeros((ny // 2, 128), F32)
        for side in (0, 1):
            x = 1 + 2 * (i + side * half)
            for r in chunks(ny):
                rp = pl.ds(24 + r, 8)
                r0 = residual_rows(v, b[0][x, rp], a, d, x, 16 + r)
                r1 = residual_rows(v, b[0][x + 1, rp], a, d, x + 1, 16 + r)
                pair[0, pl.ds(r, 8)] = r0 + r1
                pair[1, pl.ds(r, 8)] = c[0][x, rp] + c[0][x + 1, rp]
            acc = acc + dot(half_rows(pair.at[0], 0, ny), mats[side][0])
            acc = acc + dot(half_rows(pair.at[1], 0, ny), mats[side][1])
        bc[i] = acc
        return 0

    lax.fori_loop(0, half, coarse, 0)
    v_out[...] = v[0][...]


def spread(src, dst, mats, c, x_src, x_dst, r_src, n, r_dst, tmp, sets=False):
    for t, mat in enumerate(mats):
        p = dot(src, mat)
        tmp[t, pl.ds(0, n, stride=2)] = p
        tmp[t, pl.ds(1, n, stride=2)] = p
    for xd in x_dst:
        for t in range(len(mats)):
            for r in chunks(2 * n):
                rr = pl.ds(r_dst + r, 8)
                dst[t][xd, rr] = dst[t][xd, rr] + jnp.where(
                    c[t][xd, rr] > 0.0, tmp[t, pl.ds(r, 8)], 0.0
                )


def select_mat(fn):
    i = lax.broadcasted_iota(jnp.int32, (128, 128), 0)
    o = lax.broadcasted_iota(jnp.int32, (128, 128), 1)
    return jnp.where(i == fn(o), 1.0, 0.0).astype(F32)


def coarse_kernel(gy, gz, keep, blocks, v1_in, c1, b1, *s):
    if keep:
        a1, q1, s = [(s[j],) for j in range(6)], (s[6],), s[7:]
    v1_out, s = s[0], s[1:]
    if not keep:
        a1, q1, s = [(s[j],) for j in range(6)], (s[6],), s[7:]
    c2, b2, v2, w2 = [(s[i],) for i in range(4)]
    a2 = [(s[4 + j],) for j in range(6)]
    q2, d2 = (s[10],), (s[11],)
    c3, b3, v3, w3 = [(s[12 + i],) for i in range(4)]
    a3 = [(s[16 + j],) for j in range(6)]
    q3 = (s[22],)
    v1, w1 = (v1_out,), (s[23],)
    pair, tmp = s[24], s[25]
    iy, iz = lax.axis_index("gy"), lax.axis_index("gz")
    half, yb, _ = blocks.shape[1:]
    lane = lanes(yb)
    zero(c2[0], b2[0], v2[0], w2[0], c3[0], b3[0], v3[0], w3[0], w1[0])
    nx2 = 2 * half
    for jy in range(gy):
        ky = lax.bitwise_xor(jnp.int32(jy), iy)

        def plane(i, _):
            for o in (0, 64):
                for ref, oo in ((b2[0], o), (c2[0], o + 32)):
                    acc = jnp.zeros((yb, 128), F32)
                    for jz in range(gz):
                        kz = lax.bitwise_xor(jnp.int32(jz), iz)
                        idx = ((kz % 2) * (gz // 2) + kz // 2) * gy + ky
                        acc = jnp.where(lane // 32 == jz, rot(blocks[idx, i], 32 * jz - oo), acc)
                    ref[1 + i + (half if o else 0), 8 + yb * jy : 8 + yb * (jy + 1)] = acc
            return 0

        lax.fori_loop(0, half, plane, 0)
    build_coef(c2, b2, a2, q2, d2, 0.0625, True)
    copy_q(v2, q2)
    sweep(v2, w2, a2, q2)
    sweep(w2, v2, a2, q2)
    sweep(v2, w2, a2, q2)
    ny = yb * gy
    mat = pick(0, 64, 128)

    def coarse(i, _):
        x = 1 + 2 * i
        for r in chunks(ny):
            rp = pl.ds(8 + r, 8)
            r0 = residual_rows(w2, b2[0][x, rp], a2, d2, x, r)
            r1 = residual_rows(w2, b2[0][x + 1, rp], a2, d2, x + 1, r)
            pair[0, pl.ds(r, 8)] = r0 + r1
            pair[1, pl.ds(r, 8)] = c2[0][x, rp] + c2[0][x + 1, rp]
        b3[0][1 + i, 8 : 8 + ny // 2] = dot(half_rows(pair.at[0], 0, ny), mat)
        c3[0][1 + i, 8 : 8 + ny // 2] = dot(half_rows(pair.at[1], 0, ny), mat)
        return 0

    lax.fori_loop(0, nx2 // 2, coarse, 0)
    small = nx2 <= 8
    build_coef(c3, b3, a3, q3, None, 0.015625, False)
    copy_q(v3, q3)
    sweep(v3, w3, a3, q3, small)

    def two(_, carry):
        sweep(w3, v3, a3, q3, small)
        sweep(v3, w3, a3, q3, small)
        return carry

    lax.fori_loop(0, (COARSE - 2) // 2, two, 0)
    up = select_mat(lambda o: o // 2)

    def up2(i, _):
        spread(w3[0][1 + i, 8 : 8 + ny // 2], w2, [up], c2, None, (1 + 2 * i, 2 + 2 * i), None, ny // 2, 8, tmp)
        return 0

    lax.fori_loop(0, nx2 // 2, up2, 0)

    def two2(_, carry):
        sweep(w2, v2, a2, q2)
        sweep(v2, w2, a2, q2)
        return carry

    lax.fori_loop(0, SWEEPS // 2, two2, 0)
    if not keep:
        build_coef((c1,), (b1,), a1, q1, None, 0.25, False)
    v1[0][...] = v1_in[...]
    rows1 = v1[0].shape[1] - 16
    up = select_mat(lambda o: jnp.where(o < 80, o // 2, jnp.where(o >= 112, (o + 128) // 2, -1)))
    start = pl.multiple_of(yb * iy, 8)

    def up1(i, _):
        par = rot(w2[0][1 + i, pl.ds(start, rows1 // 2)], -32 * iz)
        spread(par, v1, [up], (c1,), None, (1 + 2 * i, 2 + 2 * i), None, rows1 // 2, 8, tmp)
        return 0

    lax.fori_loop(0, nx2, up1, 0)

    def two1(_, carry):
        sweep(v1, w1, a1, q1)
        sweep(w1, v1, a1, q1)
        return carry

    lax.fori_loop(0, SWEEPS // 2, two1, 0)


def spread_fine(v, c, planes, up, tmp):
    n = up.shape[0]
    for half in (0, 1):
        p = up[:, 128 * half : 128 * half + 128]
        tmp[half, pl.ds(0, n, stride=2)] = p
        tmp[half, pl.ds(1, n, stride=2)] = p
    lane = lanes()
    edge = jnp.zeros((8, 128), F32)
    for t in range(2 * n // 8):
        rows = slice(8 + 8 * t, 16 + 8 * t)
        par = tmp[0, 8 * t : 8 * t + 8]
        for x in planes:
            v[0][x, rows] = v[0][x, rows] + jnp.where(c[0][x, rows] > 0.0, par, 0.0)
        g = GW * t
        here = (lane >= g) & (lane < g + GW)
        edge = jnp.where(here, tmp[1, 8 * t : 8 * t + 8], edge)
    for x in planes:
        v[1][x] = v[1][x] + jnp.where(c[1][x] > 0.0, edge, 0.0)


def fine_up_kernel(nsx, keep, *refs):
    c_own, v_own, src = refs[:3]
    n = 7 + 2 * nsx
    r = refs[3:7] + (refs[7 : 7 + nsx], refs[7 + nsx : n])
    vr = refs[n : n + 4] + (refs[n + 4 : n + 4 + nsx], refs[n + 4 + nsx : n + 4 + 2 * nsx])
    n = n + 4 + 2 * nsx
    v1 = refs[n]
    n = n + 1
    if keep:
        c, a, q, d = split_kept(refs[n : n + 17])
        n = n + 17
    sol_hbm, res_hbm = refs[n : n + 2]
    sol, res, sems = refs[-3:]
    s = refs[n + 2 : -3]
    if not keep:
        c, a, q, d = split_kept(s[:17])
        s = s[17:]
    b, v, v2 = (s[0], s[1]), (s[2], s[3]), (s[4], s[5])
    tmp, stage, spread = s[6:9]
    nx, ny, _ = src.shape
    off = 1 + own_offset(nsx)
    if not keep:
        set_up_fine(nsx, c_own, src, r, c, b, a, q, d)
    clear_rim(v, v2)
    load_fine(nsx, 1, (0,), (v_own,), vr, (v,))
    i = lax.broadcasted_iota(jnp.int32, (128, 256), 0)
    o = lax.broadcasted_iota(jnp.int32, (128, 256), 1)
    within = lax.rem(o - 128, GW)
    z = HL - 1 - within
    par = jnp.where(within < HL, 64 + lax.div(z, 2), 128 + lax.shift_right_arithmetic(z, 1))
    mat = jnp.where(i == jnp.where(o < 128, lax.div(o, 2), par), 1.0, 0.0).astype(F32)
    nc = v1.shape[0] - 2
    ix = lax.axis_index("gx")
    half = (ny + 16) // 2
    xp = v[0].shape[0] - 2
    count = (xp + 2) // 2
    c0 = lax.shift_right_arithmetic(nx * ix + 1 - off, 1)
    for j in range(count):
        stage[j * half : (j + 1) * half] = v1[1 + jnp.clip(c0 + j, 0, nc - 1), 20 : 20 + half]
    spread[...] = dot(stage[...], mat)

    def up(j, _):
        p = 2 * (c0 + j) - nx * ix + off
        start = pl.multiple_of(half * j, 8)
        spread_fine(v, c, (p, p + 1), spread[pl.ds(start, half)], tmp)
        return 0

    lax.fori_loop(0, count, up, 0)
    v = fine_sweeps(nsx, nx, v, v2, a, q)

    step = nx // 4

    def copies(i):
        at = pl.ds(i * step, step)
        return (
            pltpu.make_async_copy(sol.at[at], sol_hbm.at[at], sems.at[0, i]),
            pltpu.make_async_copy(res.at[at], res_hbm.at[at], sems.at[1, i]),
        )

    def out(x, _):
        def put(t, val):
            w8 = slice(8 * t, 8 * t + 8)
            res[x, w8] = val
            sol[x, w8] = v[0][off + x, 16 + 8 * t : 24 + 8 * t]

        fine_residual(v, a, d, off + x, lambda t: src[x, 8 * t : 8 * t + 8], put)

    for i in range(4):
        fine_loop(i * step, step, out, 2)
        for cp in copies(i):
            cp.start()
    for i in range(4):
        for cp in copies(i):
            cp.wait()


def named(fn, *args):
    out = functools.partial(fn, *args)
    out.__name__ = fn.__name__
    return out


def exchange_rest(na, arrs, y_a, y_b, nsx):
    nx, ny, _ = arrs[0].shape
    rows = ny + 16
    r_a, r_b = swap_even(y_a, "gy"), swap_odd(y_b, "gy")
    (z,) = call(
        named(zpack_kernel, na), [(na * nx, 8, 128)], *arrs, r_a, r_b,
        scratch=[(na * nx * 8, 128)],
    )
    z_a, z_b = swap_even(z, "gz"), swap_odd(z, "gz")
    count = len(face_list(na))
    size = count * 24
    xs = call(named(xframe_kernel, na, nx, nsx), [(size, 128)] * nsx, r_a, r_b, z_a, z_b)
    x2 = swap_x(xs)
    return (r_a, r_b, z_a, z_b), x2


def swap_x(xs):
    out = [swap_even(xs[0], "gx")]
    if len(xs) > 1:
        out.append(swap_odd(xs[1], "gx"))
    return out


def body(source, first_guess, cell_classes, class_table):
    nx, ny, _ = source.shape
    gx, gy, gz = (lax.axis_size(n) for n in ("gx", "gy", "gz"))
    nsx = 1 if gx == 2 else 2
    xp = nx + nsx * HX
    rows = ny + 16
    full = (nx, ny, 128)

    out = call(
        named(start_kernel, nsx),
        [full, (3 * nx, 8, 128), (3 * nx, 8, 128)] + [(3 * HX - 1, ny, 128)] * nsx,
        source, first_guess, cell_classes, class_table,
        smem=(3,),
    )
    c_own, y_a, y_b, xs = out[0], out[1], out[2], out[3:]
    x1 = swap_x(xs)
    rec, x2 = exchange_rest(3, (c_own, first_guess, source), y_a, y_b, nsx)
    keep = gx == 2
    kept_shapes = fine_kept(xp, rows)
    outs = [full, (nx // 2, ny // 2, 128), (nx, 8, 128), (nx, 8, 128)] + [(HX, ny, 128)] * nsx
    work = fine_work(xp, rows) + [(2, ny, 128)]
    out = call(
        named(fine_down_kernel, nsx, keep),
        outs + (kept_shapes if keep else []),
        c_own, first_guess, source, *rec, *x1, *x2,
        scratch=work if keep else kept_shapes + work,
    )
    kept = out[len(outs) :]
    out = out[: len(outs)]
    v0, bc1, vy_a, vy_b, vxs = out[0], out[1], out[2], out[3], out[4:]

    n1 = gx * nx // 2
    ny1 = ny // 2
    outs = [(n1, ny1, 128), (n1, 16, 128), (n1, 16, 128)]
    if gx == 2:
        f1, y_a, y_b = call(named(mid_y_kernel, False), outs, bc1, swap_even(bc1, "gx"))
    else:
        f1, y_a, y_b = call(
            named(mid_y_kernel, True), outs, lax.all_gather(bc1, "gx", axis=0, tiled=True)
        )
    r_a, r_b = swap_even(y_a, "gy"), swap_odd(y_b, "gy")
    rows1 = ny1 + 32
    z_a, z_b = call(mid_z_kernel, [(n1 // 4, rows1, 128)] * 2, f1, r_a, r_b)
    z_a, z_b = swap_even(z_a, "gz"), swap_odd(z_b, "gz")
    pad1, bare1 = (n1 + 2, rows1 + 16, 128), (n1, rows1, 128)
    out = call(
        named(mid_down_kernel, keep),
        [pad1, (n1 // 4, ny1 // 2, 128), pad1, pad1] + ([bare1] * 7 if keep else []),
        f1, r_a, r_b, z_a, z_b,
        scratch=([] if keep else [bare1] * 7) + [bare1, pad1, pad1, (2, ny1, 128)],
    )
    v1, bc2, c1, b1 = out[:4]
    kept1 = out[4:]

    got = jnp.stack([bc2] + [swap_xor(bc2, "gy", m) for m in range(1, gy)])
    bit = gz // 2
    while bit:
        got = jnp.concatenate([got, swap_xor(got, "gz", bit)])
        bit //= 2

    vx1 = swap_x(vxs)
    vrec, vx2 = exchange_rest(1, (v0,), vy_a, vy_b, nsx)

    n2, ny2 = n1 // 2, gy * ny1 // 2
    n3, ny3 = n2 // 2, ny2 // 2
    pad2, bare2 = (n2 + 2, ny2 + 16, 128), (n2, ny2, 128)
    pad3, bare3 = (n3 + 2, ny3 + 16, 128), (n3, ny3, 128)
    (v1,) = call(
        named(coarse_kernel, gy, gz, keep),
        [pad1],
        got, v1, c1, b1, *kept1,
        scratch=([] if keep else [bare1] * 7)
        + [pad2] * 4 + [bare2] * 8 + [pad3] * 4 + [bare3] * 7 + [pad1]
        + [(2, ny2, 128), (1, max(rows1, ny2), 128)],
    )
    par_rows = (xp + 2) // 2 * (rows // 2)
    work = fine_work(xp, rows) + [(2, rows, 128), (par_rows, 128), (par_rows, 256)]
    sol, res = call(
        named(fine_up_kernel, nsx, keep),
        [full, full],
        c_own, v0, source, *rec, *x1, *x2, *vrec, *vx1, *vx2, v1, *kept,
        scratch=(work if keep else kept_shapes + work) + [full, full],
        hbm_out=True,
        more=[pltpu.SemaphoreType.DMA((2, 4))],
    )
    return sol, res


def solution(mesh):
    spec = P("gx", "gy", "gz")
    return jax.shard_map(
        body,
        mesh=mesh,
        in_specs=(spec, spec, spec, P()),
        out_specs=(spec, spec),
        check_vma=False,
    )
```

```python
import functools

import math
import jax
import jax.numpy as jnp
from jax import lax
from jax.experimental import pallas as pl
from jax.experimental.pallas import tpu as pltpu
from jax.sharding import PartitionSpec as P

LEVELS = 3
SWEEPS = 4
COARSE = 16
CLASSES = 8
W = 0.85
HX = 5
HL = 6
GW = 2 * HL
UNROLL = 4
H2 = 12
F32 = jnp.float32


def pairs_even(n):
    return [(i, i ^ 1) for i in range(n)]


def pairs_odd(n):
    out = []
    for i in range(1, n - 1, 2):
        out += [(i, i + 1), (i + 1, i)]
    return out


def swap_even(x, axis):
    return lax.ppermute(x, axis, pairs_even(lax.axis_size(axis)))


def swap_odd(x, axis):
    return lax.ppermute(x, axis, pairs_odd(lax.axis_size(axis)))


def swap_xor(x, axis, m):
    return lax.ppermute(x, axis, [(i, i ^ m) for i in range(lax.axis_size(axis))])


def even(axis):
    return lax.rem(lax.axis_index(axis), 2) == 0


def call(body, outs, *args, scratch=(), smem=(), hbm_out=False, more=()):
    specs = [
        pl.BlockSpec(memory_space=pltpu.SMEM if i in smem else pltpu.VMEM) for i in range(len(args))
    ]
    shapes = [jax.ShapeDtypeStruct(s, F32) if hbm_out else pltpu.VMEM(s, F32) for s in outs]
    space = pl.ANY if hbm_out else pltpu.VMEM
    args = [pltpu.with_memory_space_constraint(a, pltpu.VMEM) if (i not in smem and a.dtype == F32) else a for i, a in enumerate(args)]
    limit = 4 * sum(math.prod(s) for s in scratch) + 6 * 2**20
    return pl.pallas_call(
        body,
        out_shape=shapes,
        in_specs=specs,
        out_specs=[pl.BlockSpec(memory_space=space) for _ in outs],
        scratch_shapes=[pltpu.VMEM(s, F32) for s in scratch] + list(more),
        name=getattr(body, "__name__", None) or body.func.__name__,
        compiler_params=pltpu.CompilerParams(vmem_limit_bytes=limit),
    )(*args)


def lanes(rows=8):
    return lax.broadcasted_iota(jnp.int32, (rows, 128), 1)


def rot(x, shift):
    if isinstance(shift, int):
        shift = shift % 128
        if shift == 0:
            return x
    else:
        shift = lax.rem(shift + 1024, 128)
    return pltpu.roll(x, shift, 1)


def face_start(axis, total, width, want_even):
    hi = even(axis) if want_even else jnp.logical_not(even(axis))
    return jnp.where(hi, total - width, 0)


def start_kernel(nsx, src, guess, cls, table, c_out, y_a, y_b, *x_out):
    nx, ny, _ = src.shape

    def plane(x, _):
        k = cls[x]
        acc = jnp.full(k.shape, table[0], F32)
        for i in range(1, CLASSES):
            acc = jnp.where(k == i, table[i], acc)
        c_out[x] = acc
        return 0

    lax.fori_loop(0, nx, plane, 0)
    for s in range(nsx):
        p5 = face_start("gx", nx, HX, s == 0)
        p4 = face_start("gx", nx, HX - 1, s == 0)
        for f in range(HX):
            x_out[s][f] = c_out[p5 + f]
            x_out[s][HX + f] = guess[p5 + f]
        for f in range(HX - 1):
            x_out[s][2 * HX + f] = src[p4 + f]
    for ref, flag in ((y_a, True), (y_b, False)):
        r = pl.multiple_of(face_start("gy", ny, 8, flag), 8)
        for k, a in enumerate((c_out, guess, src)):
            ref[k * nx : (k + 1) * nx] = a[:, pl.ds(r, 8), :]


def zpack_kernel(na, *refs):
    arrs = refs[:na]
    r_a, r_b, z, work = refs[na:]
    nx, ny, _ = arrs[0].shape
    tiles = ny // 8 + 2
    ey = even("gy")
    lane = lanes()
    for k in range(na):
        for x in range(nx):
            acc = jnp.zeros((8, 128), F32)
            va, vb = r_a[k * nx + x], r_b[k * nx + x]
            for t in range(tiles):
                if t == 0:
                    v = jnp.where(ey, vb, va)
                elif t == tiles - 1:
                    v = jnp.where(ey, va, vb)
                else:
                    v = arrs[k][x, (t - 1) * 8 : t * 8]
                g = GW * t
                acc = jnp.where((lane >= g) & (lane < g + GW), rot(v, g + HL), acc)
            work[(k * nx + x) * 8 : (k * nx + x) * 8 + 8] = acc
    mirror = select_mat(lambda o: o + (GW - 1) - 2 * lax.rem(o, GW))
    out = dot(work[...], mirror)
    for j in range(na * nx):
        z[j] = out[8 * j : 8 * j + 8]


def halo_of(z_a, z_b, i):
    ez = even("gz")
    a, b = z_a[i], z_b[i]
    within = lax.rem(lanes(), GW)
    return jnp.where(within < HL, jnp.where(ez, a, b), jnp.where(ez, b, a))


def face_list(na):
    widths = (HX, HX, HX - 1)
    return [(k, f, widths[k]) for k in range(na) for f in range(widths[k])]


def xframe_kernel(na, nx, nsx, r_a, r_b, z_a, z_b, *x_out):
    ey = even("gy")
    planes = face_list(na)
    base = len(planes) * 16
    for s in range(nsx):
        for j, (k, f, w) in enumerate(planes):
            p = k * nx + face_start("gx", nx, w, s == 0) + f
            va, vb = r_a[p], r_b[p]
            x_out[s][j * 16 : j * 16 + 8] = jnp.where(ey, vb, va)
            x_out[s][j * 16 + 8 : j * 16 + 16] = jnp.where(ey, va, vb)
            x_out[s][base + j * 8 : base + j * 8 + 8] = halo_of(z_a, z_b, p)


def own_offset(nsx):
    return HX * lax.axis_index("gx") if nsx == 1 else HX


def assemble(nsx, planes, m, h, own, r_a, r_b, z_a, z_b, x1, x2):
    nx, ny, _ = own.shape
    off = 1 + own_offset(nsx)
    ey = even("gy")
    kk = planes[0]

    def one(x, _):
        va, vb = r_a[kk * nx + x], r_b[kk * nx + x]
        m[off + x, 8:16] = jnp.where(ey, vb, va)
        m[off + x, 16 : 16 + ny] = own[x]
        m[off + x, 16 + ny : 24 + ny] = jnp.where(ey, va, vb)
        h[off + x] = halo_of(z_a, z_b, kk * nx + x)
        return 0

    lax.fori_loop(0, nx, one, 0)
    for s in range(nsx):
        hi = even("gx") if s == 0 else jnp.logical_not(even("gx"))
        for j, _, f, w, base in planes[1]:
            p = off + jnp.where(hi, nx, -w) + f
            m[p, 8:16] = x2[s][j * 16 : j * 16 + 8]
            m[p, 16 : 16 + ny] = x1[s][j]
            m[p, 16 + ny : 24 + ny] = x2[s][j * 16 + 8 : j * 16 + 16]
            h[p] = x2[s][base + j * 8 : base + j * 8 + 8]


def plane_map(na, k):
    ps = face_list(na)
    base = len(ps) * 16
    return (k, [(j, kk, f, w, base) for j, (kk, f, w) in enumerate(ps) if kk == k])


def zshift(vals, wrap=True):
    lo = lanes(vals[0].shape[0])
    down = [rot(v, 1) for v in vals]
    up = [rot(v, -1) for v in vals]
    if len(vals) == 2:
        first, last = lo == 0, lo == 127
        down = [jnp.where(first, down[1 - t], down[t]) for t in (0, 1)]
        up = [jnp.where(last, up[1 - t], up[t]) for t in (0, 1)]
    return down, up


def neighbours(refs, x, r, n):
    vals = [ref[x, pl.ds(8 + r, n)] for ref in refs]
    down, up = zshift(vals)
    out = []
    for t, ref in enumerate(refs):
        out.append(
            (
                ref[x - 1, pl.ds(8 + r, n)],
                ref[x + 1, pl.ds(8 + r, n)],
                ref[x, pl.ds(7 + r, n)],
                ref[x, pl.ds(9 + r, n)],
                down[t],
                up[t],
            )
        )
    return vals, out


def zero(*refs):
    for ref in refs:

        def one(x, _):
            ref[x] = jnp.zeros(ref.shape[1:], F32)
            return 0

        lax.fori_loop(0, ref.shape[0], one, 0)


def chunks(rows, n=8):
    return range(0, rows, n)


def build_coef(c, b, a, q, d, scale, full_lanes):
    nx, rows = c[0].shape[0] - 2, c[0].shape[1] - 16

    def plane(x, _):
        for r in chunks(rows):
            vals, nb = neighbours(c, x, r, 8)
            lane = lanes()
            for t in range(len(c)):
                six = list(nb[t])
                if full_lanes:
                    six[4] = jnp.where(lane == 0, 0.0, six[4])
                    six[5] = jnp.where(lane == 127, 0.0, six[5])
                total = 6.0 * vals[t] + (((six[0] + six[1]) + (six[2] + six[3])) + (six[4] + six[5]))
                inside = vals[t] > 0.0
                g = jnp.where(inside, W / jnp.where(inside, total, 1.0), 0.0)
                rw = pl.ds(r, 8)
                for j in range(6):
                    face = g * (vals[t] + six[j])
                    if full_lanes and j == 4:
                        face = jnp.where(lane == 0, 0.0, face)
                    if full_lanes and j == 5:
                        face = jnp.where(lane == 127, 0.0, face)
                    a[j][t][x - 1, rw] = face
                q[t][x - 1, rw] = g * ((2.0 / scale) * b[t][x, pl.ds(8 + r, 8)])
                if d is not None:
                    d[t][x - 1, rw] = total * (0.5 * scale / W)

    fine_loop(1, nx, plane, 2)


def weighted(a, vals, nb, t, x, rw):
    s = a[0][t][x - 1, rw] * nb[t][0] + a[1][t][x - 1, rw] * nb[t][1]
    u = a[2][t][x - 1, rw] * nb[t][2] + a[3][t][x - 1, rw] * nb[t][3]
    w = a[4][t][x - 1, rw] * nb[t][4] + a[5][t][x - 1, rw] * nb[t][5]
    return (s + u) + w


def sweep(src, dst, a, q, unroll=False, r0=0, rows=None):
    nx, rows = src[0].shape[0] - 2, rows or src[0].shape[1] - 16

    def plane(x, _):
        for r in range(r0, r0 + rows, 8):
            vals, nb = neighbours(src, x, r, 8)
            rw = pl.ds(r, 8)
            for t in range(len(src)):
                dst[t][x, pl.ds(8 + r, 8)] = ((1.0 - W) * vals[t] + q[t][x - 1, rw]) + weighted(
                    a, vals, nb, t, x, rw
                )

    if unroll:
        for x in range(1, nx + 1):
            plane(x, 0)
    else:
        fine_loop(1, nx, plane, UNROLL)


def copy_q(dst, q):
    def plane(x, _):
        for t in range(len(q)):
            dst[t][x + 1, 8 : 8 + q[t].shape[1]] = q[t][x]
        return 0

    lax.fori_loop(0, q[0].shape[0], plane, 0)


def residual_rows(v, b, a, d, x, r, n=8):
    vals, nb = neighbours(v, x, r, n)
    rw = pl.ds(r, n)
    return b - d[0][x - 1, rw] * (W * vals[0] - weighted(a, vals, nb, 0, x, rw))


def pick(shift_out, cols, limit):
    i = lax.broadcasted_iota(jnp.int32, (128, 128), 0)
    o = lax.broadcasted_iota(jnp.int32, (128, 128), 1)
    return jnp.where((i // 2 == o - shift_out) & (i < limit), 0.125, 0.0).astype(F32)


def dot(a, b):
    bf = jnp.bfloat16
    b = b.astype(bf)
    hi = a.astype(bf)
    rest = a - hi.astype(F32)
    mid = rest.astype(bf)
    lo = (rest - mid.astype(F32)).astype(bf)
    one = lambda p: lax.dot_general(p, b, (((1,), (0,)), ((), ())), preferred_element_type=F32)
    return one(hi) + (one(mid) + one(lo))


def half_rows(ref, r0, n):
    return ref[pl.ds(r0, n // 2, stride=2)] + ref[pl.ds(r0 + 1, n // 2, stride=2)]


def fine_loop(lo, count, plane, unroll):
    while count % unroll:
        unroll -= 1

    def group(i, _):
        for u in range(unroll):
            plane(lo + i * unroll + u, 0)
        return 0

    lax.fori_loop(0, count // unroll, group, 0)


def fine_each(m, h, x, tiles, with_h, emit):
    lane = lanes()
    hv = h[x]
    edge = hv
    for t in tiles:
        g = GW * t
        v = m[x, 8 + 8 * t : 16 + 8 * t]
        beside = rot(hv, -(g + HL))
        down = jnp.where(lane == 0, beside, rot(v, 1))
        up = jnp.where(lane == 127, beside, rot(v, -1))
        six = (
            m[x - 1, 8 + 8 * t : 16 + 8 * t],
            m[x + 1, 8 + 8 * t : 16 + 8 * t],
            m[x, 7 + 8 * t : 15 + 8 * t],
            m[x, 9 + 8 * t : 17 + 8 * t],
            down,
            up,
        )
        emit(0, t, v, six)
        if with_h:
            edge = jnp.where((lane >= g) & (lane < g + GW), rot(v, g + HL), edge)
    if with_h:
        row = lax.broadcasted_iota(jnp.int32, (8, 128), 0)
        within = lax.rem(lane, GW)
        above, below = pltpu.roll(hv, 1, 0), pltpu.roll(hv, 7, 0)
        six = (
            h[x - 1],
            h[x + 1],
            jnp.where(row == 0, rot(above, GW), above),
            jnp.where(row == 7, rot(below, -GW), below),
            jnp.where(within == HL - 1, edge, rot(hv, -1)),
            jnp.where(within == HL, edge, rot(hv, 1)),
        )
        emit(1, 0, hv, six)


def cut(part, ref, x, t, pad):
    if part == 1:
        return (x, slice(0, 8))
    r = 8 * t + (8 if pad else 0)
    return (x, slice(r, r + 8))


def fine_coef(c, b, a, q, d, lo, count):
    tiles = range((c[0].shape[1] - 16) // 8)

    def plane(x, _):
        def emit(part, t, v, six):
            total = 6.0 * v + (((six[0] + six[1]) + (six[2] + six[3])) + (six[4] + six[5]))
            inside = v > 0.0
            g = jnp.where(inside, W / jnp.where(inside, total, 1.0), 0.0)
            at = cut(part, None, x - 1, t, False)
            for j in range(6):
                a[j][part][at] = g * (v + six[j])
            q[part][at] = g * (2.0 * b[part][cut(part, None, x, t, True)])
            if part == 0:
                d[at] = total * (0.5 / W)

        fine_each(c[0], c[1], x, tiles, True, emit)

    fine_loop(lo, count, plane, UNROLL)


def gather_sum(a, part, at, six):
    s = a[0][part][at] * six[0] + a[1][part][at] * six[1]
    u = a[2][part][at] * six[2] + a[3][part][at] * six[3]
    w = a[4][part][at] * six[4] + a[5][part][at] * six[5]
    return (s + u) + w


def fine_sweep(src, dst, a, q, lo, count):
    tiles = range((src[0].shape[1] - 16) // 8)

    def plane(x, _):
        def emit(part, t, v, six):
            at = cut(part, None, x - 1, t, False)
            dst[part][cut(part, None, x, t, True)] = (
                (1.0 - W) * v + q[part][at]
            ) + gather_sum(a, part, at, six)

        fine_each(src[0], src[1], x, tiles, True, emit)

    fine_loop(lo, count, plane, UNROLL)


def fine_residual(v, a, d, x, b_tile, put):
    def emit(part, t, val, six):
        at = cut(part, None, x - 1, t, False)
        put(t - 1, b_tile(t - 1) - d[at] * (W * val - gather_sum(a, part, at, six)))

    fine_each(v[0], v[1], x, range(1, (v[0].shape[1] - 16) // 8 - 1), False, emit)


def fine_range(nsx, nx, extra):
    off = own_offset(nsx)
    xp = nx + nsx * HX
    lo = jnp.maximum(off - extra, 0) + 1
    return lo, nx + nsx * extra


def fine_kept(xp, rows):
    m, h = (xp, rows, 128), (xp, 8, 128)
    return [(xp + 2, rows + 16, 128), (xp + 2, 8, 128)] + [m, h] * 7 + [m]


def fine_work(xp, rows):
    return [(xp + 2, rows + 16, 128), (xp + 2, 8, 128)] * 3


def split_kept(s):
    two = lambda i: (s[i], s[i + 1])
    return two(0), [two(2 + 2 * j) for j in range(6)], two(14), s[16]


def clear_rim(*pairs):
    for m, h in pairs:
        n, rows, _ = m.shape
        for x in (0, n - 1):
            m[x] = jnp.zeros(m.shape[1:], F32)
            h[x] = jnp.zeros(h.shape[1:], F32)

        def one(x, _):
            m[x, 0:8] = jnp.zeros((8, 128), F32)
            m[x, rows - 8 : rows] = jnp.zeros((8, 128), F32)
            return 0

        lax.fori_loop(0, n, one, 0)


def load_fine(nsx, na, which, refs_own, r, target):
    for k, own, (m, h) in zip(which, refs_own, target):
        assemble(nsx, plane_map(na, k), m, h, own, *r)


def set_up_fine(nsx, c_own, src, r, c, b, a, q, d):
    nx = src.shape[0]
    clear_rim(c)
    load_fine(nsx, 3, (0, 2), (c_own, src), r, (c, b))
    lo, count = fine_range(nsx, nx, HX - 1)
    fine_coef(c, b, a, q, d, lo, count)


def fine_sweeps(nsx, nx, v, w, a, q):
    for _ in range(SWEEPS):
        lo, count = fine_range(nsx, nx, HX - 1)
        fine_sweep(v, w, a, q, lo, count)
        v, w = w, v
    return v


def fine_down_kernel(nsx, keep, *refs):
    c_own, guess, src = refs[:3]
    n = 7 + 2 * nsx
    r = refs[3:7] + (refs[7 : 7 + nsx], refs[7 + nsx : n])
    v_out, bc, y_a, y_b = refs[n : n + 4]
    xf = refs[n + 4 : n + 4 + nsx]
    s = refs[n + 4 + nsx :]
    c, a, q, d = split_kept(s[:17])
    b, v, v2 = (s[17], s[18]), (s[19], s[20]), (s[21], s[22])
    pair = s[23]
    nx, ny, _ = src.shape
    off = 1 + own_offset(nsx)
    set_up_fine(nsx, c_own, src, r, c, b, a, q, d)
    clear_rim(v, v2)
    load_fine(nsx, 3, (1,), (guess,), r, (v,))
    v = fine_sweeps(nsx, nx, v, v2, a, q)
    pb, pc = pick(0, 64, 128), pick(64, 64, 128)

    def coarse(i, _):
        x = off + 2 * i
        rs = [None] * (ny // 8)

        def first(t, val):
            rs[t] = val

        def second(t, val):
            pair[0, 8 * t : 8 * t + 8] = rs[t] + val

        for o, put in ((0, first), (1, second)):
            fine_residual(
                v, a, d, x + o, lambda t: src[2 * i + o, 8 * t : 8 * t + 8], put
            )
        for t in range(ny // 8):
            w8 = slice(8 * t, 8 * t + 8)
            pair[1, w8] = c_own[2 * i, w8] + c_own[2 * i + 1, w8]
            v_out[2 * i, w8] = v[0][x, 16 + 8 * t : 24 + 8 * t]
            v_out[2 * i + 1, w8] = v[0][x + 1, 16 + 8 * t : 24 + 8 * t]
        bc[i] = dot(half_rows(pair.at[0], 0, ny), pb) + dot(half_rows(pair.at[1], 0, ny), pc)
        return 0

    lax.fori_loop(0, nx // 2, coarse, 0)
    for k in range(nsx):
        p5 = face_start("gx", nx, HX, k == 0)
        for f in range(HX):
            xf[k][f] = v_out[p5 + f]
    for ref, flag in ((y_a, True), (y_b, False)):
        r = pl.multiple_of(face_start("gy", ny, 8, flag), 8)
        ref[...] = v_out[:, pl.ds(r, 8), :]


def join_kernel(own, other, full):
    n = own.shape[0]
    ix = lax.axis_index("gx")
    full[pl.ds(n * ix, n)] = own[...]
    full[pl.ds(n - n * ix, n)] = other[...]


def mid_rows(full, r_a, r_b, x, t, tiles):
    rows = slice((t % tiles) * 8, (t % tiles) * 8 + 8)
    if t < tiles:
        return jnp.where(even("gy"), r_b[x, rows], r_a[x, rows])
    if t >= 2 * tiles:
        return jnp.where(even("gy"), r_a[x, rows], r_b[x, rows])
    return full[x, rows]


def mid_z_kernel(full, r_a, r_b, v0, vr_a, vr_b, z_a, z_b, vz, work):
    nx, ny, _ = full.shape
    tiles = ny // 8
    ez = even("gz")
    low = lax.rem(lanes(), 64) < 32

    def pair(i, _):
        for t in range(3 * tiles):
            e = mid_rows(full, r_a, r_b, 2 * i, t, tiles)
            o = mid_rows(full, r_a, r_b, 2 * i + 1, t, tiles)
            first = jnp.where(low, e, rot(o, 32))
            last = jnp.where(low, rot(o, -32), e)
            z_a[i, t * 8 : t * 8 + 8] = jnp.where(ez, last, first)
            z_b[i, t * 8 : t * 8 + 8] = jnp.where(ez, first, last)

    fine_loop(0, nx // 2, lambda i, c: pair(i, c), 2)
    zpack_kernel(1, v0, vr_a, vr_b, vz, work)


def mid_down_kernel(full, r_a, r_b, z_a, z_b, vr_a, vr_b, vz_a, vz_b, *s):
    v1_out, c = s[0], (s[1],)
    a, q = [(s[2 + j],) for j in range(6)], (s[8],)
    v2_out, c2 = s[9], (s[10],)
    a2, q2 = [(s[11 + j],) for j in range(6)], (s[17],)
    bc3, frame = s[18], s[19]
    b, d, w = (s[20],), (s[21],), (s[22],)
    b2, d2, w2 = (s[23],), (s[24],), (s[25],)
    pair = s[26]
    xframe_kernel(1, vr_a.shape[0], 1, vr_a, vr_b, vz_a, vz_b, frame)
    v, v2 = (v1_out,), (v2_out,)
    nx, ny, _ = full.shape
    tiles = ny // 8
    ez = even("gz")
    lane = lanes()
    own, low = lane < 64, lax.rem(lane, 64) < 32
    clear_pads(c[0], v[0], w[0], c2[0], v2[0], w2[0])

    def place(x, t, mine, side):
        rows = slice(8 + t * 8, 16 + t * 8)
        b[0][x + 1, rows] = jnp.where(own, mine, rot(side, 64))
        c[0][x + 1, rows] = jnp.where(own, rot(mine, 64), side)

    def two(i, _):
        for t in range(3 * tiles):
            za, zb = z_a[i, t * 8 : t * 8 + 8], z_b[i, t * 8 : t * 8 + 8]
            right = jnp.where(ez, za, zb)
            left = jnp.where(ez, zb, za)
            e = mid_rows(full, r_a, r_b, 2 * i, t, tiles)
            o = mid_rows(full, r_a, r_b, 2 * i + 1, t, tiles)
            place(2 * i, t, e, jnp.where(low, right, left))
            place(2 * i + 1, t, o, jnp.where(low, rot(right, -32), rot(left, 32)))

    fine_loop(0, nx // 2, two, 2)
    build_coef(c, b, a, q, d, 0.25, False)
    copy_q(w, q)
    sweep(w, v, a, q)
    sweep(v, w, a, q)
    sweep(w, v, a, q)
    rows2 = ny // 2 + 2 * H2
    r0 = ny - 2 * H2
    mat = ring_pick(96)

    def down(i, _):
        x = 1 + 2 * i
        for r in chunks(2 * rows2):
            rp = pl.ds(8 + r0 + r, 8)
            e = residual_rows(v, b[0][x, rp], a, d, x, r0 + r)
            o = residual_rows(v, b[0][x + 1, rp], a, d, x + 1, r0 + r)
            pair[0, pl.ds(r, 8)] = e + o
            pair[1, pl.ds(r, 8)] = c[0][x, rp] + c[0][x + 1, rp]
        b2[0][1 + i, 8 : 8 + rows2] = dot(half_rows(pair.at[0], 0, 2 * rows2), mat)
        c2[0][1 + i, 8 : 8 + rows2] = dot(half_rows(pair.at[1], 0, 2 * rows2), mat)

    fine_loop(0, nx // 2, down, 2)
    build_coef(c2, b2, a2, q2, d2, 0.0625, False)
    copy_q(w2, q2)
    sweep(w2, v2, a2, q2)
    sweep(v2, w2, a2, q2)
    sweep(w2, v2, a2, q2)
    n3, ny3 = nx // 4, ny // 4
    for i in range(n3):
        x = 1 + 2 * i
        for r in chunks(ny // 2):
            rp = pl.ds(8 + H2 + r, 8)
            e = residual_rows(v2, b2[0][x, rp], a2, d2, x, H2 + r)
            o = residual_rows(v2, b2[0][x + 1, rp], a2, d2, x + 1, H2 + r)
            pair[0, pl.ds(r, 8)] = e + o
            pair[1, pl.ds(r, 8)] = c2[0][x, rp] + c2[0][x + 1, rp]
        at = 32 * (i % 4)
        val = dot(half_rows(pair.at[0], 0, ny // 2), pick(at, 16, 32))
        val = val + dot(half_rows(pair.at[1], 0, ny // 2), pick(at + 16, 16, 32))
        if i % 4 == 0:
            acc = val
        else:
            acc = acc + val
        if i % 4 == 3 or i == n3 - 1:
            bc3[(i // 4) * ny3 : (i // 4 + 1) * ny3] = acc


def ring_pick(split):
    i = lax.broadcasted_iota(jnp.int32, (128, 128), 0)
    o = lax.broadcasted_iota(jnp.int32, (128, 128), 1)
    return jnp.where(o == jnp.where(i < split, i // 2, i // 2 + 64), 0.125, 0.0).astype(F32)


def clear_pads(*refs):
    for ref in refs:
        n, rows, _ = ref.shape
        for x in (0, n - 1):
            ref[x] = jnp.zeros(ref.shape[1:], F32)

        def one(x, _):
            ref[x, 0:8] = jnp.zeros((8, 128), F32)
            ref[x, rows - 8 : rows] = jnp.zeros((8, 128), F32)

        fine_loop(0, n, one, 6)


def spread(src, dst, mat, c, planes, skip, r_dst, rows, tmp):
    n = src.shape[0]
    p = dot(src, mat)
    tmp[pl.ds(0, n, stride=2)] = p
    tmp[pl.ds(1, n, stride=2)] = p
    for r in chunks(rows):
        rr = slice(r_dst + r, r_dst + r + 8)
        val = tmp[skip + r : skip + r + 8]
        for x in planes:
            dst[0][x, rr] = dst[0][x, rr] + jnp.where(c[0][x, rr] > 0.0, val, 0.0)


def select_mat(fn):
    i = lax.broadcasted_iota(jnp.int32, (128, 128), 0)
    o = lax.broadcasted_iota(jnp.int32, (128, 128), 1)
    return jnp.where(i == fn(o), 1.0, 0.0).astype(F32)


def coarse_kernel(gy, gz, blocks, *s):
    v1_in, c1 = s[0], (s[1],)
    a1, q1 = [(s[2 + j],) for j in range(6)], (s[8],)
    v2_in, c2 = s[9], (s[10],)
    a2, q2 = [(s[11 + j],) for j in range(6)], (s[17],)
    v1 = (s[18],)
    s = s[19:]
    w1, v2, w2 = (s[0],), (s[1],), (s[2],)
    c3, b3, v3, w3 = [(s[3 + i],) for i in range(4)]
    a3, q3 = [(s[7 + j],) for j in range(6)], (s[13],)
    tmp = s[14]
    iy, iz = lax.axis_index("gy"), lax.axis_index("gz")
    n3, ny3 = q3[0].shape[:2]
    yb = ny3 // gy
    lane = lanes(yb)
    zero(c3[0], v3[0], w3[0])
    for jy in range(gy):
        ky = lax.bitwise_xor(jnp.int32(jy), iy)
        blk = []
        for jz in range(gz):
            kz = lax.bitwise_xor(jnp.int32(jz), iz)
            blk.append(((kz % 2) * (gz // 2) + kz // 2) * gy + ky)
        for i in range(n3):
            rows = slice((i // 4) * yb, (i // 4 + 1) * yb)
            for ref, o in ((b3[0], 32 * (i % 4)), (c3[0], 32 * (i % 4) + 16)):
                acc = jnp.zeros((yb, 128), F32)
                for jz in range(gz):
                    acc = jnp.where(lane // 16 == jz, rot(blocks[blk[jz], rows], 16 * jz - o), acc)
                ref[1 + i, 8 + yb * jy : 8 + yb * (jy + 1)] = acc
    build_coef(c3, b3, a3, q3, None, 0.015625, False)
    copy_q(v3, q3)
    sweep(v3, w3, a3, q3, True)

    def two(_, carry):
        sweep(w3, v3, a3, q3, True)
        sweep(v3, w3, a3, q3, True)
        return carry

    lax.fori_loop(0, (COARSE - 2) // 2, two, 0)
    v2[0][...] = v2_in[...]
    v1[0][...] = v1_in[...]
    clear_pads(w1[0], w2[0])
    up = select_mat(lambda o: jnp.where(o < 96, o // 2, (o + 128) // 2))
    rows2 = q2[0].shape[1]
    skip = 16 - H2
    start = pl.multiple_of(yb * iy, 8)

    def up2(i, _):
        par = rot(w3[0][1 + i, pl.ds(start, yb + 16)], -16 * iz)
        spread(par, v2, up, c2, (1 + 2 * i, 2 + 2 * i), skip, 8, rows2, tmp)

    fine_loop(0, n3, up2, 2)

    def two2(_, carry):
        sweep(v2, w2, a2, q2)
        sweep(w2, v2, a2, q2)
        return carry

    lax.fori_loop(0, SWEEPS // 2, two2, 0)
    ny1 = 4 * yb
    r0 = ny1 - 8

    def up1(i, _):
        par = v2[0][1 + i, 8 + H2 - 4 : 8 + H2 + ny1 // 2 + 4]
        spread(par, v1, up, c1, (1 + 2 * i, 2 + 2 * i), 0, 8 + r0, ny1 + 16, tmp)

    fine_loop(0, 2 * n3, up1, 2)

    def two1(_, carry):
        sweep(v1, w1, a1, q1, False, r0, ny1 + 16)
        sweep(w1, v1, a1, q1, False, r0, ny1 + 16)
        return carry

    lax.fori_loop(0, SWEEPS // 2, two1, 0)


def spread_fine(v, c, planes, up, tmp):
    n = up.shape[0]
    for half in (0, 1):
        p = up[:, 128 * half : 128 * half + 128]
        tmp[half, pl.ds(0, n, stride=2)] = p
        tmp[half, pl.ds(1, n, stride=2)] = p
    lane = lanes()
    edge = jnp.zeros((8, 128), F32)
    for t in range(2 * n // 8):
        rows = slice(8 + 8 * t, 16 + 8 * t)
        par = tmp[0, 8 * t : 8 * t + 8]
        for x in planes:
            v[0][x, rows] = v[0][x, rows] + jnp.where(c[0][x, rows] > 0.0, par, 0.0)
        g = GW * t
        here = (lane >= g) & (lane < g + GW)
        edge = jnp.where(here, tmp[1, 8 * t : 8 * t + 8], edge)
    for x in planes:
        v[1][x] = v[1][x] + jnp.where(c[1][x] > 0.0, edge, 0.0)


def fine_up_kernel(nsx, keep, *refs):
    c_own, v_own, src = refs[:3]
    n = 7 + 2 * nsx
    r = refs[3:7] + (refs[7 : 7 + nsx], refs[7 + nsx : n])
    vr = refs[n : n + 4] + (refs[n + 4 : n + 4 + nsx], refs[n + 4 + nsx : n + 4 + 2 * nsx])
    n = n + 4 + 2 * nsx
    v1 = refs[n]
    n = n + 1
    if keep:
        c, a, q, d = split_kept(refs[n : n + 17])
        n = n + 17
    sol_hbm, res_hbm = refs[n : n + 2]
    sol, res, sems = refs[-3:]
    s = refs[n + 2 : -3]
    if not keep:
        c, a, q, d = split_kept(s[:17])
        s = s[17:]
    b, v, v2 = (s[0], s[1]), (s[2], s[3]), (s[4], s[5])
    tmp, stage, spread = s[6:9]
    nx, ny, _ = src.shape
    off = 1 + own_offset(nsx)
    if not keep:
        set_up_fine(nsx, c_own, src, r, c, b, a, q, d)
    clear_rim(v, v2)
    load_fine(nsx, 1, (0,), (v_own,), vr, (v,))
    i = lax.broadcasted_iota(jnp.int32, (128, 256), 0)
    o = lax.broadcasted_iota(jnp.int32, (128, 256), 1)
    within = lax.rem(o - 128, GW)
    z = HL - 1 - within
    par = jnp.where(within < HL, 64 + lax.div(z, 2), 128 + lax.shift_right_arithmetic(z, 1))
    mat = jnp.where(i == jnp.where(o < 128, lax.div(o, 2), par), 1.0, 0.0).astype(F32)
    nc = v1.shape[0] - 2
    ix = lax.axis_index("gx")
    half = (ny + 16) // 2
    xp = v[0].shape[0] - 2
    count = (xp + 2) // 2
    c0 = lax.shift_right_arithmetic(nx * ix + 1 - off, 1)
    for j in range(count):
        stage[j * half : (j + 1) * half] = v1[1 + jnp.clip(c0 + j, 0, nc - 1), 4 + ny // 2 : 4 + ny // 2 + half]
    spread[...] = dot(stage[...], mat)

    def up(j, _):
        p = 2 * (c0 + j) - nx * ix + off
        start = pl.multiple_of(half * j, 8)
        spread_fine(v, c, (p, p + 1), spread[pl.ds(start, half)], tmp)
        return 0

    lax.fori_loop(0, count, up, 0)
    v = fine_sweeps(nsx, nx, v, v2, a, q)

    step = nx // 4

    def copies(i):
        at = pl.ds(i * step, step)
        return (
            pltpu.make_async_copy(sol.at[at], sol_hbm.at[at], sems.at[0, i]),
            pltpu.make_async_copy(res.at[at], res_hbm.at[at], sems.at[1, i]),
        )

    def out(x, _):
        def put(t, val):
            w8 = slice(8 * t, 8 * t + 8)
            res[x, w8] = val
            sol[x, w8] = v[0][off + x, 16 + 8 * t : 24 + 8 * t]

        fine_residual(v, a, d, off + x, lambda t: src[x, 8 * t : 8 * t + 8], put)

    for i in range(4):
        fine_loop(i * step, step, out, 2)
        for cp in copies(i):
            cp.start()
    for i in range(4):
        for cp in copies(i):
            cp.wait()


def named(fn, *args):
    out = functools.partial(fn, *args)
    out.__name__ = fn.__name__
    return out


def exchange_rest(na, arrs, y_a, y_b, nsx):
    nx, ny, _ = arrs[0].shape
    rows = ny + 16
    r_a, r_b = swap_even(y_a, "gy"), swap_odd(y_b, "gy")
    (z,) = call(
        named(zpack_kernel, na), [(na * nx, 8, 128)], *arrs, r_a, r_b,
        scratch=[(na * nx * 8, 128)],
    )
    z_a, z_b = swap_even(z, "gz"), swap_odd(z, "gz")
    count = len(face_list(na))
    size = count * 24
    xs = call(named(xframe_kernel, na, nx, nsx), [(size, 128)] * nsx, r_a, r_b, z_a, z_b)
    x2 = swap_x(xs)
    return (r_a, r_b, z_a, z_b), x2


def swap_x(xs):
    out = [swap_even(xs[0], "gx")]
    if len(xs) > 1:
        out.append(swap_odd(xs[1], "gx"))
    return out


def plain_with_halo(block, sides, width):
    for axis, dim in sides:
        count = lax.axis_size(axis)
        forward = [(i, i + 1) for i in range(count - 1)]
        backward = [(target, source) for source, target in forward]
        low = lax.ppermute(
            lax.slice_in_dim(block, block.shape[dim] - width, None, axis=dim), axis, forward
        )
        high = lax.ppermute(lax.slice_in_dim(block, 0, width, axis=dim), axis, backward)
        block = jnp.concatenate([low, block, high], axis=dim)
    return block


def plain_neighbor(padded, axis_dim, offset):
    window = [slice(1, -1), slice(1, -1), slice(1, -1)]
    window[axis_dim] = slice(1 + offset, padded.shape[axis_dim] - 1 + offset)
    return padded[tuple(window)]


def plain_apply_padded(padded_u, padded_c, level_scale):
    center_u = padded_u[1:-1, 1:-1, 1:-1]
    center_c = padded_c[1:-1, 1:-1, 1:-1]
    stencil_sum = jnp.zeros_like(center_u)
    diagonal = jnp.zeros_like(center_u)
    for axis_dim in range(3):
        for offset in (-1, 1):
            face = 0.5 * (center_c + plain_neighbor(padded_c, axis_dim, offset))
            stencil_sum = stencil_sum + face * (center_u - plain_neighbor(padded_u, axis_dim, offset))
            diagonal = diagonal + face
    return (level_scale * stencil_sum, level_scale * diagonal)


def plain_restrict(field):
    size_x, size_y, size_z = field.shape
    return field.reshape(size_x // 2, 2, size_y // 2, 2, size_z // 2, 2).mean(axis=(1, 3, 5))


def plain_prolong(field):
    size_x, size_y, size_z = field.shape
    spread = jnp.broadcast_to(field[:, None, :, None, :, None], (size_x, 2, size_y, 2, size_z, 2))
    return spread.reshape(2 * size_x, 2 * size_y, 2 * size_z)


def plain_coef_halo(coef_value):
    return plain_with_halo(coef_value, (("gx", 0), ("gy", 1), ("gz", 2)), 1)


def plain_residual_of(values, rhs_field, coef_padded, level_scale):
    padded_u = plain_with_halo(values, (("gx", 0), ("gy", 1), ("gz", 2)), 1)
    stencil_sum, diagonal = plain_apply_padded(padded_u, coef_padded, level_scale)
    return rhs_field - stencil_sum


def plain_narrow_sweeps(values, rhs_field, coef_padded, level_scale):
    for sweep_id in range(SWEEPS):
        padded_u = plain_with_halo(values, (("gx", 0), ("gy", 1), ("gz", 2)), 1)
        stencil_sum, diagonal = plain_apply_padded(padded_u, coef_padded, level_scale)
        values = values + W * (rhs_field - stencil_sum) / diagonal
    return values


def plain_smooth(values, level_id, rhs_list, padded_list):
    level_scale = 0.25**level_id
    return plain_narrow_sweeps(values, rhs_list[level_id], padded_list[level_id], level_scale)


def plain_coarse_solve(coarse_rhs, coarse_coef):
    coarse_scale = 0.25**LEVELS
    coarse_pad = plain_coef_halo(coarse_coef)

    def local_step(sweep_id, values):
        padded_u = plain_with_halo(values, (("gx", 0), ("gy", 1), ("gz", 2)), 1)
        stencil_sum, diagonal = plain_apply_padded(padded_u, coarse_pad, coarse_scale)
        return values + W * (coarse_rhs - stencil_sum) / diagonal

    return lax.fori_loop(0, COARSE, local_step, jnp.zeros_like(coarse_rhs))


def plain_body(source, first_guess, cell_classes, class_table):
    cell_coef = jnp.zeros(cell_classes.shape, jnp.float32)
    for class_id in range(CLASSES):
        cell_coef = cell_coef + jnp.where(cell_classes == class_id, class_table[class_id], 0.0)
    coef_list = [cell_coef]
    for level_id in range(LEVELS):
        coef_list.append(plain_restrict(coef_list[-1]))
    top_level = LEVELS
    padded_list = [plain_coef_halo(coef_list[level_id]) for level_id in range(top_level)]
    rhs_list = [source]
    iterate_list = []
    values = first_guess
    for level_id in range(top_level):
        level_scale = 0.25**level_id
        if level_id > 0:
            values = jnp.zeros_like(rhs_list[level_id])
        values = plain_smooth(values, level_id, rhs_list, padded_list)
        iterate_list.append(values)
        rhs_list.append(
            plain_restrict(plain_residual_of(values, rhs_list[level_id], padded_list[level_id], level_scale))
        )
    correction = plain_coarse_solve(rhs_list[LEVELS], coef_list[LEVELS])
    for level_id in reversed(range(top_level)):
        values = iterate_list[level_id] + plain_prolong(correction)
        values = plain_smooth(values, level_id, rhs_list, padded_list)
        correction = values
    final = plain_residual_of(correction, source, padded_list[0], 1.0)
    return (correction, final)


def body(source, first_guess, cell_classes, class_table):
    nx, ny, nz = source.shape
    gx, gy, gz = (lax.axis_size(n) for n in ("gx", "gy", "gz"))
    if (gx, gy, gz, nx, ny, nz) != (2, 4, 4, 16, 64, 128):
        return plain_body(source, first_guess, cell_classes, class_table)
    nsx = 1 if gx == 2 else 2
    xp = nx + nsx * HX
    rows = ny + 16
    full = (nx, ny, 128)

    out = call(
        named(start_kernel, nsx),
        [full, (3 * nx, 8, 128), (3 * nx, 8, 128)] + [(3 * HX - 1, ny, 128)] * nsx,
        source, first_guess, cell_classes, class_table,
        smem=(3,),
    )
    c_own, y_a, y_b, xs = out[0], out[1], out[2], out[3:]
    x1 = swap_x(xs)
    rec, x2 = exchange_rest(3, (c_own, first_guess, source), y_a, y_b, nsx)
    keep = True
    kept_shapes = fine_kept(xp, rows)
    outs = [full, (nx // 2, ny // 2, 128), (nx, 8, 128), (nx, 8, 128)] + [(HX, ny, 128)] * nsx
    work = fine_work(xp, rows) + [(2, ny, 128)]
    out = call(
        named(fine_down_kernel, nsx, keep),
        outs + (kept_shapes if keep else []),
        c_own, first_guess, source, *rec, *x1, *x2,
        scratch=work if keep else kept_shapes + work,
    )
    kept = out[len(outs) :]
    out = out[: len(outs)]
    v0, bc1, vy_a, vy_b, vxs = out[0], out[1], out[2], out[3], out[4:]

    n1, ny1 = nx, ny // 2
    (f1,) = call(join_kernel, [(n1, ny1, 128)], bc1, swap_even(bc1, "gx"))
    vr_a, vr_b = swap_even(vy_a, "gy"), swap_odd(vy_b, "gy")
    vx1 = swap_x(vxs)
    r_a, r_b = swap_even(f1, "gy"), swap_odd(f1, "gy")
    rows1 = 3 * ny1
    z_a, z_b, vz = call(
        mid_z_kernel,
        [(n1 // 2, rows1, 128)] * 2 + [(nx, 8, 128)],
        f1, r_a, r_b, v0, vr_a, vr_b,
        scratch=[(nx * 8, 128)],
    )
    z_a, z_b = swap_even(z_a, "gz"), swap_odd(z_b, "gz")
    vz_a, vz_b = swap_even(vz, "gz"), swap_odd(vz, "gz")
    pad1, bare1 = (n1 + 2, rows1 + 16, 128), (n1, rows1, 128)
    n2, rows2 = n1 // 2, ny1 // 2 + 2 * H2
    pad2, bare2 = (n2 + 2, rows2 + 16, 128), (n2, rows2, 128)
    n3, yb = n1 // 4, ny1 // 4
    kept_mid = [pad1, pad1] + [bare1] * 7 + [pad2, pad2] + [bare2] * 7
    out = call(
        mid_down_kernel,
        kept_mid + [(-(-n3 // 4) * yb, 128), (HX * 24, 128)],
        f1, r_a, r_b, z_a, z_b, vr_a, vr_b, vz_a, vz_b,
        scratch=[pad1, bare1, pad1, pad2, bare2, pad2, (2, 2 * rows2, 128)],
    )
    kept_mid, (bc3, frame) = out[:-2], out[-2:]
    vx2 = [swap_even(frame, "gx")]
    vrec = (vr_a, vr_b, vz_a, vz_b)

    got = jnp.stack([bc3] + [swap_xor(bc3, "gy", m) for m in range(1, gy)])
    bit = gz // 2
    while bit:
        got = jnp.concatenate([got, swap_xor(got, "gz", bit)])
        bit //= 2

    pad3, bare3 = (n3 + 2, gy * yb + 16, 128), (n3, gy * yb, 128)
    (v1,) = call(
        named(coarse_kernel, gy, gz),
        [pad1],
        got, *kept_mid,
        scratch=[pad1, pad2, pad2] + [pad3] * 4 + [bare3] * 7 + [(2 * (ny1 + 16), 128)],
    )
    par_rows = (xp + 2) // 2 * (rows // 2)
    work = fine_work(xp, rows) + [(2, rows, 128), (par_rows, 128), (par_rows, 256)]
    sol, res = call(
        named(fine_up_kernel, nsx, keep),
        [full, full],
        c_own, v0, source, *rec, *x1, *x2, *vrec, *vx1, *vx2, v1, *kept,
        scratch=(work if keep else kept_shapes + work) + [full, full],
        hbm_out=True,
        more=[pltpu.SemaphoreType.DMA((2, 4))],
    )
    return sol, res


def solution(mesh):
    spec = P("gx", "gy", "gz")
    return jax.shard_map(
        body,
        mesh=mesh,
        in_specs=(spec, spec, spec, P()),
        out_specs=(spec, spec),
        check_vma=False,
    )
```

```python
import functools

import math
import jax
import jax.numpy as jnp
from jax import lax
from jax.experimental import pallas as pl
from jax.experimental.pallas import tpu as pltpu
from jax.sharding import PartitionSpec as P

LEVELS = 3
SWEEPS = 4
COARSE = 16
CLASSES = 8
W = 0.85
HX = 5
HL = 6
GW = 2 * HL
UNROLL = 4
H2 = 12
F32 = jnp.float32


def pairs_even(n):
    return [(i, i ^ 1) for i in range(n)]


def pairs_odd(n):
    out = []
    for i in range(1, n - 1, 2):
        out += [(i, i + 1), (i + 1, i)]
    return out


def swap_even(x, axis):
    return lax.ppermute(x, axis, pairs_even(lax.axis_size(axis)))


def swap_odd(x, axis):
    return lax.ppermute(x, axis, pairs_odd(lax.axis_size(axis)))


def swap_xor(x, axis, m):
    return lax.ppermute(x, axis, [(i, i ^ m) for i in range(lax.axis_size(axis))])


def even(axis):
    return lax.rem(lax.axis_index(axis), 2) == 0


def call(body, outs, *args, scratch=(), smem=(), hbm=(), hbm_out=False, more=(), alias=None):
    specs = [
        pl.BlockSpec(memory_space=pltpu.SMEM if i in smem else pltpu.HBM if i in hbm else pltpu.VMEM)
        for i in range(len(args))
    ]
    shapes = [jax.ShapeDtypeStruct(s, F32) if hbm_out else pltpu.VMEM(s, F32) for s in outs]
    space = pl.ANY if hbm_out else pltpu.VMEM
    spaces = [pltpu.HBM if i in hbm or i in smem else pltpu.VMEM for i in range(len(args))]
    args = [
        a if m is None or (m is pltpu.VMEM and a.dtype != F32)
        else pltpu.with_memory_space_constraint(a, m)
        for a, m in zip(args, spaces)
    ]
    limit = 4 * sum(math.prod(s) for s in scratch) + 6 * 2**20
    return pl.pallas_call(
        body,
        out_shape=shapes,
        in_specs=specs,
        out_specs=[pl.BlockSpec(memory_space=space) for _ in outs],
        scratch_shapes=[pltpu.VMEM(s, F32) for s in scratch] + list(more),
        name=getattr(body, "__name__", None) or body.func.__name__,
        compiler_params=pltpu.CompilerParams(vmem_limit_bytes=limit),
        input_output_aliases=alias or {},
    )(*args)


def lanes(rows=8):
    return lax.broadcasted_iota(jnp.int32, (rows, 128), 1)


def rot(x, shift):
    if isinstance(shift, int):
        shift = shift % 128
        if shift == 0:
            return x
    else:
        shift = lax.rem(shift + 1024, 128)
    return pltpu.roll(x, shift, 1)


def face_start(axis, total, width, want_even):
    hi = even(axis) if want_even else jnp.logical_not(even(axis))
    return jnp.where(hi, total - width, 0)


def look_up(k, table):
    acc = jnp.full(k.shape, table[0], F32)
    for i in range(1, CLASSES):
        acc = jnp.where(k == i, table[i], acc)
    return acc


def face_kernel(src, guess, cls, table, y_a, y_b, x_out, *s):
    k_x, k_a, k_b, sems = s
    nx, ny, _ = src.shape
    p5 = face_start("gx", nx, HX, True)
    p4 = face_start("gx", nx, HX - 1, True)
    r_a = pl.multiple_of(face_start("gy", ny, 8, True), 8)
    r_b = pl.multiple_of(face_start("gy", ny, 8, False), 8)
    copies = [
        (cls.at[pl.ds(p5, HX)], k_x),
        (cls.at[:, pl.ds(r_a, 8)], k_a),
        (cls.at[:, pl.ds(r_b, 8)], k_b),
        (guess.at[pl.ds(p5, HX)], x_out.at[HX : 2 * HX]),
        (src.at[pl.ds(p4, HX - 1)], x_out.at[2 * HX : 3 * HX - 1]),
        (guess.at[:, pl.ds(r_a, 8)], y_a.at[nx : 2 * nx]),
        (src.at[:, pl.ds(r_a, 8)], y_a.at[2 * nx : 3 * nx]),
        (guess.at[:, pl.ds(r_b, 8)], y_b.at[nx : 2 * nx]),
        (src.at[:, pl.ds(r_b, 8)], y_b.at[2 * nx : 3 * nx]),
    ]
    copies = [pltpu.make_async_copy(f, t, sems.at[i]) for i, (f, t) in enumerate(copies)]
    for cp in copies:
        cp.start()
    for cp in copies[:3]:
        cp.wait()
    for f in range(HX):
        x_out[f] = look_up(k_x[f], table)
    for x in range(nx):
        y_a[x] = look_up(k_a[x], table)
        y_b[x] = look_up(k_b[x], table)
    for cp in copies[3:]:
        cp.wait()


def load_kernel(src, guess, cls, table, c_out, guess_out, src_out, k, sems):
    nx = src.shape[0]
    half = nx // 2
    copies = []
    for h in range(2):
        at = pl.ds(h * half, half)
        copies.append((cls.at[at], k.at[at]))
    for h in range(2):
        at = pl.ds(h * half, half)
        copies.append((guess.at[at], guess_out.at[at]))
        copies.append((src.at[at], src_out.at[at]))
    copies = [pltpu.make_async_copy(f, t, sems.at[i]) for i, (f, t) in enumerate(copies)]
    for cp in copies:
        cp.start()

    def plane(x, _):
        c_out[x] = look_up(k[x], table)

    for h in range(2):
        copies[h].wait()
        fine_loop(h * half, half, plane, 2)
    for cp in copies[2:]:
        cp.wait()


def zpack_kernel(na, *refs):
    arrs = refs[:na]
    r_a, r_b, z, work = refs[na:]
    nx, ny, _ = arrs[0].shape
    tiles = ny // 8 + 2
    ey = even("gy")
    lane = lanes()
    for k in range(na):
        for x in range(nx):
            acc = jnp.zeros((8, 128), F32)
            va, vb = r_a[k * nx + x], r_b[k * nx + x]
            for t in range(tiles):
                if t == 0:
                    v = jnp.where(ey, vb, va)
                elif t == tiles - 1:
                    v = jnp.where(ey, va, vb)
                else:
                    v = arrs[k][x, (t - 1) * 8 : t * 8]
                g = GW * t
                acc = jnp.where((lane >= g) & (lane < g + GW), rot(v, g + HL), acc)
            work[(k * nx + x) * 8 : (k * nx + x) * 8 + 8] = acc
    mirror = select_mat(lambda o: o + (GW - 1) - 2 * lax.rem(o, GW))
    out = dot(work[...], mirror)
    for j in range(na * nx):
        z[j] = out[8 * j : 8 * j + 8]


def halo_of(z_a, z_b, i):
    ez = even("gz")
    a, b = z_a[i], z_b[i]
    within = lax.rem(lanes(), GW)
    return jnp.where(within < HL, jnp.where(ez, a, b), jnp.where(ez, b, a))


def face_list(na):
    widths = (HX, HX, HX - 1)
    return [(k, f, widths[k]) for k in range(na) for f in range(widths[k])]


def frame_list(na):
    out, row = [], 0
    for k in range(na):
        width = (HX, HX, HX - 1)[k]
        for dx in range(1, width):
            out.append((k, dx, row, width - dx))
            row += 2 * (width - dx)
    return out, -(-row // 8) * 8


def frame_rows(na):
    items, base = frame_list(na)
    return base + 8 * len(items)


def xframe_kernel(na, nx, r_a, r_b, z_a, z_b, x_out):
    ey = even("gy")
    items, base = frame_list(na)
    for j, (k, dx, row, w) in enumerate(items):
        p = k * nx + jnp.where(even("gx"), nx - dx, dx - 1)
        va, vb = r_a[p], r_b[p]
        x_out[row : row + w] = jnp.where(ey, vb, va)[8 - w : 8]
        x_out[row + w : row + 2 * w] = jnp.where(ey, va, vb)[0:w]
        x_out[base + j * 8 : base + j * 8 + 8] = halo_of(z_a, z_b, p)


def own_offset(nsx):
    return HX * lax.axis_index("gx") if nsx == 1 else HX


def assemble_own(k, m, h, own, r_a, r_b, z_a, z_b):
    nx, ny, _ = own.shape
    off = 1 + own_offset(1)
    ey = even("gy")

    def one(x, _):
        va, vb = r_a[k * nx + x], r_b[k * nx + x]
        m[off + x, 8:16] = jnp.where(ey, vb, va)
        m[off + x, 16 : 16 + ny] = own[x]
        m[off + x, 16 + ny : 24 + ny] = jnp.where(ey, va, vb)
        h[off + x] = halo_of(z_a, z_b, k * nx + x)

    fine_loop(0, nx, one, 2)


def assemble_x(na, k, m, h, nx, x1, x2):
    off = 1 + own_offset(1)
    hi = even("gx")
    ny = x1.shape[1]
    items, base = frame_list(na)
    for j, (kk, f, w) in enumerate(face_list(na)):
        if kk == k:
            p = off + jnp.where(hi, nx, -w) + f
            m[p, 8:16] = jnp.zeros((8, 128), F32)
            m[p, 16 : 16 + ny] = x1[j]
            m[p, 16 + ny : 24 + ny] = jnp.zeros((8, 128), F32)
            h[p] = jnp.zeros((8, 128), F32)
    for j, (kk, dx, row, w) in enumerate(items):
        if kk == k:
            p = off + jnp.where(hi, nx + dx - 1, -dx)
            m[p, 16 - w : 16] = x2[row : row + w]
            m[p, 16 + ny : 16 + ny + w] = x2[row + w : row + 2 * w]
            h[p] = x2[base + j * 8 : base + j * 8 + 8]


def zshift(vals, wrap=True):
    lo = lanes(vals[0].shape[0])
    down = [rot(v, 1) for v in vals]
    up = [rot(v, -1) for v in vals]
    if len(vals) == 2:
        first, last = lo == 0, lo == 127
        down = [jnp.where(first, down[1 - t], down[t]) for t in (0, 1)]
        up = [jnp.where(last, up[1 - t], up[t]) for t in (0, 1)]
    return down, up


def neighbours(refs, x, r, n):
    vals = [ref[x, pl.ds(8 + r, n)] for ref in refs]
    down, up = zshift(vals)
    out = []
    for t, ref in enumerate(refs):
        out.append(
            (
                ref[x - 1, pl.ds(8 + r, n)],
                ref[x + 1, pl.ds(8 + r, n)],
                ref[x, pl.ds(7 + r, n)],
                ref[x, pl.ds(9 + r, n)],
                down[t],
                up[t],
            )
        )
    return vals, out


def zero(*refs):
    for ref in refs:

        def one(x, _):
            ref[x] = jnp.zeros(ref.shape[1:], F32)
            return 0

        lax.fori_loop(0, ref.shape[0], one, 0)


def chunks(rows, n=8):
    return range(0, rows, n)


def build_coef(c, b, a, q, d, scale, full_lanes):
    nx, rows = c[0].shape[0] - 2, c[0].shape[1] - 16

    def plane(x, _):
        for r in chunks(rows):
            vals, nb = neighbours(c, x, r, 8)
            lane = lanes()
            for t in range(len(c)):
                six = list(nb[t])
                if full_lanes:
                    six[4] = jnp.where(lane == 0, 0.0, six[4])
                    six[5] = jnp.where(lane == 127, 0.0, six[5])
                total = 6.0 * vals[t] + (((six[0] + six[1]) + (six[2] + six[3])) + (six[4] + six[5]))
                inside = vals[t] > 0.0
                g = jnp.where(inside, W / jnp.where(inside, total, 1.0), 0.0)
                rw = pl.ds(r, 8)
                for j in range(6):
                    face = g * (vals[t] + six[j])
                    if full_lanes and j == 4:
                        face = jnp.where(lane == 0, 0.0, face)
                    if full_lanes and j == 5:
                        face = jnp.where(lane == 127, 0.0, face)
                    a[j][t][x - 1, rw] = face
                q[t][x - 1, rw] = g * ((2.0 / scale) * b[t][x, pl.ds(8 + r, 8)])
                if d is not None:
                    d[t][x - 1, rw] = total * (0.5 * scale / W)

    fine_loop(1, nx, plane, 2)


def weighted(a, vals, nb, t, x, rw):
    s = a[0][t][x - 1, rw] * nb[t][0] + a[1][t][x - 1, rw] * nb[t][1]
    u = a[2][t][x - 1, rw] * nb[t][2] + a[3][t][x - 1, rw] * nb[t][3]
    w = a[4][t][x - 1, rw] * nb[t][4] + a[5][t][x - 1, rw] * nb[t][5]
    return (s + u) + w


def sweep(src, dst, a, q, unroll=False, r0=0, rows=None):
    nx, rows = src[0].shape[0] - 2, rows or src[0].shape[1] - 16

    def plane(x, _):
        for r in range(r0, r0 + rows, 8):
            vals, nb = neighbours(src, x, r, 8)
            rw = pl.ds(r, 8)
            for t in range(len(src)):
                dst[t][x, pl.ds(8 + r, 8)] = ((1.0 - W) * vals[t] + q[t][x - 1, rw]) + weighted(
                    a, vals, nb, t, x, rw
                )

    if unroll:
        for x in range(1, nx + 1):
            plane(x, 0)
    else:
        fine_loop(1, nx, plane, UNROLL)


def copy_q(dst, q):
    def plane(x, _):
        for t in range(len(q)):
            dst[t][x + 1, 8 : 8 + q[t].shape[1]] = q[t][x]
        return 0

    lax.fori_loop(0, q[0].shape[0], plane, 0)


def residual_rows(v, b, a, d, x, r, n=8):
    vals, nb = neighbours(v, x, r, n)
    rw = pl.ds(r, n)
    return b - d[0][x - 1, rw] * (W * vals[0] - weighted(a, vals, nb, 0, x, rw))


def pick(shift_out, cols, limit):
    i = lax.broadcasted_iota(jnp.int32, (128, 128), 0)
    o = lax.broadcasted_iota(jnp.int32, (128, 128), 1)
    return jnp.where((i // 2 == o - shift_out) & (i < limit), 0.125, 0.0).astype(F32)


def dot(a, b):
    bf = jnp.bfloat16
    b = b.astype(bf)
    hi = a.astype(bf)
    rest = a - hi.astype(F32)
    mid = rest.astype(bf)
    lo = (rest - mid.astype(F32)).astype(bf)
    one = lambda p: lax.dot_general(p, b, (((1,), (0,)), ((), ())), preferred_element_type=F32)
    return one(hi) + (one(mid) + one(lo))


def half_rows(ref, r0, n):
    return ref[pl.ds(r0, n // 2, stride=2)] + ref[pl.ds(r0 + 1, n // 2, stride=2)]


def fine_loop(lo, count, plane, unroll):
    unroll = max(u for u in range(1, unroll + 2) if count % u == 0)

    def group(i, _):
        for u in range(unroll):
            plane(lo + i * unroll + u, 0)
        return 0

    lax.fori_loop(0, count // unroll, group, 0)


def fine_each(m, h, x, tiles, with_h, emit):
    lane = lanes()
    hv = h[x]
    edge = hv
    for t in tiles:
        g = GW * t
        v = m[x, 8 + 8 * t : 16 + 8 * t]
        beside = rot(hv, -(g + HL))
        down = jnp.where(lane == 0, beside, rot(v, 1))
        up = jnp.where(lane == 127, beside, rot(v, -1))
        six = (
            m[x - 1, 8 + 8 * t : 16 + 8 * t],
            m[x + 1, 8 + 8 * t : 16 + 8 * t],
            m[x, 7 + 8 * t : 15 + 8 * t],
            m[x, 9 + 8 * t : 17 + 8 * t],
            down,
            up,
        )
        emit(0, t, v, six)
        if with_h:
            edge = jnp.where((lane >= g) & (lane < g + GW), rot(v, g + HL), edge)
    if with_h:
        row = lax.broadcasted_iota(jnp.int32, (8, 128), 0)
        within = lax.rem(lane, GW)
        above, below = pltpu.roll(hv, 1, 0), pltpu.roll(hv, 7, 0)
        six = (
            h[x - 1],
            h[x + 1],
            jnp.where(row == 0, rot(above, GW), above),
            jnp.where(row == 7, rot(below, -GW), below),
            jnp.where(within == HL - 1, edge, rot(hv, -1)),
            jnp.where(within == HL, edge, rot(hv, 1)),
        )
        emit(1, 0, hv, six)


def cut(part, ref, x, t, pad):
    if part == 1:
        return (x, slice(0, 8))
    r = 8 * t + (8 if pad else 0)
    return (x, slice(r, r + 8))


def fine_coef(c, b, a, q, d, lo, count):
    tiles = range((c[0].shape[1] - 16) // 8)

    def plane(x, _):
        def emit(part, t, v, six):
            total = 6.0 * v + (((six[0] + six[1]) + (six[2] + six[3])) + (six[4] + six[5]))
            inside = v > 0.0
            g = jnp.where(inside, W / jnp.where(inside, total, 1.0), 0.0)
            at = cut(part, None, x - 1, t, False)
            for j in range(6):
                a[j][part][at] = g * (v + six[j])
            q[part][at] = g * (2.0 * b[part][cut(part, None, x, t, True)])
            if part == 0:
                d[at] = total * (0.5 / W)

        fine_each(c[0], c[1], x, tiles, True, emit)

    fine_loop(lo, count, plane, UNROLL)


def gather_sum(a, part, at, six):
    s = a[0][part][at] * six[0] + a[1][part][at] * six[1]
    u = a[2][part][at] * six[2] + a[3][part][at] * six[3]
    w = a[4][part][at] * six[4] + a[5][part][at] * six[5]
    return (s + u) + w


def fine_sweep(src, dst, a, q, lo, count):
    tiles = range((src[0].shape[1] - 16) // 8)

    def plane(x, _):
        def emit(part, t, v, six):
            at = cut(part, None, x - 1, t, False)
            dst[part][cut(part, None, x, t, True)] = (
                (1.0 - W) * v + q[part][at]
            ) + gather_sum(a, part, at, six)

        fine_each(src[0], src[1], x, tiles, True, emit)

    fine_loop(lo, count, plane, UNROLL)


def fine_residual(v, a, d, x, b_tile, put):
    def emit(part, t, val, six):
        at = cut(part, None, x - 1, t, False)
        put(t - 1, b_tile(t - 1) - d[at] * (W * val - gather_sum(a, part, at, six)))

    fine_each(v[0], v[1], x, range(1, (v[0].shape[1] - 16) // 8 - 1), False, emit)


def fine_range(nsx, nx, extra):
    off = own_offset(nsx)
    xp = nx + nsx * HX
    lo = jnp.maximum(off - extra, 0) + 1
    return lo, nx + nsx * extra


def fine_kept(xp, rows):
    m, h = (xp, rows, 128), (xp, 8, 128)
    return [(xp + 2, rows + 16, 128), (xp + 2, 8, 128)] + [m, h] * 7 + [m]


def split_kept(s):
    two = lambda i: (s[i], s[i + 1])
    return two(0), [two(2 + 2 * j) for j in range(6)], two(14), s[16]


def clear_rim(*pairs):
    for m, h in pairs:
        n, rows, _ = m.shape
        for x in (0, n - 1):
            m[x] = jnp.zeros(m.shape[1:], F32)
            h[x] = jnp.zeros(h.shape[1:], F32)

        def one(x, _):
            m[x, 0:8] = jnp.zeros((8, 128), F32)
            m[x, rows - 8 : rows] = jnp.zeros((8, 128), F32)
            return 0

        lax.fori_loop(0, n, one, 0)


def near_far():
    ix = lax.axis_index("gx")
    return 1 + (HX + 1) * ix, jnp.where(ix == 0, 16, 2)


def fine_sweeps(nx, v, w, a, q):
    for _ in range(SWEEPS - 1):
        lo, count = fine_range(1, nx, HX - 1)
        fine_sweep(w, v, a, q, lo, count)
        v, w = w, v
    return w


def fine_prep_kernel(c_own, guess, src, r_a, r_b, z_a, z_b, *s):
    c, a, q, d = split_kept(s[:17])
    b, v, w = (s[17], s[18]), (s[19], s[20]), (s[21], s[22])
    clear_rim(c, v, w)
    for k, own, (m, h) in ((0, c_own, c), (1, guess, v), (2, src, b)):
        assemble_own(k, m, h, own, r_a, r_b, z_a, z_b)
    lo, _ = near_far()
    nx = src.shape[0]
    fine_coef(c, b, a, q, d, lo, nx - 1)
    fine_sweep(v, w, a, q, lo, nx - 1)


def fine_down_kernel(c_own, src, x1, x2, *refs):
    s = refs[23:46]
    v_out, bc, y_a, y_b, xf = refs[46:51]
    pair = refs[51]
    c, a, q, d = split_kept(s[:17])
    b, v, w = (s[17], s[18]), (s[19], s[20]), (s[21], s[22])
    nx, ny, _ = src.shape
    off = 1 + own_offset(1)
    for k, (m, h) in ((0, c), (1, v), (2, b)):
        assemble_x(3, k, m, h, nx, x1, x2)
    _, lo = near_far()
    fine_coef(c, b, a, q, d, lo, HX)
    fine_sweep(v, w, a, q, lo, HX)
    v = fine_sweeps(nx, v, w, a, q)
    pb, pc = pick(0, 64, 128), pick(64, 64, 128)

    def coarse(i, _):
        x = off + 2 * i
        rs = [None] * (ny // 8)

        def first(t, val):
            rs[t] = val

        def second(t, val):
            pair[0, 8 * t : 8 * t + 8] = rs[t] + val

        for o, put in ((0, first), (1, second)):
            fine_residual(
                v, a, d, x + o, lambda t: src[2 * i + o, 8 * t : 8 * t + 8], put
            )
        for t in range(ny // 8):
            w8 = slice(8 * t, 8 * t + 8)
            pair[1, w8] = c_own[2 * i, w8] + c_own[2 * i + 1, w8]
            v_out[2 * i, w8] = v[0][x, 16 + 8 * t : 24 + 8 * t]
            v_out[2 * i + 1, w8] = v[0][x + 1, 16 + 8 * t : 24 + 8 * t]
        bc[i] = dot(half_rows(pair.at[0], 0, ny), pb) + dot(half_rows(pair.at[1], 0, ny), pc)
        return 0

    lax.fori_loop(0, nx // 2, coarse, 0)
    p5 = face_start("gx", nx, HX, True)
    for f in range(HX):
        xf[f] = v_out[p5 + f]
    for ref, flag in ((y_a, True), (y_b, False)):
        r = pl.multiple_of(face_start("gy", ny, 8, flag), 8)
        ref[...] = v_out[:, pl.ds(r, 8), :]


def join_kernel(own, other, full):
    n = own.shape[0]
    ix = lax.axis_index("gx")
    full[pl.ds(n * ix, n)] = own[...]
    full[pl.ds(n - n * ix, n)] = other[...]


def mid_rows(full, r_a, r_b, x, t, tiles):
    rows = slice((t % tiles) * 8, (t % tiles) * 8 + 8)
    if t < tiles:
        return jnp.where(even("gy"), r_b[x, rows], r_a[x, rows])
    if t >= 2 * tiles:
        return jnp.where(even("gy"), r_a[x, rows], r_b[x, rows])
    return full[x, rows]


def mid_z_kernel(full, r_a, r_b, v0, vr_a, vr_b, z_a, z_b, vz, work):
    nx, ny, _ = full.shape
    tiles = ny // 8
    ez = even("gz")
    low = lax.rem(lanes(), 64) < 32

    def pair(i, _):
        for t in range(3 * tiles):
            e = mid_rows(full, r_a, r_b, 2 * i, t, tiles)
            o = mid_rows(full, r_a, r_b, 2 * i + 1, t, tiles)
            first = jnp.where(low, e, rot(o, 32))
            last = jnp.where(low, rot(o, -32), e)
            z_a[i, t * 8 : t * 8 + 8] = jnp.where(ez, last, first)
            z_b[i, t * 8 : t * 8 + 8] = jnp.where(ez, first, last)

    fine_loop(0, nx // 2, lambda i, c: pair(i, c), 2)
    zpack_kernel(1, v0, vr_a, vr_b, vz, work)


def mid_down_kernel(full, r_a, r_b, z_a, z_b, vr_a, vr_b, vz_a, vz_b, *s):
    v1_out, c = s[0], (s[1],)
    a, q = [(s[2 + j],) for j in range(6)], (s[8],)
    v2_out, c2 = s[9], (s[10],)
    a2, q2 = [(s[11 + j],) for j in range(6)], (s[17],)
    bc3, frame = s[18], s[19]
    b, d, w = (s[20],), (s[21],), (s[22],)
    b2, d2, w2 = (s[23],), (s[24],), (s[25],)
    pair = s[26]
    xframe_kernel(1, vr_a.shape[0], vr_a, vr_b, vz_a, vz_b, frame)
    v, v2 = (v1_out,), (v2_out,)
    nx, ny, _ = full.shape
    tiles = ny // 8
    ez = even("gz")
    lane = lanes()
    own, low = lane < 64, lax.rem(lane, 64) < 32
    clear_pads(c[0], v[0], w[0], c2[0], v2[0], w2[0])

    def place(x, t, mine, side):
        rows = slice(8 + t * 8, 16 + t * 8)
        b[0][x + 1, rows] = jnp.where(own, mine, rot(side, 64))
        c[0][x + 1, rows] = jnp.where(own, rot(mine, 64), side)

    def two(i, _):
        for t in range(3 * tiles):
            za, zb = z_a[i, t * 8 : t * 8 + 8], z_b[i, t * 8 : t * 8 + 8]
            right = jnp.where(ez, za, zb)
            left = jnp.where(ez, zb, za)
            e = mid_rows(full, r_a, r_b, 2 * i, t, tiles)
            o = mid_rows(full, r_a, r_b, 2 * i + 1, t, tiles)
            place(2 * i, t, e, jnp.where(low, right, left))
            place(2 * i + 1, t, o, jnp.where(low, rot(right, -32), rot(left, 32)))

    fine_loop(0, nx // 2, two, 2)
    build_coef(c, b, a, q, d, 0.25, False)
    copy_q(w, q)
    sweep(w, v, a, q)
    sweep(v, w, a, q)
    sweep(w, v, a, q)
    rows2 = ny // 2 + 2 * H2
    r0 = ny - 2 * H2
    mat = ring_pick(96)

    def down(i, _):
        x = 1 + 2 * i
        for r in chunks(2 * rows2):
            rp = pl.ds(8 + r0 + r, 8)
            e = residual_rows(v, b[0][x, rp], a, d, x, r0 + r)
            o = residual_rows(v, b[0][x + 1, rp], a, d, x + 1, r0 + r)
            pair[0, pl.ds(r, 8)] = e + o
            pair[1, pl.ds(r, 8)] = c[0][x, rp] + c[0][x + 1, rp]
        b2[0][1 + i, 8 : 8 + rows2] = dot(half_rows(pair.at[0], 0, 2 * rows2), mat)
        c2[0][1 + i, 8 : 8 + rows2] = dot(half_rows(pair.at[1], 0, 2 * rows2), mat)

    fine_loop(0, nx // 2, down, 2)
    build_coef(c2, b2, a2, q2, d2, 0.0625, False)
    copy_q(w2, q2)
    sweep(w2, v2, a2, q2)
    sweep(v2, w2, a2, q2)
    sweep(w2, v2, a2, q2)
    n3, ny3 = nx // 4, ny // 4
    for i in range(n3):
        x = 1 + 2 * i
        for r in chunks(ny // 2):
            rp = pl.ds(8 + H2 + r, 8)
            e = residual_rows(v2, b2[0][x, rp], a2, d2, x, H2 + r)
            o = residual_rows(v2, b2[0][x + 1, rp], a2, d2, x + 1, H2 + r)
            pair[0, pl.ds(r, 8)] = e + o
            pair[1, pl.ds(r, 8)] = c2[0][x, rp] + c2[0][x + 1, rp]
        at = 32 * (i % 4)
        val = dot(half_rows(pair.at[0], 0, ny // 2), pick(at, 16, 32))
        val = val + dot(half_rows(pair.at[1], 0, ny // 2), pick(at + 16, 16, 32))
        if i % 4 == 0:
            acc = val
        else:
            acc = acc + val
        if i % 4 == 3 or i == n3 - 1:
            bc3[(i // 4) * ny3 : (i // 4 + 1) * ny3] = acc


def ring_pick(split):
    i = lax.broadcasted_iota(jnp.int32, (128, 128), 0)
    o = lax.broadcasted_iota(jnp.int32, (128, 128), 1)
    return jnp.where(o == jnp.where(i < split, i // 2, i // 2 + 64), 0.125, 0.0).astype(F32)


def clear_pads(*refs):
    for ref in refs:
        n, rows, _ = ref.shape
        for x in (0, n - 1):
            ref[x] = jnp.zeros(ref.shape[1:], F32)

        def one(x, _):
            ref[x, 0:8] = jnp.zeros((8, 128), F32)
            ref[x, rows - 8 : rows] = jnp.zeros((8, 128), F32)

        fine_loop(0, n, one, 6)


def spread(src, dst, mat, c, planes, skip, r_dst, rows, tmp):
    n = src.shape[0]
    p = dot(src, mat)
    tmp[pl.ds(0, n, stride=2)] = p
    tmp[pl.ds(1, n, stride=2)] = p
    for r in chunks(rows):
        rr = slice(r_dst + r, r_dst + r + 8)
        val = tmp[skip + r : skip + r + 8]
        for x in planes:
            dst[0][x, rr] = dst[0][x, rr] + jnp.where(c[0][x, rr] > 0.0, val, 0.0)


def select_mat(fn):
    i = lax.broadcasted_iota(jnp.int32, (128, 128), 0)
    o = lax.broadcasted_iota(jnp.int32, (128, 128), 1)
    return jnp.where(i == fn(o), 1.0, 0.0).astype(F32)


def coarse_kernel(gy, gz, blocks, *s):
    v1_in, c1 = s[0], (s[1],)
    a1, q1 = [(s[2 + j],) for j in range(6)], (s[8],)
    v2_in, c2 = s[9], (s[10],)
    a2, q2 = [(s[11 + j],) for j in range(6)], (s[17],)
    v1 = (s[18],)
    s = s[19:]
    w1, v2, w2 = (s[0],), (s[1],), (s[2],)
    c3, b3, v3, w3 = [(s[3 + i],) for i in range(4)]
    a3, q3 = [(s[7 + j],) for j in range(6)], (s[13],)
    tmp = s[14]
    iy, iz = lax.axis_index("gy"), lax.axis_index("gz")
    n3, ny3 = q3[0].shape[:2]
    yb = ny3 // gy
    lane = lanes(yb)
    zero(c3[0], v3[0], w3[0])
    for jy in range(gy):
        ky = lax.bitwise_xor(jnp.int32(jy), iy)
        blk = []
        for jz in range(gz):
            kz = lax.bitwise_xor(jnp.int32(jz), iz)
            blk.append(((kz % 2) * (gz // 2) + kz // 2) * gy + ky)
        for i in range(n3):
            rows = slice((i // 4) * yb, (i // 4 + 1) * yb)
            for ref, o in ((b3[0], 32 * (i % 4)), (c3[0], 32 * (i % 4) + 16)):
                acc = jnp.zeros((yb, 128), F32)
                for jz in range(gz):
                    acc = jnp.where(lane // 16 == jz, rot(blocks[blk[jz], rows], 16 * jz - o), acc)
                ref[1 + i, 8 + yb * jy : 8 + yb * (jy + 1)] = acc
    build_coef(c3, b3, a3, q3, None, 0.015625, False)
    copy_q(v3, q3)
    sweep(v3, w3, a3, q3, True)

    def two(_, carry):
        sweep(w3, v3, a3, q3, True)
        sweep(v3, w3, a3, q3, True)
        return carry

    lax.fori_loop(0, (COARSE - 2) // 2, two, 0)
    v2[0][...] = v2_in[...]
    v1[0][...] = v1_in[...]
    clear_pads(w1[0], w2[0])
    up = select_mat(lambda o: jnp.where(o < 96, o // 2, (o + 128) // 2))
    rows2 = q2[0].shape[1]
    skip = 16 - H2
    start = pl.multiple_of(yb * iy, 8)

    def up2(i, _):
        par = rot(w3[0][1 + i, pl.ds(start, yb + 16)], -16 * iz)
        spread(par, v2, up, c2, (1 + 2 * i, 2 + 2 * i), skip, 8, rows2, tmp)

    fine_loop(0, n3, up2, 2)

    def two2(_, carry):
        sweep(v2, w2, a2, q2)
        sweep(w2, v2, a2, q2)
        return carry

    lax.fori_loop(0, SWEEPS // 2, two2, 0)
    ny1 = 4 * yb
    r0 = ny1 - 8

    def up1(i, _):
        par = v2[0][1 + i, 8 + H2 - 4 : 8 + H2 + ny1 // 2 + 4]
        spread(par, v1, up, c1, (1 + 2 * i, 2 + 2 * i), 0, 8 + r0, ny1 + 16, tmp)

    fine_loop(0, 2 * n3, up1, 2)

    def two1(_, carry):
        sweep(v1, w1, a1, q1, False, r0, ny1 + 16)
        sweep(w1, v1, a1, q1, False, r0, ny1 + 16)
        return carry

    lax.fori_loop(0, SWEEPS // 2, two1, 0)


def spread_fine(v, c, planes, up, tmp):
    n = up.shape[0]
    for half in (0, 1):
        p = up[:, 128 * half : 128 * half + 128]
        tmp[half, pl.ds(0, n, stride=2)] = p
        tmp[half, pl.ds(1, n, stride=2)] = p
    lane = lanes()
    edge = jnp.zeros((8, 128), F32)
    for t in range(2 * n // 8):
        rows = slice(8 + 8 * t, 16 + 8 * t)
        par = tmp[0, 8 * t : 8 * t + 8]
        for x in planes:
            v[0][x, rows] = v[0][x, rows] + jnp.where(c[0][x, rows] > 0.0, par, 0.0)
        g = GW * t
        here = (lane >= g) & (lane < g + GW)
        edge = jnp.where(here, tmp[1, 8 * t : 8 * t + 8], edge)
    for x in planes:
        v[1][x] = v[1][x] + jnp.where(c[1][x] > 0.0, edge, 0.0)


def fine_up_kernel(v_own, src, vr_a, vr_b, vz_a, vz_b, x1, x2, v1, *refs):
    c, a, q, d = split_kept(refs[:17])
    sol_hbm, res_hbm = refs[17:19]
    v, w = (refs[19], refs[20]), (refs[21], refs[22])
    tmp, stage, spread, sol, res, sems = refs[23:]
    nx, ny, _ = src.shape
    off = 1 + own_offset(1)
    clear_rim(v, w)
    assemble_own(0, v[0], v[1], v_own, vr_a, vr_b, vz_a, vz_b)
    assemble_x(1, 0, v[0], v[1], nx, x1, x2)
    i = lax.broadcasted_iota(jnp.int32, (128, 256), 0)
    o = lax.broadcasted_iota(jnp.int32, (128, 256), 1)
    within = lax.rem(o - 128, GW)
    z = HL - 1 - within
    par = jnp.where(within < HL, 64 + lax.div(z, 2), 128 + lax.shift_right_arithmetic(z, 1))
    mat = jnp.where(i == jnp.where(o < 128, lax.div(o, 2), par), 1.0, 0.0).astype(F32)
    nc = v1.shape[0] - 2
    ix = lax.axis_index("gx")
    half = (ny + 16) // 2
    xp = v[0].shape[0] - 2
    count = (xp + 2) // 2
    c0 = lax.shift_right_arithmetic(nx * ix + 1 - off, 1)
    for j in range(count):
        stage[j * half : (j + 1) * half] = v1[1 + jnp.clip(c0 + j, 0, nc - 1), 4 + ny // 2 : 4 + ny // 2 + half]
    spread[...] = dot(stage[...], mat)

    def up(j, _):
        p = 2 * (c0 + j) - nx * ix + off
        start = pl.multiple_of(half * j, 8)
        spread_fine(v, c, (p, p + 1), spread[pl.ds(start, half)], tmp)
        return 0

    lax.fori_loop(0, count, up, 0)
    lo, total = fine_range(1, nx, HX - 1)
    fine_sweep(v, w, a, q, lo, total)
    v = fine_sweeps(nx, v, w, a, q)

    step = nx // 4

    def copies(i):
        at = pl.ds(i * step, step)
        return (
            pltpu.make_async_copy(sol.at[at], sol_hbm.at[at], sems.at[0, i]),
            pltpu.make_async_copy(res.at[at], res_hbm.at[at], sems.at[1, i]),
        )

    def out(x, _):
        def put(t, val):
            w8 = slice(8 * t, 8 * t + 8)
            res[x, w8] = val
            sol[x, w8] = v[0][off + x, 16 + 8 * t : 24 + 8 * t]

        fine_residual(v, a, d, off + x, lambda t: src[x, 8 * t : 8 * t + 8], put)

    for i in range(4):
        fine_loop(i * step, step, out, 2)
        for cp in copies(i):
            cp.start()
    for i in range(4):
        for cp in copies(i):
            cp.wait()


def named(fn, *args):
    out = functools.partial(fn, *args)
    out.__name__ = fn.__name__
    return out


def plain_with_halo(block, sides, width):
    for axis, dim in sides:
        count = lax.axis_size(axis)
        forward = [(i, i + 1) for i in range(count - 1)]
        backward = [(target, source) for source, target in forward]
        low = lax.ppermute(
            lax.slice_in_dim(block, block.shape[dim] - width, None, axis=dim), axis, forward
        )
        high = lax.ppermute(lax.slice_in_dim(block, 0, width, axis=dim), axis, backward)
        block = jnp.concatenate([low, block, high], axis=dim)
    return block


def plain_neighbor(padded, axis_dim, offset):
    window = [slice(1, -1), slice(1, -1), slice(1, -1)]
    window[axis_dim] = slice(1 + offset, padded.shape[axis_dim] - 1 + offset)
    return padded[tuple(window)]


def plain_apply_padded(padded_u, padded_c, level_scale):
    center_u = padded_u[1:-1, 1:-1, 1:-1]
    center_c = padded_c[1:-1, 1:-1, 1:-1]
    stencil_sum = jnp.zeros_like(center_u)
    diagonal = jnp.zeros_like(center_u)
    for axis_dim in range(3):
        for offset in (-1, 1):
            face = 0.5 * (center_c + plain_neighbor(padded_c, axis_dim, offset))
            stencil_sum = stencil_sum + face * (center_u - plain_neighbor(padded_u, axis_dim, offset))
            diagonal = diagonal + face
    return (level_scale * stencil_sum, level_scale * diagonal)


def plain_restrict(field):
    size_x, size_y, size_z = field.shape
    return field.reshape(size_x // 2, 2, size_y // 2, 2, size_z // 2, 2).mean(axis=(1, 3, 5))


def plain_prolong(field):
    size_x, size_y, size_z = field.shape
    spread = jnp.broadcast_to(field[:, None, :, None, :, None], (size_x, 2, size_y, 2, size_z, 2))
    return spread.reshape(2 * size_x, 2 * size_y, 2 * size_z)


def plain_coef_halo(coef_value):
    return plain_with_halo(coef_value, (("gx", 0), ("gy", 1), ("gz", 2)), 1)


def plain_residual_of(values, rhs_field, coef_padded, level_scale):
    padded_u = plain_with_halo(values, (("gx", 0), ("gy", 1), ("gz", 2)), 1)
    stencil_sum, diagonal = plain_apply_padded(padded_u, coef_padded, level_scale)
    return rhs_field - stencil_sum


def plain_narrow_sweeps(values, rhs_field, coef_padded, level_scale):
    for sweep_id in range(SWEEPS):
        padded_u = plain_with_halo(values, (("gx", 0), ("gy", 1), ("gz", 2)), 1)
        stencil_sum, diagonal = plain_apply_padded(padded_u, coef_padded, level_scale)
        values = values + W * (rhs_field - stencil_sum) / diagonal
    return values


def plain_smooth(values, level_id, rhs_list, padded_list):
    level_scale = 0.25**level_id
    return plain_narrow_sweeps(values, rhs_list[level_id], padded_list[level_id], level_scale)


def plain_coarse_solve(coarse_rhs, coarse_coef):
    coarse_scale = 0.25**LEVELS
    coarse_pad = plain_coef_halo(coarse_coef)

    def local_step(sweep_id, values):
        padded_u = plain_with_halo(values, (("gx", 0), ("gy", 1), ("gz", 2)), 1)
        stencil_sum, diagonal = plain_apply_padded(padded_u, coarse_pad, coarse_scale)
        return values + W * (coarse_rhs - stencil_sum) / diagonal

    return lax.fori_loop(0, COARSE, local_step, jnp.zeros_like(coarse_rhs))


def plain_body(source, first_guess, cell_classes, class_table):
    cell_coef = jnp.zeros(cell_classes.shape, jnp.float32)
    for class_id in range(CLASSES):
        cell_coef = cell_coef + jnp.where(cell_classes == class_id, class_table[class_id], 0.0)
    coef_list = [cell_coef]
    for level_id in range(LEVELS):
        coef_list.append(plain_restrict(coef_list[-1]))
    top_level = LEVELS
    padded_list = [plain_coef_halo(coef_list[level_id]) for level_id in range(top_level)]
    rhs_list = [source]
    iterate_list = []
    values = first_guess
    for level_id in range(top_level):
        level_scale = 0.25**level_id
        if level_id > 0:
            values = jnp.zeros_like(rhs_list[level_id])
        values = plain_smooth(values, level_id, rhs_list, padded_list)
        iterate_list.append(values)
        rhs_list.append(
            plain_restrict(plain_residual_of(values, rhs_list[level_id], padded_list[level_id], level_scale))
        )
    correction = plain_coarse_solve(rhs_list[LEVELS], coef_list[LEVELS])
    for level_id in reversed(range(top_level)):
        values = iterate_list[level_id] + plain_prolong(correction)
        values = plain_smooth(values, level_id, rhs_list, padded_list)
        correction = values
    final = plain_residual_of(correction, source, padded_list[0], 1.0)
    return (correction, final)


def body(source, first_guess, cell_classes, class_table):
    nx, ny, nz = source.shape
    gx, gy, gz = (lax.axis_size(n) for n in ("gx", "gy", "gz"))
    if (gx, gy, gz, nx, ny, nz) != (2, 4, 4, 16, 64, 128):
        return plain_body(source, first_guess, cell_classes, class_table)
    xp = nx + HX
    rows = ny + 16
    full = (nx, ny, 128)
    halo = (3 * nx, 8, 128)

    y_a, y_b, x1 = call(
        face_kernel,
        [halo, halo, (3 * HX - 1, ny, 128)],
        source, first_guess, cell_classes, class_table,
        smem=(3,),
        hbm=(0, 1, 2),
        more=[pltpu.VMEM((HX, ny, 128), jnp.int32)]
        + [pltpu.VMEM((nx, 8, 128), jnp.int32)] * 2
        + [pltpu.SemaphoreType.DMA((9,))],
    )
    x1 = swap_even(x1, "gx")
    r_a, r_b = swap_even(y_a, "gy"), swap_odd(y_b, "gy")
    own = call(
        load_kernel,
        [full, full, full],
        source, first_guess, cell_classes, class_table,
        smem=(3,),
        hbm=(0, 1, 2),
        more=[pltpu.VMEM(full, jnp.int32), pltpu.SemaphoreType.DMA((6,))],
    )
    c_own, _, source = own
    (z,) = call(named(zpack_kernel, 3), [halo], *own, r_a, r_b, scratch=[(3 * nx * 8, 128)])
    rec = (r_a, r_b, swap_even(z, "gz"), swap_odd(z, "gz"))
    (x2,) = call(named(xframe_kernel, 3, nx), [(frame_rows(3), 128)], *rec)
    x2 = swap_even(x2, "gx")
    pad = [(xp + 2, rows + 16, 128), (xp + 2, 8, 128)]
    state_shapes = fine_kept(xp, rows) + pad * 3
    state = call(fine_prep_kernel, state_shapes, *own, *rec)
    out = call(
        fine_down_kernel,
        state_shapes
        + [full, (nx // 2, ny // 2, 128), (nx, 8, 128), (nx, 8, 128), (HX, ny, 128)],
        c_own, source, x1, x2, *state,
        scratch=[(2, ny, 128)],
        alias={4 + i: i for i in range(23)},
    )
    kept = out[:17]
    v0, bc1, vy_a, vy_b, vx1 = out[23:]

    n1, ny1 = nx, ny // 2
    (f1,) = call(join_kernel, [(n1, ny1, 128)], bc1, swap_even(bc1, "gx"))
    vr_a, vr_b = swap_even(vy_a, "gy"), swap_odd(vy_b, "gy")
    vx1 = swap_even(vx1, "gx")
    r_a, r_b = swap_even(f1, "gy"), swap_odd(f1, "gy")
    rows1 = 3 * ny1
    z_a, z_b, vz = call(
        mid_z_kernel,
        [(n1 // 2, rows1, 128)] * 2 + [(nx, 8, 128)],
        f1, r_a, r_b, v0, vr_a, vr_b,
        scratch=[(nx * 8, 128)],
    )
    z_a, z_b = swap_even(z_a, "gz"), swap_odd(z_b, "gz")
    vz_a, vz_b = swap_even(vz, "gz"), swap_odd(vz, "gz")
    pad1, bare1 = (n1 + 2, rows1 + 16, 128), (n1, rows1, 128)
    n2, rows2 = n1 // 2, ny1 // 2 + 2 * H2
    pad2, bare2 = (n2 + 2, rows2 + 16, 128), (n2, rows2, 128)
    n3, yb = n1 // 4, ny1 // 4
    kept_mid = [pad1, pad1] + [bare1] * 7 + [pad2, pad2] + [bare2] * 7
    out = call(
        mid_down_kernel,
        kept_mid + [(-(-n3 // 4) * yb, 128), (frame_rows(1), 128)],
        f1, r_a, r_b, z_a, z_b, vr_a, vr_b, vz_a, vz_b,
        scratch=[pad1, bare1, pad1, pad2, bare2, pad2, (2, 2 * rows2, 128)],
    )
    kept_mid, (bc3, frame) = out[:-2], out[-2:]
    vx2 = swap_even(frame, "gx")
    vrec = (vr_a, vr_b, vz_a, vz_b)

    got = jnp.stack([bc3] + [swap_xor(bc3, "gy", m) for m in range(1, gy)])
    bit = gz // 2
    while bit:
        got = jnp.concatenate([got, swap_xor(got, "gz", bit)])
        bit //= 2

    pad3, bare3 = (n3 + 2, gy * yb + 16, 128), (n3, gy * yb, 128)
    (v1,) = call(
        named(coarse_kernel, gy, gz),
        [pad1],
        got, *kept_mid,
        scratch=[pad1, pad2, pad2] + [pad3] * 4 + [bare3] * 7 + [(2 * (ny1 + 16), 128)],
    )
    par_rows = (xp + 2) // 2 * (rows // 2)
    sol, res = call(
        fine_up_kernel,
        [full, full],
        v0, source, *vrec, vx1, vx2, v1, *kept,
        scratch=pad * 2 + [(2, rows, 128), (par_rows, 128), (par_rows, 256), full, full],
        hbm_out=True,
        more=[pltpu.SemaphoreType.DMA((2, 4))],
    )
    return sol, res


def solution(mesh):
    spec = P("gx", "gy", "gz")
    return jax.shard_map(
        body,
        mesh=mesh,
        in_specs=(spec, spec, spec, P()),
        out_specs=(spec, spec),
        check_vma=False,
    )
```

```python
import functools

import math
import jax
import jax.numpy as jnp
from jax import lax
from jax.experimental import pallas as pl
from jax.experimental.pallas import tpu as pltpu
from jax.sharding import PartitionSpec as P

LEVELS = 3
SWEEPS = 4
COARSE = 16
CLASSES = 8
W = 0.85
HX = 5
HL = 6
GW = 2 * HL
UNROLL = 4
H2 = 12
F32 = jnp.float32


def pairs_even(n):
    return [(i, i ^ 1) for i in range(n)]


def pairs_odd(n):
    out = []
    for i in range(1, n - 1, 2):
        out += [(i, i + 1), (i + 1, i)]
    return out


def swap_even(x, axis):
    return lax.ppermute(x, axis, pairs_even(lax.axis_size(axis)))


def swap_odd(x, axis):
    return lax.ppermute(x, axis, pairs_odd(lax.axis_size(axis)))


def swap_xor(x, axis, m):
    return lax.ppermute(x, axis, [(i, i ^ m) for i in range(lax.axis_size(axis))])


def even(axis):
    return lax.rem(lax.axis_index(axis), 2) == 0


def call(body, outs, *args, scratch=(), smem=(), hbm=(), hbm_out=False, more=(), alias=None):
    specs = [
        pl.BlockSpec(memory_space=pltpu.SMEM if i in smem else pltpu.HBM if i in hbm else pltpu.VMEM)
        for i in range(len(args))
    ]
    shapes = [jax.ShapeDtypeStruct(s, F32) if hbm_out else pltpu.VMEM(s, F32) for s in outs]
    space = pl.ANY if hbm_out else pltpu.VMEM
    spaces = [pltpu.HBM if i in hbm or i in smem else pltpu.VMEM for i in range(len(args))]
    args = [
        a if m is None or (m is pltpu.VMEM and a.dtype != F32)
        else pltpu.with_memory_space_constraint(a, m)
        for a, m in zip(args, spaces)
    ]
    limit = 4 * sum(math.prod(s) for s in scratch) + 6 * 2**20
    return pl.pallas_call(
        body,
        out_shape=shapes,
        in_specs=specs,
        out_specs=[pl.BlockSpec(memory_space=space) for _ in outs],
        scratch_shapes=[pltpu.VMEM(s, F32) for s in scratch] + list(more),
        name=getattr(body, "__name__", None) or body.func.__name__,
        compiler_params=pltpu.CompilerParams(vmem_limit_bytes=limit),
        input_output_aliases=alias or {},
    )(*args)


def lanes(rows=8):
    return lax.broadcasted_iota(jnp.int32, (rows, 128), 1)


def rot(x, shift):
    if isinstance(shift, int):
        shift = shift % 128
        if shift == 0:
            return x
    else:
        shift = lax.rem(shift + 1024, 128)
    return pltpu.roll(x, shift, 1)


def face_start(axis, total, width, want_even):
    hi = even(axis) if want_even else jnp.logical_not(even(axis))
    return jnp.where(hi, total - width, 0)


def look_up(k, table):
    acc = jnp.full(k.shape, table[0], F32)
    for i in range(1, CLASSES):
        acc = jnp.where(k == i, table[i], acc)
    return acc


def y_tiles(r_a, r_b, k, x):
    ey = even("gy")
    if r_a.shape[1] == 8:
        va, vb = r_a[x], r_b[x]
        return jnp.where(ey, vb, va), jnp.where(ey, va, vb)
    pick_of = lambda f: (f(r_a), f(r_b))
    if k == 0:
        low, high = pick_of(lambda r: r[x, 1:9]), pick_of(lambda r: r[x, 4:12])
    elif k == 1:
        low = pick_of(lambda r: r[x, 6:14])
        high = pick_of(lambda r: pltpu.roll(r[x, 8:16], 7, 0))
    else:
        low = pick_of(lambda r: pltpu.roll(r[x, 0:8], 4, 0))
        high = pick_of(lambda r: r[x, 0:8])
    return jnp.where(ey, low[1], low[0]), jnp.where(ey, high[0], high[1])


def face_kernel(src, guess, cls, table, y_a, y_b, x_out, *s):
    k_x, k_y, g_y, b_y, sems = s
    nx, ny, _ = src.shape
    p5 = face_start("gx", nx, HX, True)
    p4 = face_start("gx", nx, HX - 1, True)
    hi = [even("gy"), jnp.logical_not(even("gy"))]
    rows = [pl.multiple_of(face_start("gy", ny, 8, flag), 8) for flag in (True, False)]
    copies = [(cls.at[pl.ds(p5, HX)], k_x)]
    for i, r in enumerate(rows):
        copies.append((cls.at[:, pl.ds(r, 8)], k_y.at[i]))
        copies.append((guess.at[:, pl.ds(r, 8)], g_y.at[i]))
        copies.append((src.at[:, pl.ds(r, 8)], b_y.at[i]))
    copies.append((guess.at[pl.ds(p5, HX)], x_out.at[HX : 2 * HX]))
    copies.append((src.at[pl.ds(p4, HX - 1)], x_out.at[2 * HX : 3 * HX - 1]))
    copies = [pltpu.make_async_copy(f, t, sems.at[i]) for i, (f, t) in enumerate(copies)]
    for cp in copies:
        cp.start()
    copies[0].wait()
    for f in range(HX):
        x_out[f] = look_up(k_x[f], table)
    for i, out in ((0, y_a), (1, y_b)):
        for cp in copies[1 + 3 * i : 4 + 3 * i]:
            cp.wait()
        for x in range(nx):
            c8, v8, b8 = look_up(k_y[i, x], table), g_y[i, x], b_y[i, x]
            out[x, 8:16] = jnp.zeros((8, 128), F32)
            out[x, 0:4] = jnp.where(hi[i], b8[4:8], b8[0:4])
            out[x, 4:9] = jnp.where(hi[i], c8[3:8], c8[0:5])
            out[x, 9:14] = jnp.where(hi[i], v8[3:8], v8[0:5])
    for cp in copies[7:]:
        cp.wait()


def load_kernel(src, guess, cls, table, c_out, guess_out, src_out, k, sems):
    nx = src.shape[0]
    half = nx // 2
    copies = []
    for h in range(2):
        at = pl.ds(h * half, half)
        copies.append((cls.at[at], k.at[at]))
    for h in range(2):
        at = pl.ds(h * half, half)
        copies.append((guess.at[at], guess_out.at[at]))
        copies.append((src.at[at], src_out.at[at]))
    copies = [pltpu.make_async_copy(f, t, sems.at[i]) for i, (f, t) in enumerate(copies)]
    for cp in copies:
        cp.start()

    def plane(x, _):
        c_out[x] = look_up(k[x], table)

    for h in range(2):
        copies[h].wait()
        fine_loop(h * half, half, plane, 2)
    for cp in copies[2:]:
        cp.wait()


def zpack_kernel(na, *refs):
    arrs = refs[:na]
    r_a, r_b, z, work = refs[na:]
    nx, ny, _ = arrs[0].shape
    tiles = ny // 8 + 2
    lane = lanes()
    for k in range(na):
        for x in range(nx):
            acc = jnp.zeros((8, 128), F32)
            low, high = y_tiles(r_a, r_b, k, x)
            for t in range(tiles):
                if t == 0:
                    v = low
                elif t == tiles - 1:
                    v = high
                else:
                    v = arrs[k][x, (t - 1) * 8 : t * 8]
                g = GW * t
                acc = jnp.where((lane >= g) & (lane < g + GW), rot(v, g + HL), acc)
            work[(k * nx + x) * 8 : (k * nx + x) * 8 + 8] = acc
    mirror = select_mat(lambda o: o + (GW - 1) - 2 * lax.rem(o, GW))
    out = dot(work[...], mirror)
    for j in range(na * nx):
        z[j] = out[8 * j : 8 * j + 8]


def halo_of(z_a, z_b, i):
    ez = even("gz")
    a, b = z_a[i], z_b[i]
    within = lax.rem(lanes(), GW)
    return jnp.where(within < HL, jnp.where(ez, a, b), jnp.where(ez, b, a))


def face_list(na):
    widths = (HX, HX, HX - 1)
    return [(k, f, widths[k]) for k in range(na) for f in range(widths[k])]


def frame_list(na):
    out, row = [], 0
    for k in range(na):
        width = (HX, HX, HX - 1)[k]
        for dx in range(1, width):
            out.append((k, dx, row, width - dx))
            row += 2 * (width - dx)
    return out, -(-row // 8) * 8


def frame_rows(na):
    items, base = frame_list(na)
    return base + 8 * len(items)


def xframe_kernel(na, nx, r_a, r_b, z_a, z_b, x_out):
    items, base = frame_list(na)
    for j, (k, dx, row, w) in enumerate(items):
        p = jnp.where(even("gx"), nx - dx, dx - 1)
        low, high = y_tiles(r_a, r_b, k, p)
        x_out[row : row + w] = low[8 - w : 8]
        x_out[row + w : row + 2 * w] = high[0:w]
        x_out[base + j * 8 : base + j * 8 + 8] = halo_of(z_a, z_b, k * nx + p)


def own_offset(nsx):
    return HX * lax.axis_index("gx") if nsx == 1 else HX


def assemble_own(k, m, h, own, r_a, r_b, z_a, z_b):
    nx, ny, _ = own.shape
    off = 1 + own_offset(1)

    def one(x, _):
        low, high = y_tiles(r_a, r_b, k, x)
        m[off + x, 8:16] = low
        m[off + x, 16 : 16 + ny] = own[x]
        m[off + x, 16 + ny : 24 + ny] = high
        h[off + x] = halo_of(z_a, z_b, k * nx + x)

    fine_loop(0, nx, one, 2)


def assemble_x(na, k, m, h, nx, x1, x2):
    off = 1 + own_offset(1)
    hi = even("gx")
    ny = x1.shape[1]
    items, base = frame_list(na)
    for j, (kk, f, w) in enumerate(face_list(na)):
        if kk == k:
            p = off + jnp.where(hi, nx, -w) + f
            m[p, 8:16] = jnp.zeros((8, 128), F32)
            m[p, 16 : 16 + ny] = x1[j]
            m[p, 16 + ny : 24 + ny] = jnp.zeros((8, 128), F32)
            h[p] = jnp.zeros((8, 128), F32)
    for j, (kk, dx, row, w) in enumerate(items):
        if kk == k:
            p = off + jnp.where(hi, nx + dx - 1, -dx)
            m[p, 16 - w : 16] = x2[row : row + w]
            m[p, 16 + ny : 16 + ny + w] = x2[row + w : row + 2 * w]
            h[p] = x2[base + j * 8 : base + j * 8 + 8]


def zshift(vals, wrap=True):
    lo = lanes(vals[0].shape[0])
    down = [rot(v, 1) for v in vals]
    up = [rot(v, -1) for v in vals]
    if len(vals) == 2:
        first, last = lo == 0, lo == 127
        down = [jnp.where(first, down[1 - t], down[t]) for t in (0, 1)]
        up = [jnp.where(last, up[1 - t], up[t]) for t in (0, 1)]
    return down, up


def neighbours(refs, x, r, n):
    vals = [ref[x, pl.ds(8 + r, n)] for ref in refs]
    down, up = zshift(vals)
    out = []
    for t, ref in enumerate(refs):
        out.append(
            (
                ref[x - 1, pl.ds(8 + r, n)],
                ref[x + 1, pl.ds(8 + r, n)],
                ref[x, pl.ds(7 + r, n)],
                ref[x, pl.ds(9 + r, n)],
                down[t],
                up[t],
            )
        )
    return vals, out


def zero(*refs):
    for ref in refs:

        def one(x, _):
            ref[x] = jnp.zeros(ref.shape[1:], F32)
            return 0

        lax.fori_loop(0, ref.shape[0], one, 0)


def chunks(rows, n=8):
    return range(0, rows, n)


def build_coef(c, b, a, q, d, scale, full_lanes):
    nx, rows = c[0].shape[0] - 2, c[0].shape[1] - 16

    def plane(x, _):
        for r in chunks(rows):
            vals, nb = neighbours(c, x, r, 8)
            lane = lanes()
            for t in range(len(c)):
                six = list(nb[t])
                if full_lanes:
                    six[4] = jnp.where(lane == 0, 0.0, six[4])
                    six[5] = jnp.where(lane == 127, 0.0, six[5])
                total = 6.0 * vals[t] + (((six[0] + six[1]) + (six[2] + six[3])) + (six[4] + six[5]))
                inside = vals[t] > 0.0
                g = jnp.where(inside, W / jnp.where(inside, total, 1.0), 0.0)
                rw = pl.ds(r, 8)
                for j in range(6):
                    face = g * (vals[t] + six[j])
                    if full_lanes and j == 4:
                        face = jnp.where(lane == 0, 0.0, face)
                    if full_lanes and j == 5:
                        face = jnp.where(lane == 127, 0.0, face)
                    a[j][t][x - 1, rw] = face
                q[t][x - 1, rw] = g * ((2.0 / scale) * b[t][x, pl.ds(8 + r, 8)])
                if d is not None:
                    d[t][x - 1, rw] = total * (0.5 * scale / W)

    fine_loop(1, nx, plane, 2)


def weighted(a, vals, nb, t, x, rw):
    s = a[0][t][x - 1, rw] * nb[t][0] + a[1][t][x - 1, rw] * nb[t][1]
    u = a[2][t][x - 1, rw] * nb[t][2] + a[3][t][x - 1, rw] * nb[t][3]
    w = a[4][t][x - 1, rw] * nb[t][4] + a[5][t][x - 1, rw] * nb[t][5]
    return (s + u) + w


def sweep(src, dst, a, q, unroll=False, r0=0, rows=None):
    nx, rows = src[0].shape[0] - 2, rows or src[0].shape[1] - 16

    def plane(x, _):
        for r in range(r0, r0 + rows, 8):
            vals, nb = neighbours(src, x, r, 8)
            rw = pl.ds(r, 8)
            for t in range(len(src)):
                dst[t][x, pl.ds(8 + r, 8)] = ((1.0 - W) * vals[t] + q[t][x - 1, rw]) + weighted(
                    a, vals, nb, t, x, rw
                )

    if unroll:
        for x in range(1, nx + 1):
            plane(x, 0)
    else:
        fine_loop(1, nx, plane, UNROLL)


def copy_q(dst, q):
    def plane(x, _):
        for t in range(len(q)):
            dst[t][x + 1, 8 : 8 + q[t].shape[1]] = q[t][x]
        return 0

    lax.fori_loop(0, q[0].shape[0], plane, 0)


def residual_rows(v, b, a, d, x, r, n=8):
    vals, nb = neighbours(v, x, r, n)
    rw = pl.ds(r, n)
    return b - d[0][x - 1, rw] * (W * vals[0] - weighted(a, vals, nb, 0, x, rw))


def pick(shift_out, cols, limit):
    i = lax.broadcasted_iota(jnp.int32, (128, 128), 0)
    o = lax.broadcasted_iota(jnp.int32, (128, 128), 1)
    return jnp.where((i // 2 == o - shift_out) & (i < limit), 0.125, 0.0).astype(F32)


def dot(a, b):
    bf = jnp.bfloat16
    b = b.astype(bf)
    hi = a.astype(bf)
    rest = a - hi.astype(F32)
    mid = rest.astype(bf)
    lo = (rest - mid.astype(F32)).astype(bf)
    one = lambda p: lax.dot_general(p, b, (((1,), (0,)), ((), ())), preferred_element_type=F32)
    return one(hi) + (one(mid) + one(lo))


def half_rows(ref, r0, n):
    return ref[pl.ds(r0, n // 2, stride=2)] + ref[pl.ds(r0 + 1, n // 2, stride=2)]


def fine_loop(lo, count, plane, unroll):
    unroll = max(u for u in range(1, unroll + 2) if count % u == 0)

    def group(i, _):
        for u in range(unroll):
            plane(lo + i * unroll + u, 0)
        return 0

    lax.fori_loop(0, count // unroll, group, 0)


def fine_each(m, h, x, tiles, with_h, emit):
    lane = lanes()
    hv = h[x]
    edge = hv
    for t in tiles:
        g = GW * t
        v = m[x, 8 + 8 * t : 16 + 8 * t]
        beside = rot(hv, -(g + HL))
        down = jnp.where(lane == 0, beside, rot(v, 1))
        up = jnp.where(lane == 127, beside, rot(v, -1))
        six = (
            m[x - 1, 8 + 8 * t : 16 + 8 * t],
            m[x + 1, 8 + 8 * t : 16 + 8 * t],
            m[x, 7 + 8 * t : 15 + 8 * t],
            m[x, 9 + 8 * t : 17 + 8 * t],
            down,
            up,
        )
        emit(0, t, v, six)
        if with_h:
            edge = jnp.where((lane >= g) & (lane < g + GW), rot(v, g + HL), edge)
    if with_h:
        row = lax.broadcasted_iota(jnp.int32, (8, 128), 0)
        within = lax.rem(lane, GW)
        above, below = pltpu.roll(hv, 1, 0), pltpu.roll(hv, 7, 0)
        six = (
            h[x - 1],
            h[x + 1],
            jnp.where(row == 0, rot(above, GW), above),
            jnp.where(row == 7, rot(below, -GW), below),
            jnp.where(within == HL - 1, edge, rot(hv, -1)),
            jnp.where(within == HL, edge, rot(hv, 1)),
        )
        emit(1, 0, hv, six)


def cut(part, ref, x, t, pad):
    if part == 1:
        return (x, slice(0, 8))
    r = 8 * t + (8 if pad else 0)
    return (x, slice(r, r + 8))


def fine_coef(c, b, a, q, d, lo, count):
    tiles = range((c[0].shape[1] - 16) // 8)

    def plane(x, _):
        def emit(part, t, v, six):
            total = 6.0 * v + (((six[0] + six[1]) + (six[2] + six[3])) + (six[4] + six[5]))
            inside = v > 0.0
            g = jnp.where(inside, W / jnp.where(inside, total, 1.0), 0.0)
            at = cut(part, None, x - 1, t, False)
            for j in range(6):
                a[j][part][at] = g * (v + six[j])
            q[part][at] = g * (2.0 * b[part][cut(part, None, x, t, True)])
            if part == 0:
                d[at] = total * (0.5 / W)

        fine_each(c[0], c[1], x, tiles, True, emit)

    fine_loop(lo, count, plane, UNROLL)


def gather_sum(a, part, at, six):
    s = a[0][part][at] * six[0] + a[1][part][at] * six[1]
    u = a[2][part][at] * six[2] + a[3][part][at] * six[3]
    w = a[4][part][at] * six[4] + a[5][part][at] * six[5]
    return (s + u) + w


def fine_sweep(src, dst, a, q, lo, count):
    tiles = range((src[0].shape[1] - 16) // 8)

    def plane(x, _):
        def emit(part, t, v, six):
            at = cut(part, None, x - 1, t, False)
            dst[part][cut(part, None, x, t, True)] = (
                (1.0 - W) * v + q[part][at]
            ) + gather_sum(a, part, at, six)

        fine_each(src[0], src[1], x, tiles, True, emit)

    fine_loop(lo, count, plane, UNROLL)


def fine_residual(v, a, d, x, b_tile, put):
    def emit(part, t, val, six):
        at = cut(part, None, x - 1, t, False)
        put(t - 1, b_tile(t - 1) - d[at] * (W * val - gather_sum(a, part, at, six)))

    fine_each(v[0], v[1], x, range(1, (v[0].shape[1] - 16) // 8 - 1), False, emit)


def fine_range(nsx, nx, extra):
    off = own_offset(nsx)
    xp = nx + nsx * HX
    lo = jnp.maximum(off - extra, 0) + 1
    return lo, nx + nsx * extra


def fine_kept(xp, rows):
    m, h = (xp, rows, 128), (xp, 8, 128)
    return [(xp + 2, rows + 16, 128), (xp + 2, 8, 128)] + [m, h] * 7 + [m]


def split_kept(s):
    two = lambda i: (s[i], s[i + 1])
    return two(0), [two(2 + 2 * j) for j in range(6)], two(14), s[16]


def clear_rim(*pairs):
    for m, h in pairs:
        n, rows, _ = m.shape
        for x in (0, n - 1):
            m[x] = jnp.zeros(m.shape[1:], F32)
            h[x] = jnp.zeros(h.shape[1:], F32)

        def one(x, _):
            m[x, 0:8] = jnp.zeros((8, 128), F32)
            m[x, rows - 8 : rows] = jnp.zeros((8, 128), F32)
            return 0

        lax.fori_loop(0, n, one, 0)


def near_far():
    ix = lax.axis_index("gx")
    return 1 + (HX + 1) * ix, jnp.where(ix == 0, 16, 2)


def fine_sweeps(nx, v, w, a, q):
    for _ in range(SWEEPS - 1):
        lo, count = fine_range(1, nx, HX - 1)
        fine_sweep(w, v, a, q, lo, count)
        v, w = w, v
    return w


def fine_prep_kernel(c_own, guess, src, r_a, r_b, z_a, z_b, *s):
    c, a, q, d = split_kept(s[:17])
    b, v, w = (s[17], s[18]), (s[19], s[20]), (s[21], s[22])
    clear_rim(c, v, w)
    for k, own, (m, h) in ((0, c_own, c), (1, guess, v), (2, src, b)):
        assemble_own(k, m, h, own, r_a, r_b, z_a, z_b)
    lo, _ = near_far()
    nx = src.shape[0]
    fine_coef(c, b, a, q, d, lo, nx - 1)
    fine_sweep(v, w, a, q, lo, nx - 1)


def fine_down_kernel(c_own, src, x1, x2, *refs):
    s = refs[23:46]
    v_out, bc, y_a, y_b, xf = refs[46:51]
    pair = refs[51]
    c, a, q, d = split_kept(s[:17])
    b, v, w = (s[17], s[18]), (s[19], s[20]), (s[21], s[22])
    nx, ny, _ = src.shape
    off = 1 + own_offset(1)
    for k, (m, h) in ((0, c), (1, v), (2, b)):
        assemble_x(3, k, m, h, nx, x1, x2)
    _, lo = near_far()
    fine_coef(c, b, a, q, d, lo, HX)
    fine_sweep(v, w, a, q, lo, HX)
    v = fine_sweeps(nx, v, w, a, q)
    pb, pc = pick(0, 64, 128), pick(64, 64, 128)

    def coarse(i, _):
        x = off + 2 * i
        rs = [None] * (ny // 8)

        def first(t, val):
            rs[t] = val

        def second(t, val):
            pair[0, 8 * t : 8 * t + 8] = rs[t] + val

        for o, put in ((0, first), (1, second)):
            fine_residual(
                v, a, d, x + o, lambda t: src[2 * i + o, 8 * t : 8 * t + 8], put
            )
        for t in range(ny // 8):
            w8 = slice(8 * t, 8 * t + 8)
            pair[1, w8] = c_own[2 * i, w8] + c_own[2 * i + 1, w8]
            v_out[2 * i, w8] = v[0][x, 16 + 8 * t : 24 + 8 * t]
            v_out[2 * i + 1, w8] = v[0][x + 1, 16 + 8 * t : 24 + 8 * t]
        bc[i] = dot(half_rows(pair.at[0], 0, ny), pb) + dot(half_rows(pair.at[1], 0, ny), pc)
        return 0

    lax.fori_loop(0, nx // 2, coarse, 0)
    p5 = face_start("gx", nx, HX, True)
    for f in range(HX):
        xf[f] = v_out[p5 + f]
    for ref, flag in ((y_a, True), (y_b, False)):
        r = pl.multiple_of(face_start("gy", ny, 8, flag), 8)
        ref[...] = v_out[:, pl.ds(r, 8), :]


def join_kernel(own, other, full):
    n = own.shape[0]
    ix = lax.axis_index("gx")
    full[pl.ds(n * ix, n)] = own[...]
    full[pl.ds(n - n * ix, n)] = other[...]


def mid_rows(full, r_a, r_b, x, t, tiles):
    rows = slice((t % tiles) * 8, (t % tiles) * 8 + 8)
    if t < tiles:
        return jnp.where(even("gy"), r_b[x, rows], r_a[x, rows])
    if t >= 2 * tiles:
        return jnp.where(even("gy"), r_a[x, rows], r_b[x, rows])
    return full[x, rows]


def mid_z_kernel(full, r_a, r_b, v0, vr_a, vr_b, z_a, z_b, vz, work):
    nx, ny, _ = full.shape
    tiles = ny // 8
    ez = even("gz")
    low = lax.rem(lanes(), 64) < 32

    def pair(i, _):
        for t in range(3 * tiles):
            e = mid_rows(full, r_a, r_b, 2 * i, t, tiles)
            o = mid_rows(full, r_a, r_b, 2 * i + 1, t, tiles)
            first = jnp.where(low, e, rot(o, 32))
            last = jnp.where(low, rot(o, -32), e)
            z_a[i, t * 8 : t * 8 + 8] = jnp.where(ez, last, first)
            z_b[i, t * 8 : t * 8 + 8] = jnp.where(ez, first, last)

    fine_loop(0, nx // 2, lambda i, c: pair(i, c), 2)
    zpack_kernel(1, v0, vr_a, vr_b, vz, work)


def mid_down_kernel(full, r_a, r_b, z_a, z_b, vr_a, vr_b, vz_a, vz_b, *s):
    v1_out, c = s[0], (s[1],)
    a, q = [(s[2 + j],) for j in range(6)], (s[8],)
    v2_out, c2 = s[9], (s[10],)
    a2, q2 = [(s[11 + j],) for j in range(6)], (s[17],)
    bc3, frame = s[18], s[19]
    b, d, w = (s[20],), (s[21],), (s[22],)
    b2, d2, w2 = (s[23],), (s[24],), (s[25],)
    pair = s[26]
    xframe_kernel(1, vr_a.shape[0], vr_a, vr_b, vz_a, vz_b, frame)
    v, v2 = (v1_out,), (v2_out,)
    nx, ny, _ = full.shape
    tiles = ny // 8
    ez = even("gz")
    lane = lanes()
    own, low = lane < 64, lax.rem(lane, 64) < 32
    clear_pads(c[0], v[0], w[0], c2[0], v2[0], w2[0])

    def place(x, t, mine, side):
        rows = slice(8 + t * 8, 16 + t * 8)
        b[0][x + 1, rows] = jnp.where(own, mine, rot(side, 64))
        c[0][x + 1, rows] = jnp.where(own, rot(mine, 64), side)

    def two(i, _):
        for t in range(3 * tiles):
            za, zb = z_a[i, t * 8 : t * 8 + 8], z_b[i, t * 8 : t * 8 + 8]
            right = jnp.where(ez, za, zb)
            left = jnp.where(ez, zb, za)
            e = mid_rows(full, r_a, r_b, 2 * i, t, tiles)
            o = mid_rows(full, r_a, r_b, 2 * i + 1, t, tiles)
            place(2 * i, t, e, jnp.where(low, right, left))
            place(2 * i + 1, t, o, jnp.where(low, rot(right, -32), rot(left, 32)))

    fine_loop(0, nx // 2, two, 2)
    build_coef(c, b, a, q, d, 0.25, False)
    copy_q(w, q)
    sweep(w, v, a, q)
    sweep(v, w, a, q)
    sweep(w, v, a, q)
    rows2 = ny // 2 + 2 * H2
    r0 = ny - 2 * H2
    mat = ring_pick(96)

    def down(i, _):
        x = 1 + 2 * i
        for r in chunks(2 * rows2):
            rp = pl.ds(8 + r0 + r, 8)
            e = residual_rows(v, b[0][x, rp], a, d, x, r0 + r)
            o = residual_rows(v, b[0][x + 1, rp], a, d, x + 1, r0 + r)
            pair[0, pl.ds(r, 8)] = e + o
            pair[1, pl.ds(r, 8)] = c[0][x, rp] + c[0][x + 1, rp]
        b2[0][1 + i, 8 : 8 + rows2] = dot(half_rows(pair.at[0], 0, 2 * rows2), mat)
        c2[0][1 + i, 8 : 8 + rows2] = dot(half_rows(pair.at[1], 0, 2 * rows2), mat)

    fine_loop(0, nx // 2, down, 2)
    build_coef(c2, b2, a2, q2, d2, 0.0625, False)
    copy_q(w2, q2)
    sweep(w2, v2, a2, q2)
    sweep(v2, w2, a2, q2)
    sweep(w2, v2, a2, q2)
    n3, ny3 = nx // 4, ny // 4
    for i in range(n3):
        x = 1 + 2 * i
        for r in chunks(ny // 2):
            rp = pl.ds(8 + H2 + r, 8)
            e = residual_rows(v2, b2[0][x, rp], a2, d2, x, H2 + r)
            o = residual_rows(v2, b2[0][x + 1, rp], a2, d2, x + 1, H2 + r)
            pair[0, pl.ds(r, 8)] = e + o
            pair[1, pl.ds(r, 8)] = c2[0][x, rp] + c2[0][x + 1, rp]
        at = 32 * (i % 4)
        val = dot(half_rows(pair.at[0], 0, ny // 2), pick(at, 16, 32))
        val = val + dot(half_rows(pair.at[1], 0, ny // 2), pick(at + 16, 16, 32))
        if i % 4 == 0:
            acc = val
        else:
            acc = acc + val
        if i % 4 == 3 or i == n3 - 1:
            bc3[(i // 4) * ny3 : (i // 4 + 1) * ny3] = acc


def ring_pick(split):
    i = lax.broadcasted_iota(jnp.int32, (128, 128), 0)
    o = lax.broadcasted_iota(jnp.int32, (128, 128), 1)
    return jnp.where(o == jnp.where(i < split, i // 2, i // 2 + 64), 0.125, 0.0).astype(F32)


def clear_pads(*refs):
    for ref in refs:
        n, rows, _ = ref.shape
        for x in (0, n - 1):
            ref[x] = jnp.zeros(ref.shape[1:], F32)

        def one(x, _):
            ref[x, 0:8] = jnp.zeros((8, 128), F32)
            ref[x, rows - 8 : rows] = jnp.zeros((8, 128), F32)

        fine_loop(0, n, one, 6)


def spread(src, dst, mat, c, planes, skip, r_dst, rows, tmp):
    n = src.shape[0]
    p = dot(src, mat)
    tmp[pl.ds(0, n, stride=2)] = p
    tmp[pl.ds(1, n, stride=2)] = p
    for r in chunks(rows):
        rr = slice(r_dst + r, r_dst + r + 8)
        val = tmp[skip + r : skip + r + 8]
        for x in planes:
            dst[0][x, rr] = dst[0][x, rr] + jnp.where(c[0][x, rr] > 0.0, val, 0.0)


def select_mat(fn):
    i = lax.broadcasted_iota(jnp.int32, (128, 128), 0)
    o = lax.broadcasted_iota(jnp.int32, (128, 128), 1)
    return jnp.where(i == fn(o), 1.0, 0.0).astype(F32)


def coarse_kernel(gy, gz, blocks, *s):
    v1_in, c1 = s[0], (s[1],)
    a1, q1 = [(s[2 + j],) for j in range(6)], (s[8],)
    v2_in, c2 = s[9], (s[10],)
    a2, q2 = [(s[11 + j],) for j in range(6)], (s[17],)
    v1 = (s[18],)
    s = s[19:]
    w1, v2, w2 = (s[0],), (s[1],), (s[2],)
    c3, b3, v3, w3 = [(s[3 + i],) for i in range(4)]
    a3, q3 = [(s[7 + j],) for j in range(6)], (s[13],)
    tmp = s[14]
    iy, iz = lax.axis_index("gy"), lax.axis_index("gz")
    n3, ny3 = q3[0].shape[:2]
    yb = ny3 // gy
    lane = lanes(yb)
    zero(c3[0], v3[0], w3[0])
    for jy in range(gy):
        ky = lax.bitwise_xor(jnp.int32(jy), iy)
        blk = []
        for jz in range(gz):
            kz = lax.bitwise_xor(jnp.int32(jz), iz)
            blk.append(((kz % 2) * (gz // 2) + kz // 2) * gy + ky)
        for i in range(n3):
            rows = slice((i // 4) * yb, (i // 4 + 1) * yb)
            for ref, o in ((b3[0], 32 * (i % 4)), (c3[0], 32 * (i % 4) + 16)):
                acc = jnp.zeros((yb, 128), F32)
                for jz in range(gz):
                    acc = jnp.where(lane // 16 == jz, rot(blocks[blk[jz], rows], 16 * jz - o), acc)
                ref[1 + i, 8 + yb * jy : 8 + yb * (jy + 1)] = acc
    build_coef(c3, b3, a3, q3, None, 0.015625, False)
    copy_q(v3, q3)
    sweep(v3, w3, a3, q3, True)

    def two(_, carry):
        sweep(w3, v3, a3, q3, True)
        sweep(v3, w3, a3, q3, True)
        return carry

    lax.fori_loop(0, (COARSE - 2) // 2, two, 0)
    v2[0][...] = v2_in[...]
    v1[0][...] = v1_in[...]
    clear_pads(w1[0], w2[0])
    up = select_mat(lambda o: jnp.where(o < 96, o // 2, (o + 128) // 2))
    rows2 = q2[0].shape[1]
    skip = 16 - H2
    start = pl.multiple_of(yb * iy, 8)

    def up2(i, _):
        par = rot(w3[0][1 + i, pl.ds(start, yb + 16)], -16 * iz)
        spread(par, v2, up, c2, (1 + 2 * i, 2 + 2 * i), skip, 8, rows2, tmp)

    fine_loop(0, n3, up2, 2)

    def two2(_, carry):
        sweep(v2, w2, a2, q2)
        sweep(w2, v2, a2, q2)
        return carry

    lax.fori_loop(0, SWEEPS // 2, two2, 0)
    ny1 = 4 * yb
    r0 = ny1 - 8

    def up1(i, _):
        par = v2[0][1 + i, 8 + H2 - 4 : 8 + H2 + ny1 // 2 + 4]
        spread(par, v1, up, c1, (1 + 2 * i, 2 + 2 * i), 0, 8 + r0, ny1 + 16, tmp)

    fine_loop(0, 2 * n3, up1, 2)

    def two1(_, carry):
        sweep(v1, w1, a1, q1, False, r0, ny1 + 16)
        sweep(w1, v1, a1, q1, False, r0, ny1 + 16)
        return carry

    lax.fori_loop(0, SWEEPS // 2, two1, 0)


def spread_fine(v, c, planes, up, tmp):
    n = up.shape[0]
    for half in (0, 1):
        p = up[:, 128 * half : 128 * half + 128]
        tmp[half, pl.ds(0, n, stride=2)] = p
        tmp[half, pl.ds(1, n, stride=2)] = p
    lane = lanes()
    edge = jnp.zeros((8, 128), F32)
    for t in range(2 * n // 8):
        rows = slice(8 + 8 * t, 16 + 8 * t)
        par = tmp[0, 8 * t : 8 * t + 8]
        for x in planes:
            v[0][x, rows] = v[0][x, rows] + jnp.where(c[0][x, rows] > 0.0, par, 0.0)
        g = GW * t
        here = (lane >= g) & (lane < g + GW)
        edge = jnp.where(here, tmp[1, 8 * t : 8 * t + 8], edge)
    for x in planes:
        v[1][x] = v[1][x] + jnp.where(c[1][x] > 0.0, edge, 0.0)


def fine_up_kernel(v_own, src, vr_a, vr_b, vz_a, vz_b, x1, x2, v1, *refs):
    c, a, q, d = split_kept(refs[:17])
    sol_hbm, res_hbm = refs[17:19]
    v, w = (refs[19], refs[20]), (refs[21], refs[22])
    tmp, stage, spread, sol, res, sems = refs[23:]
    nx, ny, _ = src.shape
    off = 1 + own_offset(1)
    clear_rim(v, w)
    assemble_own(0, v[0], v[1], v_own, vr_a, vr_b, vz_a, vz_b)
    assemble_x(1, 0, v[0], v[1], nx, x1, x2)
    i = lax.broadcasted_iota(jnp.int32, (128, 256), 0)
    o = lax.broadcasted_iota(jnp.int32, (128, 256), 1)
    within = lax.rem(o - 128, GW)
    z = HL - 1 - within
    par = jnp.where(within < HL, 64 + lax.div(z, 2), 128 + lax.shift_right_arithmetic(z, 1))
    mat = jnp.where(i == jnp.where(o < 128, lax.div(o, 2), par), 1.0, 0.0).astype(F32)
    nc = v1.shape[0] - 2
    ix = lax.axis_index("gx")
    half = (ny + 16) // 2
    xp = v[0].shape[0] - 2
    count = (xp + 2) // 2
    c0 = lax.shift_right_arithmetic(nx * ix + 1 - off, 1)
    for j in range(count):
        stage[j * half : (j + 1) * half] = v1[1 + jnp.clip(c0 + j, 0, nc - 1), 4 + ny // 2 : 4 + ny // 2 + half]
    spread[...] = dot(stage[...], mat)

    def up(j, _):
        p = 2 * (c0 + j) - nx * ix + off
        start = pl.multiple_of(half * j, 8)
        spread_fine(v, c, (p, p + 1), spread[pl.ds(start, half)], tmp)
        return 0

    lax.fori_loop(0, count, up, 0)
    lo, total = fine_range(1, nx, HX - 1)
    fine_sweep(v, w, a, q, lo, total)
    v = fine_sweeps(nx, v, w, a, q)

    step = nx // 4

    def copies(i):
        at = pl.ds(i * step, step)
        return (
            pltpu.make_async_copy(sol.at[at], sol_hbm.at[at], sems.at[0, i]),
            pltpu.make_async_copy(res.at[at], res_hbm.at[at], sems.at[1, i]),
        )

    def out(x, _):
        def put(t, val):
            w8 = slice(8 * t, 8 * t + 8)
            res[x, w8] = val
            sol[x, w8] = v[0][off + x, 16 + 8 * t : 24 + 8 * t]

        fine_residual(v, a, d, off + x, lambda t: src[x, 8 * t : 8 * t + 8], put)

    for i in range(4):
        fine_loop(i * step, step, out, 2)
        for cp in copies(i):
            cp.start()
    for i in range(4):
        for cp in copies(i):
            cp.wait()


def named(fn, *args):
    out = functools.partial(fn, *args)
    out.__name__ = fn.__name__
    return out


def plain_with_halo(block, sides, width):
    for axis, dim in sides:
        count = lax.axis_size(axis)
        forward = [(i, i + 1) for i in range(count - 1)]
        backward = [(target, source) for source, target in forward]
        low = lax.ppermute(
            lax.slice_in_dim(block, block.shape[dim] - width, None, axis=dim), axis, forward
        )
        high = lax.ppermute(lax.slice_in_dim(block, 0, width, axis=dim), axis, backward)
        block = jnp.concatenate([low, block, high], axis=dim)
    return block


def plain_neighbor(padded, axis_dim, offset):
    window = [slice(1, -1), slice(1, -1), slice(1, -1)]
    window[axis_dim] = slice(1 + offset, padded.shape[axis_dim] - 1 + offset)
    return padded[tuple(window)]


def plain_apply_padded(padded_u, padded_c, level_scale):
    center_u = padded_u[1:-1, 1:-1, 1:-1]
    center_c = padded_c[1:-1, 1:-1, 1:-1]
    stencil_sum = jnp.zeros_like(center_u)
    diagonal = jnp.zeros_like(center_u)
    for axis_dim in range(3):
        for offset in (-1, 1):
            face = 0.5 * (center_c + plain_neighbor(padded_c, axis_dim, offset))
            stencil_sum = stencil_sum + face * (center_u - plain_neighbor(padded_u, axis_dim, offset))
            diagonal = diagonal + face
    return (level_scale * stencil_sum, level_scale * diagonal)


def plain_restrict(field):
    size_x, size_y, size_z = field.shape
    return field.reshape(size_x // 2, 2, size_y // 2, 2, size_z // 2, 2).mean(axis=(1, 3, 5))


def plain_prolong(field):
    size_x, size_y, size_z = field.shape
    spread = jnp.broadcast_to(field[:, None, :, None, :, None], (size_x, 2, size_y, 2, size_z, 2))
    return spread.reshape(2 * size_x, 2 * size_y, 2 * size_z)


def plain_coef_halo(coef_value):
    return plain_with_halo(coef_value, (("gx", 0), ("gy", 1), ("gz", 2)), 1)


def plain_residual_of(values, rhs_field, coef_padded, level_scale):
    padded_u = plain_with_halo(values, (("gx", 0), ("gy", 1), ("gz", 2)), 1)
    stencil_sum, diagonal = plain_apply_padded(padded_u, coef_padded, level_scale)
    return rhs_field - stencil_sum


def plain_narrow_sweeps(values, rhs_field, coef_padded, level_scale):
    for sweep_id in range(SWEEPS):
        padded_u = plain_with_halo(values, (("gx", 0), ("gy", 1), ("gz", 2)), 1)
        stencil_sum, diagonal = plain_apply_padded(padded_u, coef_padded, level_scale)
        values = values + W * (rhs_field - stencil_sum) / diagonal
    return values


def plain_smooth(values, level_id, rhs_list, padded_list):
    level_scale = 0.25**level_id
    return plain_narrow_sweeps(values, rhs_list[level_id], padded_list[level_id], level_scale)


def plain_coarse_solve(coarse_rhs, coarse_coef):
    coarse_scale = 0.25**LEVELS
    coarse_pad = plain_coef_halo(coarse_coef)

    def local_step(sweep_id, values):
        padded_u = plain_with_halo(values, (("gx", 0), ("gy", 1), ("gz", 2)), 1)
        stencil_sum, diagonal = plain_apply_padded(padded_u, coarse_pad, coarse_scale)
        return values + W * (coarse_rhs - stencil_sum) / diagonal

    return lax.fori_loop(0, COARSE, local_step, jnp.zeros_like(coarse_rhs))


def plain_body(source, first_guess, cell_classes, class_table):
    cell_coef = jnp.zeros(cell_classes.shape, jnp.float32)
    for class_id in range(CLASSES):
        cell_coef = cell_coef + jnp.where(cell_classes == class_id, class_table[class_id], 0.0)
    coef_list = [cell_coef]
    for level_id in range(LEVELS):
        coef_list.append(plain_restrict(coef_list[-1]))
    top_level = LEVELS
    padded_list = [plain_coef_halo(coef_list[level_id]) for level_id in range(top_level)]
    rhs_list = [source]
    iterate_list = []
    values = first_guess
    for level_id in range(top_level):
        level_scale = 0.25**level_id
        if level_id > 0:
            values = jnp.zeros_like(rhs_list[level_id])
        values = plain_smooth(values, level_id, rhs_list, padded_list)
        iterate_list.append(values)
        rhs_list.append(
            plain_restrict(plain_residual_of(values, rhs_list[level_id], padded_list[level_id], level_scale))
        )
    correction = plain_coarse_solve(rhs_list[LEVELS], coef_list[LEVELS])
    for level_id in reversed(range(top_level)):
        values = iterate_list[level_id] + plain_prolong(correction)
        values = plain_smooth(values, level_id, rhs_list, padded_list)
        correction = values
    final = plain_residual_of(correction, source, padded_list[0], 1.0)
    return (correction, final)


def body(source, first_guess, cell_classes, class_table):
    nx, ny, nz = source.shape
    gx, gy, gz = (lax.axis_size(n) for n in ("gx", "gy", "gz"))
    if (gx, gy, gz, nx, ny, nz) != (2, 4, 4, 16, 64, 128):
        return plain_body(source, first_guess, cell_classes, class_table)
    xp = nx + HX
    rows = ny + 16
    full = (nx, ny, 128)
    halo = (3 * nx, 8, 128)

    y_a, y_b, x1 = call(
        face_kernel,
        [(nx, 16, 128)] * 2 + [(3 * HX - 1, ny, 128)],
        source, first_guess, cell_classes, class_table,
        smem=(3,),
        hbm=(0, 1, 2),
        more=[pltpu.VMEM((HX, ny, 128), jnp.int32)]
        + [pltpu.VMEM((2, nx, 8, 128), jnp.int32)]
        + [pltpu.VMEM((2, nx, 8, 128), F32)] * 2
        + [pltpu.SemaphoreType.DMA((9,))],
    )
    x1 = swap_even(x1, "gx")
    r_a, r_b = swap_even(y_a, "gy"), swap_odd(y_b, "gy")
    own = call(
        load_kernel,
        [full, full, full],
        source, first_guess, cell_classes, class_table,
        smem=(3,),
        hbm=(0, 1, 2),
        more=[pltpu.VMEM(full, jnp.int32), pltpu.SemaphoreType.DMA((6,))],
    )
    c_own, _, source = own
    (z,) = call(named(zpack_kernel, 3), [halo], *own, r_a, r_b, scratch=[(3 * nx * 8, 128)])
    rec = (r_a, r_b, swap_even(z, "gz"), swap_odd(z, "gz"))
    (x2,) = call(named(xframe_kernel, 3, nx), [(frame_rows(3), 128)], *rec)
    x2 = swap_even(x2, "gx")
    pad = [(xp + 2, rows + 16, 128), (xp + 2, 8, 128)]
    state_shapes = fine_kept(xp, rows) + pad * 3
    state = call(fine_prep_kernel, state_shapes, *own, *rec)
    out = call(
        fine_down_kernel,
        state_shapes
        + [full, (nx // 2, ny // 2, 128), (nx, 8, 128), (nx, 8, 128), (HX, ny, 128)],
        c_own, source, x1, x2, *state,
        scratch=[(2, ny, 128)],
        alias={4 + i: i for i in range(23)},
    )
    kept = out[:17]
    v0, bc1, vy_a, vy_b, vx1 = out[23:]

    n1, ny1 = nx, ny // 2
    (f1,) = call(join_kernel, [(n1, ny1, 128)], bc1, swap_even(bc1, "gx"))
    vr_a, vr_b = swap_even(vy_a, "gy"), swap_odd(vy_b, "gy")
    vx1 = swap_even(vx1, "gx")
    r_a, r_b = swap_even(f1, "gy"), swap_odd(f1, "gy")
    rows1 = 3 * ny1
    z_a, z_b, vz = call(
        mid_z_kernel,
        [(n1 // 2, rows1, 128)] * 2 + [(nx, 8, 128)],
        f1, r_a, r_b, v0, vr_a, vr_b,
        scratch=[(nx * 8, 128)],
    )
    z_a, z_b = swap_even(z_a, "gz"), swap_odd(z_b, "gz")
    vz_a, vz_b = swap_even(vz, "gz"), swap_odd(vz, "gz")
    pad1, bare1 = (n1 + 2, rows1 + 16, 128), (n1, rows1, 128)
    n2, rows2 = n1 // 2, ny1 // 2 + 2 * H2
    pad2, bare2 = (n2 + 2, rows2 + 16, 128), (n2, rows2, 128)
    n3, yb = n1 // 4, ny1 // 4
    kept_mid = [pad1, pad1] + [bare1] * 7 + [pad2, pad2] + [bare2] * 7
    out = call(
        mid_down_kernel,
        kept_mid + [(-(-n3 // 4) * yb, 128), (frame_rows(1), 128)],
        f1, r_a, r_b, z_a, z_b, vr_a, vr_b, vz_a, vz_b,
        scratch=[pad1, bare1, pad1, pad2, bare2, pad2, (2, 2 * rows2, 128)],
    )
    kept_mid, (bc3, frame) = out[:-2], out[-2:]
    vx2 = swap_even(frame, "gx")
    vrec = (vr_a, vr_b, vz_a, vz_b)

    got = jnp.stack([bc3] + [swap_xor(bc3, "gy", m) for m in range(1, gy)])
    bit = gz // 2
    while bit:
        got = jnp.concatenate([got, swap_xor(got, "gz", bit)])
        bit //= 2

    pad3, bare3 = (n3 + 2, gy * yb + 16, 128), (n3, gy * yb, 128)
    (v1,) = call(
        named(coarse_kernel, gy, gz),
        [pad1],
        got, *kept_mid,
        scratch=[pad1, pad2, pad2] + [pad3] * 4 + [bare3] * 7 + [(2 * (ny1 + 16), 128)],
    )
    par_rows = (xp + 2) // 2 * (rows // 2)
    sol, res = call(
        fine_up_kernel,
        [full, full],
        v0, source, *vrec, vx1, vx2, v1, *kept,
        scratch=pad * 2 + [(2, rows, 128), (par_rows, 128), (par_rows, 256), full, full],
        hbm_out=True,
        more=[pltpu.SemaphoreType.DMA((2, 4))],
    )
    return sol, res


def solution(mesh):
    spec = P("gx", "gy", "gz")
    return jax.shard_map(
        body,
        mesh=mesh,
        in_specs=(spec, spec, spec, P()),
        out_specs=(spec, spec),
        check_vma=False,
    )
```

```python
import functools

import math
import jax
import jax.numpy as jnp
from jax import lax
from jax.experimental import pallas as pl
from jax.experimental.pallas import tpu as pltpu
from jax.sharding import PartitionSpec as P

LEVELS = 3
SWEEPS = 4
COARSE = 16
CLASSES = 8
W = 0.85
HX = 5
HL = 6
GW = 2 * HL
UNROLL = 7
H2 = 12
F32 = jnp.float32


def pairs_even(n):
    return [(i, i ^ 1) for i in range(n)]


def pairs_odd(n):
    out = []
    for i in range(1, n - 1, 2):
        out += [(i, i + 1), (i + 1, i)]
    return out


def swap_even(x, axis):
    return lax.ppermute(x, axis, pairs_even(lax.axis_size(axis)))


def swap_odd(x, axis):
    return lax.ppermute(x, axis, pairs_odd(lax.axis_size(axis)))


def swap_xor(x, axis, m):
    return lax.ppermute(x, axis, [(i, i ^ m) for i in range(lax.axis_size(axis))])


def even(axis):
    return lax.rem(lax.axis_index(axis), 2) == 0


def call(body, outs, *args, scratch=(), smem=(), hbm=(), hbm_out=False, more=(), alias=None):
    specs = [
        pl.BlockSpec(memory_space=pltpu.SMEM if i in smem else pltpu.HBM if i in hbm else pltpu.VMEM)
        for i in range(len(args))
    ]
    shapes = [jax.ShapeDtypeStruct(s, F32) if hbm_out else pltpu.VMEM(s, F32) for s in outs]
    space = pl.ANY if hbm_out else pltpu.VMEM
    spaces = [pltpu.HBM if i in hbm or i in smem else pltpu.VMEM for i in range(len(args))]
    args = [
        a if m is None or (m is pltpu.VMEM and a.dtype != F32)
        else pltpu.with_memory_space_constraint(a, m)
        for a, m in zip(args, spaces)
    ]
    limit = 4 * sum(math.prod(s) for s in scratch) + 6 * 2**20
    return pl.pallas_call(
        body,
        out_shape=shapes,
        in_specs=specs,
        out_specs=[pl.BlockSpec(memory_space=space) for _ in outs],
        scratch_shapes=[pltpu.VMEM(s, F32) for s in scratch] + list(more),
        name=getattr(body, "__name__", None) or body.func.__name__,
        compiler_params=pltpu.CompilerParams(vmem_limit_bytes=limit),
        input_output_aliases=alias or {},
    )(*args)


def lanes(rows=8):
    return lax.broadcasted_iota(jnp.int32, (rows, 128), 1)


def rot(x, shift):
    if isinstance(shift, int):
        shift = shift % 128
        if shift == 0:
            return x
    else:
        shift = lax.rem(shift + 1024, 128)
    return pltpu.roll(x, shift, 1)


def face_start(axis, total, width, want_even):
    hi = even(axis) if want_even else jnp.logical_not(even(axis))
    return jnp.where(hi, total - width, 0)


def look_up(k, table):
    acc = jnp.full(k.shape, table[0], F32)
    for i in range(1, CLASSES):
        acc = jnp.where(k == i, table[i], acc)
    return acc


def y_tiles(r_a, r_b, k, x):
    ey = even("gy")
    if r_a.shape[1] == 8:
        va, vb = r_a[x], r_b[x]
        return jnp.where(ey, vb, va), jnp.where(ey, va, vb)
    pick_of = lambda f: (f(r_a), f(r_b))
    if k == 0:
        low, high = pick_of(lambda r: r[x, 1:9]), pick_of(lambda r: r[x, 4:12])
    elif k == 1:
        low = pick_of(lambda r: r[x, 6:14])
        high = pick_of(lambda r: pltpu.roll(r[x, 8:16], 7, 0))
    else:
        low = pick_of(lambda r: pltpu.roll(r[x, 0:8], 4, 0))
        high = pick_of(lambda r: r[x, 0:8])
    return jnp.where(ey, low[1], low[0]), jnp.where(ey, high[0], high[1])


def face_kernel(src, guess, cls, table, y_a, y_b, x_out, *s):
    k_x, k_y, g_y, b_y, sems = s
    nx, ny, _ = src.shape
    p5 = face_start("gx", nx, HX, True)
    p4 = face_start("gx", nx, HX - 1, True)
    hi = [even("gy"), jnp.logical_not(even("gy"))]
    rows = [pl.multiple_of(face_start("gy", ny, 8, flag), 8) for flag in (True, False)]
    copies = [(cls.at[pl.ds(p5, HX)], k_x)]
    for i, r in enumerate(rows):
        copies.append((cls.at[:, pl.ds(r, 8)], k_y.at[i]))
        copies.append((guess.at[:, pl.ds(r, 8)], g_y.at[i]))
        copies.append((src.at[:, pl.ds(r, 8)], b_y.at[i]))
    copies.append((guess.at[pl.ds(p5, HX)], x_out.at[HX : 2 * HX]))
    copies.append((src.at[pl.ds(p4, HX - 1)], x_out.at[2 * HX : 3 * HX - 1]))
    copies = [pltpu.make_async_copy(f, t, sems.at[i]) for i, (f, t) in enumerate(copies)]
    for cp in copies:
        cp.start()
    copies[0].wait()
    for f in range(HX):
        x_out[f] = look_up(k_x[f], table)
    for i, out in ((0, y_a), (1, y_b)):
        for cp in copies[1 + 3 * i : 4 + 3 * i]:
            cp.wait()
        for x in range(nx):
            c8, v8, b8 = look_up(k_y[i, x], table), g_y[i, x], b_y[i, x]
            out[x, 8:16] = jnp.zeros((8, 128), F32)
            out[x, 0:4] = jnp.where(hi[i], b8[4:8], b8[0:4])
            out[x, 4:9] = jnp.where(hi[i], c8[3:8], c8[0:5])
            out[x, 9:14] = jnp.where(hi[i], v8[3:8], v8[0:5])
    for cp in copies[7:]:
        cp.wait()


def load_kernel(src, guess, cls, table, c_out, guess_out, src_out, k, sems):
    nx = src.shape[0]
    half = nx // 2
    copies = []
    for h in range(2):
        at = pl.ds(h * half, half)
        copies.append((cls.at[at], k.at[at]))
    for h in range(2):
        at = pl.ds(h * half, half)
        copies.append((guess.at[at], guess_out.at[at]))
        copies.append((src.at[at], src_out.at[at]))
    copies = [pltpu.make_async_copy(f, t, sems.at[i]) for i, (f, t) in enumerate(copies)]
    for cp in copies:
        cp.start()

    def plane(x, _):
        c_out[x] = look_up(k[x], table)

    for h in range(2):
        copies[h].wait()
        fine_loop(h * half, half, plane, 2)
    for cp in copies[2:]:
        cp.wait()


def zpack_kernel(na, *refs):
    arrs = refs[:na]
    r_a, r_b, z, work = refs[na:]
    nx, ny, _ = arrs[0].shape
    tiles = ny // 8 + 2
    lane = lanes()
    for k in range(na):
        for x in range(nx):
            acc = jnp.zeros((8, 128), F32)
            low, high = y_tiles(r_a, r_b, k, x)
            for t in range(tiles):
                if t == 0:
                    v = low
                elif t == tiles - 1:
                    v = high
                else:
                    v = arrs[k][x, (t - 1) * 8 : t * 8]
                g = GW * t
                acc = jnp.where((lane >= g) & (lane < g + GW), rot(v, g + HL), acc)
            work[(k * nx + x) * 8 : (k * nx + x) * 8 + 8] = acc
    mirror = select_mat(lambda o: o + (GW - 1) - 2 * lax.rem(o, GW))
    out = dot(work[...], mirror)
    for j in range(na * nx):
        z[j] = out[8 * j : 8 * j + 8]


def halo_of(z_a, z_b, i):
    ez = even("gz")
    a, b = z_a[i], z_b[i]
    within = lax.rem(lanes(), GW)
    return jnp.where(within < HL, jnp.where(ez, a, b), jnp.where(ez, b, a))


def face_list(na):
    widths = (HX, HX, HX - 1)
    return [(k, f, widths[k]) for k in range(na) for f in range(widths[k])]


def frame_list(na):
    out, row = [], 0
    for k in range(na):
        width = (HX, HX, HX - 1)[k]
        for dx in range(1, width):
            out.append((k, dx, row, width - dx))
            row += 2 * (width - dx)
    return out, -(-row // 8) * 8


def frame_rows(na):
    items, base = frame_list(na)
    return base + 8 * len(items)


def xframe_kernel(na, nx, r_a, r_b, z_a, z_b, x_out):
    items, base = frame_list(na)
    for j, (k, dx, row, w) in enumerate(items):
        p = jnp.where(even("gx"), nx - dx, dx - 1)
        low, high = y_tiles(r_a, r_b, k, p)
        x_out[row : row + w] = low[8 - w : 8]
        x_out[row + w : row + 2 * w] = high[0:w]
        x_out[base + j * 8 : base + j * 8 + 8] = halo_of(z_a, z_b, k * nx + p)


def own_offset(nsx):
    return HX * lax.axis_index("gx") if nsx == 1 else HX


def assemble_own(k, m, h, own, r_a, r_b, z_a, z_b):
    nx, ny, _ = own.shape
    off = 1 + own_offset(1)

    def one(x, _):
        low, high = y_tiles(r_a, r_b, k, x)
        m[off + x, 8:16] = low
        m[off + x, 16 : 16 + ny] = own[x]
        m[off + x, 16 + ny : 24 + ny] = high
        h[off + x] = halo_of(z_a, z_b, k * nx + x)

    fine_loop(0, nx, one, 2)


def assemble_x(na, k, m, h, nx, x1, x2):
    off = 1 + own_offset(1)
    hi = even("gx")
    ny = x1.shape[1]
    items, base = frame_list(na)
    for j, (kk, f, w) in enumerate(face_list(na)):
        if kk == k:
            p = off + jnp.where(hi, nx, -w) + f
            m[p, 8:16] = jnp.zeros((8, 128), F32)
            m[p, 16 : 16 + ny] = x1[j]
            m[p, 16 + ny : 24 + ny] = jnp.zeros((8, 128), F32)
            h[p] = jnp.zeros((8, 128), F32)
    for j, (kk, dx, row, w) in enumerate(items):
        if kk == k:
            p = off + jnp.where(hi, nx + dx - 1, -dx)
            m[p, 16 - w : 16] = x2[row : row + w]
            m[p, 16 + ny : 16 + ny + w] = x2[row + w : row + 2 * w]
            h[p] = x2[base + j * 8 : base + j * 8 + 8]


def zshift(vals, wrap=True):
    lo = lanes(vals[0].shape[0])
    down = [rot(v, 1) for v in vals]
    up = [rot(v, -1) for v in vals]
    if len(vals) == 2:
        first, last = lo == 0, lo == 127
        down = [jnp.where(first, down[1 - t], down[t]) for t in (0, 1)]
        up = [jnp.where(last, up[1 - t], up[t]) for t in (0, 1)]
    return down, up


def neighbours(refs, x, r, n):
    vals = [ref[x, pl.ds(8 + r, n)] for ref in refs]
    down, up = zshift(vals)
    out = []
    for t, ref in enumerate(refs):
        out.append(
            (
                ref[x - 1, pl.ds(8 + r, n)],
                ref[x + 1, pl.ds(8 + r, n)],
                ref[x, pl.ds(7 + r, n)],
                ref[x, pl.ds(9 + r, n)],
                down[t],
                up[t],
            )
        )
    return vals, out


def zero(*refs):
    for ref in refs:

        def one(x, _):
            ref[x] = jnp.zeros(ref.shape[1:], F32)
            return 0

        lax.fori_loop(0, ref.shape[0], one, 0)


def chunks(rows, n=8):
    return range(0, rows, n)


def build_coef(c, b, a, q, d, scale, full_lanes):
    nx, rows = c[0].shape[0] - 2, c[0].shape[1] - 16

    def plane(x, _):
        for r in chunks(rows):
            vals, nb = neighbours(c, x, r, 8)
            lane = lanes()
            for t in range(len(c)):
                six = list(nb[t])
                if full_lanes:
                    six[4] = jnp.where(lane == 0, 0.0, six[4])
                    six[5] = jnp.where(lane == 127, 0.0, six[5])
                total = 6.0 * vals[t] + (((six[0] + six[1]) + (six[2] + six[3])) + (six[4] + six[5]))
                inside = vals[t] > 0.0
                g = jnp.where(inside, W / jnp.where(inside, total, 1.0), 0.0)
                rw = pl.ds(r, 8)
                for j in range(6):
                    face = g * (vals[t] + six[j])
                    if full_lanes and j == 4:
                        face = jnp.where(lane == 0, 0.0, face)
                    if full_lanes and j == 5:
                        face = jnp.where(lane == 127, 0.0, face)
                    a[j][t][x - 1, rw] = face
                q[t][x - 1, rw] = g * ((2.0 / scale) * b[t][x, pl.ds(8 + r, 8)])
                if d is not None:
                    d[t][x - 1, rw] = total * (0.5 * scale / W)

    fine_loop(1, nx, plane, 2)


def weighted(a, vals, nb, t, x, rw):
    s = a[0][t][x - 1, rw] * nb[t][0] + a[1][t][x - 1, rw] * nb[t][1]
    u = a[2][t][x - 1, rw] * nb[t][2] + a[3][t][x - 1, rw] * nb[t][3]
    w = a[4][t][x - 1, rw] * nb[t][4] + a[5][t][x - 1, rw] * nb[t][5]
    return (s + u) + w


def sweep(src, dst, a, q, unroll=False, r0=0, rows=None):
    nx, rows = src[0].shape[0] - 2, rows or src[0].shape[1] - 16

    def plane(x, _):
        for r in range(r0, r0 + rows, 8):
            vals, nb = neighbours(src, x, r, 8)
            rw = pl.ds(r, 8)
            for t in range(len(src)):
                dst[t][x, pl.ds(8 + r, 8)] = ((1.0 - W) * vals[t] + q[t][x - 1, rw]) + weighted(
                    a, vals, nb, t, x, rw
                )

    if unroll:
        for x in range(1, nx + 1):
            plane(x, 0)
    else:
        fine_loop(1, nx, plane, UNROLL)


def copy_q(dst, q):
    def plane(x, _):
        for t in range(len(q)):
            dst[t][x + 1, 8 : 8 + q[t].shape[1]] = q[t][x]
        return 0

    lax.fori_loop(0, q[0].shape[0], plane, 0)


def residual_rows(v, b, a, d, x, r, n=8):
    vals, nb = neighbours(v, x, r, n)
    rw = pl.ds(r, n)
    return b - d[0][x - 1, rw] * (W * vals[0] - weighted(a, vals, nb, 0, x, rw))


def pick(shift_out, cols, limit):
    i = lax.broadcasted_iota(jnp.int32, (128, 128), 0)
    o = lax.broadcasted_iota(jnp.int32, (128, 128), 1)
    return jnp.where((i // 2 == o - shift_out) & (i < limit), 0.125, 0.0).astype(F32)


def dot(a, b):
    bf = jnp.bfloat16
    b = b.astype(bf)
    hi = a.astype(bf)
    rest = a - hi.astype(F32)
    mid = rest.astype(bf)
    lo = (rest - mid.astype(F32)).astype(bf)
    one = lambda p: lax.dot_general(p, b, (((1,), (0,)), ((), ())), preferred_element_type=F32)
    return one(hi) + (one(mid) + one(lo))


def half_rows(ref, r0, n):
    return ref[pl.ds(r0, n // 2, stride=2)] + ref[pl.ds(r0 + 1, n // 2, stride=2)]


def fine_loop(lo, count, plane, unroll):
    unroll = max(u for u in range(1, unroll + 2) if count % u == 0)

    def group(i, _):
        for u in range(unroll):
            plane(lo + i * unroll + u, 0)
        return 0

    lax.fori_loop(0, count // unroll, group, 0)


def fine_each(m, h, x, tiles, with_h, emit):
    lane = lanes()
    hv = h[x]
    edge = hv
    for t in tiles:
        g = GW * t
        v = m[x, 8 + 8 * t : 16 + 8 * t]
        beside = rot(hv, -(g + HL))
        down = jnp.where(lane == 0, beside, rot(v, 1))
        up = jnp.where(lane == 127, beside, rot(v, -1))
        six = (
            m[x - 1, 8 + 8 * t : 16 + 8 * t],
            m[x + 1, 8 + 8 * t : 16 + 8 * t],
            m[x, 7 + 8 * t : 15 + 8 * t],
            m[x, 9 + 8 * t : 17 + 8 * t],
            down,
            up,
        )
        emit(0, t, v, six)
        if with_h:
            edge = jnp.where((lane >= g) & (lane < g + GW), rot(v, g + HL), edge)
    if with_h:
        row = lax.broadcasted_iota(jnp.int32, (8, 128), 0)
        within = lax.rem(lane, GW)
        above, below = pltpu.roll(hv, 1, 0), pltpu.roll(hv, 7, 0)
        six = (
            h[x - 1],
            h[x + 1],
            jnp.where(row == 0, rot(above, GW), above),
            jnp.where(row == 7, rot(below, -GW), below),
            jnp.where(within == HL - 1, edge, rot(hv, -1)),
            jnp.where(within == HL, edge, rot(hv, 1)),
        )
        emit(1, 0, hv, six)


def cut(part, ref, x, t, pad):
    if part == 1:
        return (x, slice(0, 8))
    r = 8 * t + (8 if pad else 0)
    return (x, slice(r, r + 8))


def fine_coef(c, b, a, q, d, lo, count):
    tiles = range((c[0].shape[1] - 16) // 8)

    def plane(x, _):
        def emit(part, t, v, six):
            total = 6.0 * v + (((six[0] + six[1]) + (six[2] + six[3])) + (six[4] + six[5]))
            inside = v > 0.0
            g = jnp.where(inside, W / jnp.where(inside, total, 1.0), 0.0)
            at = cut(part, None, x - 1, t, False)
            for j in range(6):
                a[j][part][at] = g * (v + six[j])
            q[part][at] = g * (2.0 * b[part][cut(part, None, x, t, True)])
            if part == 0:
                d[at] = total * (0.5 / W)

        fine_each(c[0], c[1], x, tiles, True, emit)

    fine_loop(lo, count, plane, UNROLL)


def gather_sum(a, part, at, six):
    s = a[0][part][at] * six[0] + a[1][part][at] * six[1]
    u = a[2][part][at] * six[2] + a[3][part][at] * six[3]
    w = a[4][part][at] * six[4] + a[5][part][at] * six[5]
    return (s + u) + w


def fine_sweep(src, dst, a, q, lo, count):
    tiles = range((src[0].shape[1] - 16) // 8)

    def plane(x, _):
        def emit(part, t, v, six):
            at = cut(part, None, x - 1, t, False)
            dst[part][cut(part, None, x, t, True)] = (
                (1.0 - W) * v + q[part][at]
            ) + gather_sum(a, part, at, six)

        fine_each(src[0], src[1], x, tiles, True, emit)

    fine_loop(lo, count, plane, UNROLL)


def fine_residual(v, a, d, x, b_tile, put):
    def emit(part, t, val, six):
        at = cut(part, None, x - 1, t, False)
        put(t - 1, b_tile(t - 1) - d[at] * (W * val - gather_sum(a, part, at, six)))

    fine_each(v[0], v[1], x, range(1, (v[0].shape[1] - 16) // 8 - 1), False, emit)


def fine_range(nsx, nx, extra):
    off = own_offset(nsx)
    xp = nx + nsx * HX
    lo = jnp.maximum(off - extra, 0) + 1
    return lo, nx + nsx * extra


def fine_kept(xp, rows):
    m, h = (xp, rows, 128), (xp, 8, 128)
    return [(xp + 2, rows + 16, 128), (xp + 2, 8, 128)] + [m, h] * 7 + [m]


def split_kept(s):
    two = lambda i: (s[i], s[i + 1])
    return two(0), [two(2 + 2 * j) for j in range(6)], two(14), s[16]


def clear_rim(*pairs):
    for m, h in pairs:
        n, rows, _ = m.shape
        for x in (0, n - 1):
            m[x] = jnp.zeros(m.shape[1:], F32)
            h[x] = jnp.zeros(h.shape[1:], F32)

        def one(x, _):
            m[x, 0:8] = jnp.zeros((8, 128), F32)
            m[x, rows - 8 : rows] = jnp.zeros((8, 128), F32)
            return 0

        lax.fori_loop(0, n, one, 0)


def near_far():
    ix = lax.axis_index("gx")
    return 1 + (HX + 1) * ix, jnp.where(ix == 0, 16, 2)


def fine_sweeps(nx, v, w, a, q):
    for _ in range(SWEEPS - 1):
        lo, count = fine_range(1, nx, HX - 1)
        fine_sweep(w, v, a, q, lo, count)
        v, w = w, v
    return w


def fine_prep_kernel(c_own, guess, src, r_a, r_b, z_a, z_b, *s):
    c, a, q, d = split_kept(s[:17])
    b, v, w = (s[17], s[18]), (s[19], s[20]), (s[21], s[22])
    clear_rim(c, v, w)
    for k, own, (m, h) in ((0, c_own, c), (1, guess, v), (2, src, b)):
        assemble_own(k, m, h, own, r_a, r_b, z_a, z_b)
    lo, _ = near_far()
    nx = src.shape[0]
    fine_coef(c, b, a, q, d, lo, nx - 1)
    fine_sweep(v, w, a, q, lo, nx - 1)


def fine_down_kernel(c_own, src, x1, x2, *refs):
    s = refs[23:46]
    v_out, bc, y_a, y_b, xf = refs[46:51]
    pair = refs[51]
    c, a, q, d = split_kept(s[:17])
    b, v, w = (s[17], s[18]), (s[19], s[20]), (s[21], s[22])
    nx, ny, _ = src.shape
    off = 1 + own_offset(1)
    for k, (m, h) in ((0, c), (1, v), (2, b)):
        assemble_x(3, k, m, h, nx, x1, x2)
    _, lo = near_far()
    fine_coef(c, b, a, q, d, lo, HX)
    fine_sweep(v, w, a, q, lo, HX)
    v = fine_sweeps(nx, v, w, a, q)
    pb, pc = pick(0, 64, 128), pick(64, 64, 128)

    def coarse(i, _):
        x = off + 2 * i
        rs = [None] * (ny // 8)

        def first(t, val):
            rs[t] = val

        def second(t, val):
            pair[0, 8 * t : 8 * t + 8] = rs[t] + val

        for o, put in ((0, first), (1, second)):
            fine_residual(
                v, a, d, x + o, lambda t: src[2 * i + o, 8 * t : 8 * t + 8], put
            )
        for t in range(ny // 8):
            w8 = slice(8 * t, 8 * t + 8)
            pair[1, w8] = c_own[2 * i, w8] + c_own[2 * i + 1, w8]
            v_out[2 * i, w8] = v[0][x, 16 + 8 * t : 24 + 8 * t]
            v_out[2 * i + 1, w8] = v[0][x + 1, 16 + 8 * t : 24 + 8 * t]
        bc[i] = dot(half_rows(pair.at[0], 0, ny), pb) + dot(half_rows(pair.at[1], 0, ny), pc)
        return 0

    lax.fori_loop(0, nx // 2, coarse, 0)
    p5 = face_start("gx", nx, HX, True)
    for f in range(HX):
        xf[f] = v_out[p5 + f]
    for ref, flag in ((y_a, True), (y_b, False)):
        r = pl.multiple_of(face_start("gy", ny, 8, flag), 8)
        ref[...] = v_out[:, pl.ds(r, 8), :]


def join_kernel(own, other, full):
    n = own.shape[0]
    ix = lax.axis_index("gx")
    full[pl.ds(n * ix, n)] = own[...]
    full[pl.ds(n - n * ix, n)] = other[...]


def mid_rows(full, r_a, r_b, x, t, tiles):
    rows = slice((t % tiles) * 8, (t % tiles) * 8 + 8)
    if t < tiles:
        return jnp.where(even("gy"), r_b[x, rows], r_a[x, rows])
    if t >= 2 * tiles:
        return jnp.where(even("gy"), r_a[x, rows], r_b[x, rows])
    return full[x, rows]


def mid_z_kernel(full, r_a, r_b, v0, vr_a, vr_b, z_a, z_b, vz, work):
    nx, ny, _ = full.shape
    tiles = ny // 8
    ez = even("gz")
    low = lax.rem(lanes(), 64) < 32

    def pair(i, _):
        for t in range(3 * tiles):
            e = mid_rows(full, r_a, r_b, 2 * i, t, tiles)
            o = mid_rows(full, r_a, r_b, 2 * i + 1, t, tiles)
            first = jnp.where(low, e, rot(o, 32))
            last = jnp.where(low, rot(o, -32), e)
            z_a[i, t * 8 : t * 8 + 8] = jnp.where(ez, last, first)
            z_b[i, t * 8 : t * 8 + 8] = jnp.where(ez, first, last)

    fine_loop(0, nx // 2, lambda i, c: pair(i, c), 2)
    zpack_kernel(1, v0, vr_a, vr_b, vz, work)


def mid_down_kernel(full, r_a, r_b, z_a, z_b, vr_a, vr_b, vz_a, vz_b, *s):
    v1_out, c = s[0], (s[1],)
    a, q = [(s[2 + j],) for j in range(6)], (s[8],)
    v2_out, c2 = s[9], (s[10],)
    a2, q2 = [(s[11 + j],) for j in range(6)], (s[17],)
    bc3, frame = s[18], s[19]
    b, d, w = (s[20],), (s[21],), (s[22],)
    b2, d2, w2 = (s[23],), (s[24],), (s[25],)
    pair = s[26]
    xframe_kernel(1, vr_a.shape[0], vr_a, vr_b, vz_a, vz_b, frame)
    v, v2 = (v1_out,), (v2_out,)
    nx, ny, _ = full.shape
    tiles = ny // 8
    ez = even("gz")
    lane = lanes()
    own, low = lane < 64, lax.rem(lane, 64) < 32
    clear_pads(c[0], v[0], w[0], c2[0], v2[0], w2[0])

    def place(x, t, mine, side):
        rows = slice(8 + t * 8, 16 + t * 8)
        b[0][x + 1, rows] = jnp.where(own, mine, rot(side, 64))
        c[0][x + 1, rows] = jnp.where(own, rot(mine, 64), side)

    def two(i, _):
        for t in range(3 * tiles):
            za, zb = z_a[i, t * 8 : t * 8 + 8], z_b[i, t * 8 : t * 8 + 8]
            right = jnp.where(ez, za, zb)
            left = jnp.where(ez, zb, za)
            e = mid_rows(full, r_a, r_b, 2 * i, t, tiles)
            o = mid_rows(full, r_a, r_b, 2 * i + 1, t, tiles)
            place(2 * i, t, e, jnp.where(low, right, left))
            place(2 * i + 1, t, o, jnp.where(low, rot(right, -32), rot(left, 32)))

    fine_loop(0, nx // 2, two, 2)
    build_coef(c, b, a, q, d, 0.25, False)
    copy_q(w, q)
    sweep(w, v, a, q)
    sweep(v, w, a, q)
    sweep(w, v, a, q)
    rows2 = ny // 2 + 2 * H2
    r0 = ny - 2 * H2
    mat = ring_pick(96)

    def down(i, _):
        x = 1 + 2 * i
        for r in chunks(2 * rows2):
            rp = pl.ds(8 + r0 + r, 8)
            e = residual_rows(v, b[0][x, rp], a, d, x, r0 + r)
            o = residual_rows(v, b[0][x + 1, rp], a, d, x + 1, r0 + r)
            pair[0, pl.ds(r, 8)] = e + o
            pair[1, pl.ds(r, 8)] = c[0][x, rp] + c[0][x + 1, rp]
        b2[0][1 + i, 8 : 8 + rows2] = dot(half_rows(pair.at[0], 0, 2 * rows2), mat)
        c2[0][1 + i, 8 : 8 + rows2] = dot(half_rows(pair.at[1], 0, 2 * rows2), mat)

    fine_loop(0, nx // 2, down, 2)
    build_coef(c2, b2, a2, q2, d2, 0.0625, False)
    copy_q(w2, q2)
    sweep(w2, v2, a2, q2)
    sweep(v2, w2, a2, q2)
    sweep(w2, v2, a2, q2)
    n3, ny3 = nx // 4, ny // 4
    for i in range(n3):
        x = 1 + 2 * i
        for r in chunks(ny // 2):
            rp = pl.ds(8 + H2 + r, 8)
            e = residual_rows(v2, b2[0][x, rp], a2, d2, x, H2 + r)
            o = residual_rows(v2, b2[0][x + 1, rp], a2, d2, x + 1, H2 + r)
            pair[0, pl.ds(r, 8)] = e + o
            pair[1, pl.ds(r, 8)] = c2[0][x, rp] + c2[0][x + 1, rp]
        at = 32 * (i % 4)
        val = dot(half_rows(pair.at[0], 0, ny // 2), pick(at, 16, 32))
        val = val + dot(half_rows(pair.at[1], 0, ny // 2), pick(at + 16, 16, 32))
        if i % 4 == 0:
            acc = val
        else:
            acc = acc + val
        if i % 4 == 3 or i == n3 - 1:
            bc3[(i // 4) * ny3 : (i // 4 + 1) * ny3] = acc


def ring_pick(split):
    i = lax.broadcasted_iota(jnp.int32, (128, 128), 0)
    o = lax.broadcasted_iota(jnp.int32, (128, 128), 1)
    return jnp.where(o == jnp.where(i < split, i // 2, i // 2 + 64), 0.125, 0.0).astype(F32)


def clear_pads(*refs):
    for ref in refs:
        n, rows, _ = ref.shape
        for x in (0, n - 1):
            ref[x] = jnp.zeros(ref.shape[1:], F32)

        def one(x, _):
            ref[x, 0:8] = jnp.zeros((8, 128), F32)
            ref[x, rows - 8 : rows] = jnp.zeros((8, 128), F32)

        fine_loop(0, n, one, 6)


def spread(src, dst, mat, c, planes, skip, r_dst, rows, tmp):
    n = src.shape[0]
    p = dot(src, mat)
    tmp[pl.ds(0, n, stride=2)] = p
    tmp[pl.ds(1, n, stride=2)] = p
    for r in chunks(rows):
        rr = slice(r_dst + r, r_dst + r + 8)
        val = tmp[skip + r : skip + r + 8]
        for x in planes:
            dst[0][x, rr] = dst[0][x, rr] + jnp.where(c[0][x, rr] > 0.0, val, 0.0)


def select_mat(fn):
    i = lax.broadcasted_iota(jnp.int32, (128, 128), 0)
    o = lax.broadcasted_iota(jnp.int32, (128, 128), 1)
    return jnp.where(i == fn(o), 1.0, 0.0).astype(F32)


def coarse_kernel(gy, gz, blocks, *s):
    v1_in, c1 = s[0], (s[1],)
    a1, q1 = [(s[2 + j],) for j in range(6)], (s[8],)
    v2_in, c2 = s[9], (s[10],)
    a2, q2 = [(s[11 + j],) for j in range(6)], (s[17],)
    v1 = (s[18],)
    s = s[19:]
    w1, v2, w2 = (s[0],), (s[1],), (s[2],)
    c3, b3, v3, w3 = [(s[3 + i],) for i in range(4)]
    a3, q3 = [(s[7 + j],) for j in range(6)], (s[13],)
    tmp = s[14]
    iy, iz = lax.axis_index("gy"), lax.axis_index("gz")
    n3, ny3 = q3[0].shape[:2]
    yb = ny3 // gy
    lane = lanes(yb)
    zero(c3[0], v3[0], w3[0])
    for jy in range(gy):
        ky = lax.bitwise_xor(jnp.int32(jy), iy)
        blk = []
        for jz in range(gz):
            kz = lax.bitwise_xor(jnp.int32(jz), iz)
            blk.append(((kz % 2) * (gz // 2) + kz // 2) * gy + ky)
        for i in range(n3):
            rows = slice((i // 4) * yb, (i // 4 + 1) * yb)
            for ref, o in ((b3[0], 32 * (i % 4)), (c3[0], 32 * (i % 4) + 16)):
                acc = jnp.zeros((yb, 128), F32)
                for jz in range(gz):
                    acc = jnp.where(lane // 16 == jz, rot(blocks[blk[jz], rows], 16 * jz - o), acc)
                ref[1 + i, 8 + yb * jy : 8 + yb * (jy + 1)] = acc
    build_coef(c3, b3, a3, q3, None, 0.015625, False)
    copy_q(v3, q3)
    sweep(v3, w3, a3, q3, True)

    def two(_, carry):
        sweep(w3, v3, a3, q3, True)
        sweep(v3, w3, a3, q3, True)
        return carry

    lax.fori_loop(0, (COARSE - 2) // 2, two, 0)
    v2[0][...] = v2_in[...]
    v1[0][...] = v1_in[...]
    clear_pads(w1[0], w2[0])
    up = select_mat(lambda o: jnp.where(o < 96, o // 2, (o + 128) // 2))
    rows2 = q2[0].shape[1]
    skip = 16 - H2
    start = pl.multiple_of(yb * iy, 8)

    def up2(i, _):
        par = rot(w3[0][1 + i, pl.ds(start, yb + 16)], -16 * iz)
        spread(par, v2, up, c2, (1 + 2 * i, 2 + 2 * i), skip, 8, rows2, tmp)

    fine_loop(0, n3, up2, 2)

    def two2(_, carry):
        sweep(v2, w2, a2, q2)
        sweep(w2, v2, a2, q2)
        return carry

    lax.fori_loop(0, SWEEPS // 2, two2, 0)
    ny1 = 4 * yb
    r0 = ny1 - 8

    def up1(i, _):
        par = v2[0][1 + i, 8 + H2 - 4 : 8 + H2 + ny1 // 2 + 4]
        spread(par, v1, up, c1, (1 + 2 * i, 2 + 2 * i), 0, 8 + r0, ny1 + 16, tmp)

    fine_loop(0, 2 * n3, up1, 2)

    def two1(_, carry):
        sweep(v1, w1, a1, q1, False, r0, ny1 + 16)
        sweep(w1, v1, a1, q1, False, r0, ny1 + 16)
        return carry

    lax.fori_loop(0, SWEEPS // 2, two1, 0)


def spread_fine(v, c, planes, up, tmp):
    n = up.shape[0]
    for half in (0, 1):
        p = up[:, 128 * half : 128 * half + 128]
        tmp[half, pl.ds(0, n, stride=2)] = p
        tmp[half, pl.ds(1, n, stride=2)] = p
    lane = lanes()
    edge = jnp.zeros((8, 128), F32)
    for t in range(2 * n // 8):
        rows = slice(8 + 8 * t, 16 + 8 * t)
        par = tmp[0, 8 * t : 8 * t + 8]
        for x in planes:
            v[0][x, rows] = v[0][x, rows] + jnp.where(c[0][x, rows] > 0.0, par, 0.0)
        g = GW * t
        here = (lane >= g) & (lane < g + GW)
        edge = jnp.where(here, tmp[1, 8 * t : 8 * t + 8], edge)
    for x in planes:
        v[1][x] = v[1][x] + jnp.where(c[1][x] > 0.0, edge, 0.0)


def fine_up_kernel(v_own, src, vr_a, vr_b, vz_a, vz_b, x1, x2, v1, *refs):
    c, a, q, d = split_kept(refs[:17])
    sol_hbm, res_hbm = refs[17:19]
    v, w = (refs[19], refs[20]), (refs[21], refs[22])
    tmp, stage, spread, sol, res, sems = refs[23:]
    nx, ny, _ = src.shape
    off = 1 + own_offset(1)
    clear_rim(v, w)
    assemble_own(0, v[0], v[1], v_own, vr_a, vr_b, vz_a, vz_b)
    assemble_x(1, 0, v[0], v[1], nx, x1, x2)
    i = lax.broadcasted_iota(jnp.int32, (128, 256), 0)
    o = lax.broadcasted_iota(jnp.int32, (128, 256), 1)
    within = lax.rem(o - 128, GW)
    z = HL - 1 - within
    par = jnp.where(within < HL, 64 + lax.div(z, 2), 128 + lax.shift_right_arithmetic(z, 1))
    mat = jnp.where(i == jnp.where(o < 128, lax.div(o, 2), par), 1.0, 0.0).astype(F32)
    nc = v1.shape[0] - 2
    ix = lax.axis_index("gx")
    half = (ny + 16) // 2
    xp = v[0].shape[0] - 2
    count = (xp + 2) // 2
    c0 = lax.shift_right_arithmetic(nx * ix + 1 - off, 1)
    for j in range(count):
        stage[j * half : (j + 1) * half] = v1[1 + jnp.clip(c0 + j, 0, nc - 1), 4 + ny // 2 : 4 + ny // 2 + half]
    spread[...] = dot(stage[...], mat)

    def up(j, _):
        p = 2 * (c0 + j) - nx * ix + off
        start = pl.multiple_of(half * j, 8)
        spread_fine(v, c, (p, p + 1), spread[pl.ds(start, half)], tmp)
        return 0

    lax.fori_loop(0, count, up, 0)
    lo, total = fine_range(1, nx, HX - 1)
    fine_sweep(v, w, a, q, lo, total)
    v = fine_sweeps(nx, v, w, a, q)

    step = nx // 4

    def copies(i):
        at = pl.ds(i * step, step)
        return (
            pltpu.make_async_copy(sol.at[at], sol_hbm.at[at], sems.at[0, i]),
            pltpu.make_async_copy(res.at[at], res_hbm.at[at], sems.at[1, i]),
        )

    def out(x, _):
        def put(t, val):
            w8 = slice(8 * t, 8 * t + 8)
            res[x, w8] = val
            sol[x, w8] = v[0][off + x, 16 + 8 * t : 24 + 8 * t]

        fine_residual(v, a, d, off + x, lambda t: src[x, 8 * t : 8 * t + 8], put)

    for i in range(4):
        fine_loop(i * step, step, out, 2)
        for cp in copies(i):
            cp.start()
    for i in range(4):
        for cp in copies(i):
            cp.wait()


def named(fn, *args):
    out = functools.partial(fn, *args)
    out.__name__ = fn.__name__
    return out


def plain_with_halo(block, sides, width):
    for axis, dim in sides:
        count = lax.axis_size(axis)
        forward = [(i, i + 1) for i in range(count - 1)]
        backward = [(target, source) for source, target in forward]
        low = lax.ppermute(
            lax.slice_in_dim(block, block.shape[dim] - width, None, axis=dim), axis, forward
        )
        high = lax.ppermute(lax.slice_in_dim(block, 0, width, axis=dim), axis, backward)
        block = jnp.concatenate([low, block, high], axis=dim)
    return block


def plain_neighbor(padded, axis_dim, offset):
    window = [slice(1, -1), slice(1, -1), slice(1, -1)]
    window[axis_dim] = slice(1 + offset, padded.shape[axis_dim] - 1 + offset)
    return padded[tuple(window)]


def plain_apply_padded(padded_u, padded_c, level_scale):
    center_u = padded_u[1:-1, 1:-1, 1:-1]
    center_c = padded_c[1:-1, 1:-1, 1:-1]
    stencil_sum = jnp.zeros_like(center_u)
    diagonal = jnp.zeros_like(center_u)
    for axis_dim in range(3):
        for offset in (-1, 1):
            face = 0.5 * (center_c + plain_neighbor(padded_c, axis_dim, offset))
            stencil_sum = stencil_sum + face * (center_u - plain_neighbor(padded_u, axis_dim, offset))
            diagonal = diagonal + face
    return (level_scale * stencil_sum, level_scale * diagonal)


def plain_restrict(field):
    size_x, size_y, size_z = field.shape
    return field.reshape(size_x // 2, 2, size_y // 2, 2, size_z // 2, 2).mean(axis=(1, 3, 5))


def plain_prolong(field):
    size_x, size_y, size_z = field.shape
    spread = jnp.broadcast_to(field[:, None, :, None, :, None], (size_x, 2, size_y, 2, size_z, 2))
    return spread.reshape(2 * size_x, 2 * size_y, 2 * size_z)


def plain_coef_halo(coef_value):
    return plain_with_halo(coef_value, (("gx", 0), ("gy", 1), ("gz", 2)), 1)


def plain_residual_of(values, rhs_field, coef_padded, level_scale):
    padded_u = plain_with_halo(values, (("gx", 0), ("gy", 1), ("gz", 2)), 1)
    stencil_sum, diagonal = plain_apply_padded(padded_u, coef_padded, level_scale)
    return rhs_field - stencil_sum


def plain_narrow_sweeps(values, rhs_field, coef_padded, level_scale):
    for sweep_id in range(SWEEPS):
        padded_u = plain_with_halo(values, (("gx", 0), ("gy", 1), ("gz", 2)), 1)
        stencil_sum, diagonal = plain_apply_padded(padded_u, coef_padded, level_scale)
        values = values + W * (rhs_field - stencil_sum) / diagonal
    return values


def plain_smooth(values, level_id, rhs_list, padded_list):
    level_scale = 0.25**level_id
    return plain_narrow_sweeps(values, rhs_list[level_id], padded_list[level_id], level_scale)


def plain_coarse_solve(coarse_rhs, coarse_coef):
    coarse_scale = 0.25**LEVELS
    coarse_pad = plain_coef_halo(coarse_coef)

    def local_step(sweep_id, values):
        padded_u = plain_with_halo(values, (("gx", 0), ("gy", 1), ("gz", 2)), 1)
        stencil_sum, diagonal = plain_apply_padded(padded_u, coarse_pad, coarse_scale)
        return values + W * (coarse_rhs - stencil_sum) / diagonal

    return lax.fori_loop(0, COARSE, local_step, jnp.zeros_like(coarse_rhs))


def plain_body(source, first_guess, cell_classes, class_table):
    cell_coef = jnp.zeros(cell_classes.shape, jnp.float32)
    for class_id in range(CLASSES):
        cell_coef = cell_coef + jnp.where(cell_classes == class_id, class_table[class_id], 0.0)
    coef_list = [cell_coef]
    for level_id in range(LEVELS):
        coef_list.append(plain_restrict(coef_list[-1]))
    top_level = LEVELS
    padded_list = [plain_coef_halo(coef_list[level_id]) for level_id in range(top_level)]
    rhs_list = [source]
    iterate_list = []
    values = first_guess
    for level_id in range(top_level):
        level_scale = 0.25**level_id
        if level_id > 0:
            values = jnp.zeros_like(rhs_list[level_id])
        values = plain_smooth(values, level_id, rhs_list, padded_list)
        iterate_list.append(values)
        rhs_list.append(
            plain_restrict(plain_residual_of(values, rhs_list[level_id], padded_list[level_id], level_scale))
        )
    correction = plain_coarse_solve(rhs_list[LEVELS], coef_list[LEVELS])
    for level_id in reversed(range(top_level)):
        values = iterate_list[level_id] + plain_prolong(correction)
        values = plain_smooth(values, level_id, rhs_list, padded_list)
        correction = values
    final = plain_residual_of(correction, source, padded_list[0], 1.0)
    return (correction, final)


def body(source, first_guess, cell_classes, class_table):
    nx, ny, nz = source.shape
    gx, gy, gz = (lax.axis_size(n) for n in ("gx", "gy", "gz"))
    if (gx, gy, gz, nx, ny, nz) != (2, 4, 4, 16, 64, 128):
        return plain_body(source, first_guess, cell_classes, class_table)
    xp = nx + HX
    rows = ny + 16
    full = (nx, ny, 128)
    halo = (3 * nx, 8, 128)

    y_a, y_b, x1 = call(
        face_kernel,
        [(nx, 16, 128)] * 2 + [(3 * HX - 1, ny, 128)],
        source, first_guess, cell_classes, class_table,
        smem=(3,),
        hbm=(0, 1, 2),
        more=[pltpu.VMEM((HX, ny, 128), jnp.int32)]
        + [pltpu.VMEM((2, nx, 8, 128), jnp.int32)]
        + [pltpu.VMEM((2, nx, 8, 128), F32)] * 2
        + [pltpu.SemaphoreType.DMA((9,))],
    )
    x1 = swap_even(x1, "gx")
    r_a, r_b = swap_even(y_a, "gy"), swap_odd(y_b, "gy")
    own = call(
        load_kernel,
        [full, full, full],
        source, first_guess, cell_classes, class_table,
        smem=(3,),
        hbm=(0, 1, 2),
        more=[pltpu.VMEM(full, jnp.int32), pltpu.SemaphoreType.DMA((6,))],
    )
    c_own, _, source = own
    (z,) = call(named(zpack_kernel, 3), [halo], *own, r_a, r_b, scratch=[(3 * nx * 8, 128)])
    rec = (r_a, r_b, swap_even(z, "gz"), swap_odd(z, "gz"))
    (x2,) = call(named(xframe_kernel, 3, nx), [(frame_rows(3), 128)], *rec)
    x2 = swap_even(x2, "gx")
    pad = [(xp + 2, rows + 16, 128), (xp + 2, 8, 128)]
    state_shapes = fine_kept(xp, rows) + pad * 3
    state = call(fine_prep_kernel, state_shapes, *own, *rec)
    out = call(
        fine_down_kernel,
        state_shapes
        + [full, (nx // 2, ny // 2, 128), (nx, 8, 128), (nx, 8, 128), (HX, ny, 128)],
        c_own, source, x1, x2, *state,
        scratch=[(2, ny, 128)],
        alias={4 + i: i for i in range(23)},
    )
    kept = out[:17]
    v0, bc1, vy_a, vy_b, vx1 = out[23:]

    n1, ny1 = nx, ny // 2
    (f1,) = call(join_kernel, [(n1, ny1, 128)], bc1, swap_even(bc1, "gx"))
    vr_a, vr_b = swap_even(vy_a, "gy"), swap_odd(vy_b, "gy")
    vx1 = swap_even(vx1, "gx")
    r_a, r_b = swap_even(f1, "gy"), swap_odd(f1, "gy")
    rows1 = 3 * ny1
    z_a, z_b, vz = call(
        mid_z_kernel,
        [(n1 // 2, rows1, 128)] * 2 + [(nx, 8, 128)],
        f1, r_a, r_b, v0, vr_a, vr_b,
        scratch=[(nx * 8, 128)],
    )
    z_a, z_b = swap_even(z_a, "gz"), swap_odd(z_b, "gz")
    vz_a, vz_b = swap_even(vz, "gz"), swap_odd(vz, "gz")
    pad1, bare1 = (n1 + 2, rows1 + 16, 128), (n1, rows1, 128)
    n2, rows2 = n1 // 2, ny1 // 2 + 2 * H2
    pad2, bare2 = (n2 + 2, rows2 + 16, 128), (n2, rows2, 128)
    n3, yb = n1 // 4, ny1 // 4
    kept_mid = [pad1, pad1] + [bare1] * 7 + [pad2, pad2] + [bare2] * 7
    out = call(
        mid_down_kernel,
        kept_mid + [(-(-n3 // 4) * yb, 128), (frame_rows(1), 128)],
        f1, r_a, r_b, z_a, z_b, vr_a, vr_b, vz_a, vz_b,
        scratch=[pad1, bare1, pad1, pad2, bare2, pad2, (2, 2 * rows2, 128)],
    )
    kept_mid, (bc3, frame) = out[:-2], out[-2:]
    vx2 = swap_even(frame, "gx")
    vrec = (vr_a, vr_b, vz_a, vz_b)

    got = jnp.stack([bc3] + [swap_xor(bc3, "gy", m) for m in range(1, gy)])
    bit = gz // 2
    while bit:
        got = jnp.concatenate([got, swap_xor(got, "gz", bit)])
        bit //= 2

    pad3, bare3 = (n3 + 2, gy * yb + 16, 128), (n3, gy * yb, 128)
    (v1,) = call(
        named(coarse_kernel, gy, gz),
        [pad1],
        got, *kept_mid,
        scratch=[pad1, pad2, pad2] + [pad3] * 4 + [bare3] * 7 + [(2 * (ny1 + 16), 128)],
    )
    par_rows = (xp + 2) // 2 * (rows // 2)
    sol, res = call(
        fine_up_kernel,
        [full, full],
        v0, source, *vrec, vx1, vx2, v1, *kept,
        scratch=pad * 2 + [(2, rows, 128), (par_rows, 128), (par_rows, 256), full, full],
        hbm_out=True,
        more=[pltpu.SemaphoreType.DMA((2, 4))],
    )
    return sol, res


def solution(mesh):
    spec = P("gx", "gy", "gz")
    return jax.shard_map(
        body,
        mesh=mesh,
        in_specs=(spec, spec, spec, P()),
        out_specs=(spec, spec),
        check_vma=False,
    )
```

```python
import functools

import math
import jax
import jax.numpy as jnp
from jax import lax
from jax.experimental import pallas as pl
from jax.experimental.pallas import tpu as pltpu
from jax.sharding import PartitionSpec as P

LEVELS = 3
SWEEPS = 4
COARSE = 16
CLASSES = 8
W = 0.85
HX = 5
HL = 6
GW = 2 * HL
UNROLL = 7
H2 = 12
F32 = jnp.float32


def pairs_even(n):
    return [(i, i ^ 1) for i in range(n)]


def pairs_odd(n):
    out = []
    for i in range(1, n - 1, 2):
        out += [(i, i + 1), (i + 1, i)]
    return out


def swap_even(x, axis):
    return lax.ppermute(x, axis, pairs_even(lax.axis_size(axis)))


def swap_odd(x, axis):
    return lax.ppermute(x, axis, pairs_odd(lax.axis_size(axis)))


def swap_xor(x, axis, m):
    return lax.ppermute(x, axis, [(i, i ^ m) for i in range(lax.axis_size(axis))])


def even(axis):
    return lax.rem(lax.axis_index(axis), 2) == 0


def call(body, outs, *args, scratch=(), smem=(), hbm=(), hbm_out=False, more=(), alias=None):
    specs = [
        pl.BlockSpec(memory_space=pltpu.SMEM if i in smem else pltpu.HBM if i in hbm else pltpu.VMEM)
        for i in range(len(args))
    ]
    shapes = [jax.ShapeDtypeStruct(s, F32) if hbm_out else pltpu.VMEM(s, F32) for s in outs]
    space = pl.ANY if hbm_out else pltpu.VMEM
    spaces = [pltpu.HBM if i in hbm or i in smem else pltpu.VMEM for i in range(len(args))]
    args = [
        a if m is None or (m is pltpu.VMEM and a.dtype != F32)
        else pltpu.with_memory_space_constraint(a, m)
        for a, m in zip(args, spaces)
    ]
    limit = 4 * sum(math.prod(s) for s in scratch) + 6 * 2**20
    return pl.pallas_call(
        body,
        out_shape=shapes,
        in_specs=specs,
        out_specs=[pl.BlockSpec(memory_space=space) for _ in outs],
        scratch_shapes=[pltpu.VMEM(s, F32) for s in scratch] + list(more),
        name=getattr(body, "__name__", None) or body.func.__name__,
        compiler_params=pltpu.CompilerParams(vmem_limit_bytes=limit),
        input_output_aliases=alias or {},
    )(*args)


def lanes(rows=8):
    return lax.broadcasted_iota(jnp.int32, (rows, 128), 1)


def rot(x, shift):
    if isinstance(shift, int):
        shift = shift % 128
        if shift == 0:
            return x
    else:
        shift = lax.rem(shift + 1024, 128)
    return pltpu.roll(x, shift, 1)


def face_start(axis, total, width, want_even):
    hi = even(axis) if want_even else jnp.logical_not(even(axis))
    return jnp.where(hi, total - width, 0)


def look_up(k, table):
    acc = jnp.full(k.shape, table[0], F32)
    for i in range(1, CLASSES):
        acc = jnp.where(k == i, table[i], acc)
    return acc


def y_tiles(r_a, r_b, k, x):
    ey = even("gy")
    if r_a.shape[1] == 8:
        va, vb = r_a[x], r_b[x]
        return jnp.where(ey, vb, va), jnp.where(ey, va, vb)
    pick_of = lambda f: (f(r_a), f(r_b))
    if k == 0:
        low, high = pick_of(lambda r: r[x, 1:9]), pick_of(lambda r: r[x, 4:12])
    elif k == 1:
        low = pick_of(lambda r: r[x, 6:14])
        high = pick_of(lambda r: pltpu.roll(r[x, 8:16], 7, 0))
    else:
        low = pick_of(lambda r: pltpu.roll(r[x, 0:8], 4, 0))
        high = pick_of(lambda r: r[x, 0:8])
    return jnp.where(ey, low[1], low[0]), jnp.where(ey, high[0], high[1])


def face_kernel(src, guess, cls, table, y_a, y_b, x_out, *s):
    k_x, k_y, g_y, b_y, sems = s
    nx, ny, _ = src.shape
    p5 = face_start("gx", nx, HX, True)
    p4 = face_start("gx", nx, HX - 1, True)
    hi = [even("gy"), jnp.logical_not(even("gy"))]
    rows = [pl.multiple_of(face_start("gy", ny, 8, flag), 8) for flag in (True, False)]
    copies = [(cls.at[pl.ds(p5, HX)], k_x)]
    for i, r in enumerate(rows):
        copies.append((cls.at[:, pl.ds(r, 8)], k_y.at[i]))
        copies.append((guess.at[:, pl.ds(r, 8)], g_y.at[i]))
        copies.append((src.at[:, pl.ds(r, 8)], b_y.at[i]))
    copies.append((guess.at[pl.ds(p5, HX)], x_out.at[HX : 2 * HX]))
    copies.append((src.at[pl.ds(p4, HX - 1)], x_out.at[2 * HX : 3 * HX - 1]))
    copies = [pltpu.make_async_copy(f, t, sems.at[i]) for i, (f, t) in enumerate(copies)]
    for cp in copies:
        cp.start()
    copies[0].wait()
    for f in range(HX):
        x_out[f] = look_up(k_x[f], table)
    for i, out in ((0, y_a), (1, y_b)):
        for cp in copies[1 + 3 * i : 4 + 3 * i]:
            cp.wait()
        for x in range(nx):
            c8, v8, b8 = look_up(k_y[i, x], table), g_y[i, x], b_y[i, x]
            out[x, 8:16] = jnp.zeros((8, 128), F32)
            out[x, 0:4] = jnp.where(hi[i], b8[4:8], b8[0:4])
            out[x, 4:9] = jnp.where(hi[i], c8[3:8], c8[0:5])
            out[x, 9:14] = jnp.where(hi[i], v8[3:8], v8[0:5])
    for cp in copies[7:]:
        cp.wait()


def load_kernel(src, guess, cls, table, c_out, guess_out, src_out, k, sems):
    nx = src.shape[0]
    half = nx // 2
    copies = []
    for h in range(2):
        at = pl.ds(h * half, half)
        copies.append((cls.at[at], k.at[at]))
    for h in range(2):
        at = pl.ds(h * half, half)
        copies.append((guess.at[at], guess_out.at[at]))
        copies.append((src.at[at], src_out.at[at]))
    copies = [pltpu.make_async_copy(f, t, sems.at[i]) for i, (f, t) in enumerate(copies)]
    for cp in copies:
        cp.start()

    def plane(x, _):
        c_out[x] = look_up(k[x], table)

    for h in range(2):
        copies[h].wait()
        fine_loop(h * half, half, plane, 2)
    for cp in copies[2:]:
        cp.wait()


def zpack_kernel(na, *refs):
    arrs = refs[:na]
    r_a, r_b, z, work = refs[na:]
    nx, ny, _ = arrs[0].shape
    tiles = ny // 8 + 2
    lane = lanes()
    for k in range(na):
        for x in range(nx):
            acc = jnp.zeros((8, 128), F32)
            low, high = y_tiles(r_a, r_b, k, x)
            for t in range(tiles):
                if t == 0:
                    v = low
                elif t == tiles - 1:
                    v = high
                else:
                    v = arrs[k][x, (t - 1) * 8 : t * 8]
                g = GW * t
                acc = jnp.where((lane >= g) & (lane < g + GW), rot(v, g + HL), acc)
            work[(k * nx + x) * 8 : (k * nx + x) * 8 + 8] = acc
    mirror = select_mat(lambda o: o + (GW - 1) - 2 * lax.rem(o, GW))
    out = dot(work[...], mirror)
    for j in range(na * nx):
        z[j] = out[8 * j : 8 * j + 8]


def halo_of(z_a, z_b, i):
    ez = even("gz")
    a, b = z_a[i], z_b[i]
    within = lax.rem(lanes(), GW)
    return jnp.where(within < HL, jnp.where(ez, a, b), jnp.where(ez, b, a))


def face_list(na):
    widths = (HX, HX, HX - 1)
    return [(k, f, widths[k]) for k in range(na) for f in range(widths[k])]


def frame_list(na):
    out, row = [], 0
    for k in range(na):
        width = (HX, HX, HX - 1)[k]
        for dx in range(1, width):
            out.append((k, dx, row, width - dx))
            row += 2 * (width - dx)
    return out, -(-row // 8) * 8


def frame_rows(na):
    items, base = frame_list(na)
    return base + 8 * len(items)


def xframe_kernel(na, nx, r_a, r_b, z_a, z_b, x_out):
    items, base = frame_list(na)
    for j, (k, dx, row, w) in enumerate(items):
        p = jnp.where(even("gx"), nx - dx, dx - 1)
        low, high = y_tiles(r_a, r_b, k, p)
        x_out[row : row + w] = low[8 - w : 8]
        x_out[row + w : row + 2 * w] = high[0:w]
        x_out[base + j * 8 : base + j * 8 + 8] = halo_of(z_a, z_b, k * nx + p)


def own_offset(nsx):
    return HX * lax.axis_index("gx") if nsx == 1 else HX


def assemble_own(k, m, h, own, r_a, r_b, z_a, z_b):
    nx, ny, _ = own.shape
    off = 1 + own_offset(1)

    def one(x, _):
        low, high = y_tiles(r_a, r_b, k, x)
        m[off + x, 8:16] = low
        m[off + x, 16 : 16 + ny] = own[x]
        m[off + x, 16 + ny : 24 + ny] = high
        h[off + x] = halo_of(z_a, z_b, k * nx + x)

    fine_loop(0, nx, one, 2)


def assemble_x(na, k, m, h, nx, x1, x2):
    off = 1 + own_offset(1)
    hi = even("gx")
    ny = x1.shape[1]
    items, base = frame_list(na)
    for j, (kk, f, w) in enumerate(face_list(na)):
        if kk == k:
            p = off + jnp.where(hi, nx, -w) + f
            m[p, 8:16] = jnp.zeros((8, 128), F32)
            m[p, 16 : 16 + ny] = x1[j]
            m[p, 16 + ny : 24 + ny] = jnp.zeros((8, 128), F32)
            h[p] = jnp.zeros((8, 128), F32)
    for j, (kk, dx, row, w) in enumerate(items):
        if kk == k:
            p = off + jnp.where(hi, nx + dx - 1, -dx)
            m[p, 16 - w : 16] = x2[row : row + w]
            m[p, 16 + ny : 16 + ny + w] = x2[row + w : row + 2 * w]
            h[p] = x2[base + j * 8 : base + j * 8 + 8]


def zshift(vals, wrap=True):
    lo = lanes(vals[0].shape[0])
    down = [rot(v, 1) for v in vals]
    up = [rot(v, -1) for v in vals]
    if len(vals) == 2:
        first, last = lo == 0, lo == 127
        down = [jnp.where(first, down[1 - t], down[t]) for t in (0, 1)]
        up = [jnp.where(last, up[1 - t], up[t]) for t in (0, 1)]
    return down, up


def neighbours(refs, x, r, n):
    vals = [ref[x, pl.ds(8 + r, n)] for ref in refs]
    down, up = zshift(vals)
    out = []
    for t, ref in enumerate(refs):
        out.append(
            (
                ref[x - 1, pl.ds(8 + r, n)],
                ref[x + 1, pl.ds(8 + r, n)],
                ref[x, pl.ds(7 + r, n)],
                ref[x, pl.ds(9 + r, n)],
                down[t],
                up[t],
            )
        )
    return vals, out


def zero(*refs):
    for ref in refs:

        def one(x, _):
            ref[x] = jnp.zeros(ref.shape[1:], F32)
            return 0

        lax.fori_loop(0, ref.shape[0], one, 0)


def chunks(rows, n=8):
    return range(0, rows, n)


def build_coef(c, b, a, q, d, scale, full_lanes):
    nx, rows = c[0].shape[0] - 2, c[0].shape[1] - 16

    def plane(x, _):
        for r in chunks(rows):
            vals, nb = neighbours(c, x, r, 8)
            lane = lanes()
            for t in range(len(c)):
                six = list(nb[t])
                if full_lanes:
                    six[4] = jnp.where(lane == 0, 0.0, six[4])
                    six[5] = jnp.where(lane == 127, 0.0, six[5])
                total = 6.0 * vals[t] + (((six[0] + six[1]) + (six[2] + six[3])) + (six[4] + six[5]))
                inside = vals[t] > 0.0
                g = jnp.where(inside, W / jnp.where(inside, total, 1.0), 0.0)
                rw = pl.ds(r, 8)
                for j in range(6):
                    face = g * (vals[t] + six[j])
                    if full_lanes and j == 4:
                        face = jnp.where(lane == 0, 0.0, face)
                    if full_lanes and j == 5:
                        face = jnp.where(lane == 127, 0.0, face)
                    a[j][t][x - 1, rw] = face
                q[t][x - 1, rw] = g * ((2.0 / scale) * b[t][x, pl.ds(8 + r, 8)])
                if d is not None:
                    d[t][x - 1, rw] = total * (0.5 * scale / W)

    fine_loop(1, nx, plane, 3)


def weighted(a, vals, nb, t, x, rw):
    s = a[0][t][x - 1, rw] * nb[t][0] + a[1][t][x - 1, rw] * nb[t][1]
    u = a[2][t][x - 1, rw] * nb[t][2] + a[3][t][x - 1, rw] * nb[t][3]
    w = a[4][t][x - 1, rw] * nb[t][4] + a[5][t][x - 1, rw] * nb[t][5]
    return (s + u) + w


def sweep(src, dst, a, q, unroll=False, r0=0, rows=None):
    nx, rows = src[0].shape[0] - 2, rows or src[0].shape[1] - 16

    def plane(x, _):
        for r in range(r0, r0 + rows, 8):
            vals, nb = neighbours(src, x, r, 8)
            rw = pl.ds(r, 8)
            for t in range(len(src)):
                dst[t][x, pl.ds(8 + r, 8)] = ((1.0 - W) * vals[t] + q[t][x - 1, rw]) + weighted(
                    a, vals, nb, t, x, rw
                )

    if unroll:
        for x in range(1, nx + 1):
            plane(x, 0)
    else:
        fine_loop(1, nx, plane, UNROLL)


def copy_q(dst, q):
    def plane(x, _):
        for t in range(len(q)):
            dst[t][x + 1, 8 : 8 + q[t].shape[1]] = q[t][x]
        return 0

    lax.fori_loop(0, q[0].shape[0], plane, 0)


def residual_rows(v, b, a, d, x, r, n=8):
    vals, nb = neighbours(v, x, r, n)
    rw = pl.ds(r, n)
    return b - d[0][x - 1, rw] * (W * vals[0] - weighted(a, vals, nb, 0, x, rw))


def pick(shift_out, cols, limit):
    i = lax.broadcasted_iota(jnp.int32, (128, 128), 0)
    o = lax.broadcasted_iota(jnp.int32, (128, 128), 1)
    return jnp.where((i // 2 == o - shift_out) & (i < limit), 0.125, 0.0).astype(F32)


def dot(a, b):
    bf = jnp.bfloat16
    b = b.astype(bf)
    hi = a.astype(bf)
    rest = a - hi.astype(F32)
    mid = rest.astype(bf)
    lo = (rest - mid.astype(F32)).astype(bf)
    one = lambda p: lax.dot_general(p, b, (((1,), (0,)), ((), ())), preferred_element_type=F32)
    return one(hi) + (one(mid) + one(lo))


def half_rows(ref, r0, n):
    return ref[pl.ds(r0, n // 2, stride=2)] + ref[pl.ds(r0 + 1, n // 2, stride=2)]


def fine_loop(lo, count, plane, unroll):
    unroll = max(u for u in range(1, unroll + 2) if count % u == 0)

    def group(i, _):
        for u in range(unroll):
            plane(lo + i * unroll + u, 0)
        return 0

    lax.fori_loop(0, count // unroll, group, 0)


def fine_each(m, h, x, tiles, with_h, emit):
    lane = lanes()
    hv = h[x]
    edge = hv
    for t in tiles:
        g = GW * t
        v = m[x, 8 + 8 * t : 16 + 8 * t]
        beside = rot(hv, -(g + HL))
        down = jnp.where(lane == 0, beside, rot(v, 1))
        up = jnp.where(lane == 127, beside, rot(v, -1))
        six = (
            m[x - 1, 8 + 8 * t : 16 + 8 * t],
            m[x + 1, 8 + 8 * t : 16 + 8 * t],
            m[x, 7 + 8 * t : 15 + 8 * t],
            m[x, 9 + 8 * t : 17 + 8 * t],
            down,
            up,
        )
        emit(0, t, v, six)
        if with_h:
            edge = jnp.where((lane >= g) & (lane < g + GW), rot(v, g + HL), edge)
    if with_h:
        row = lax.broadcasted_iota(jnp.int32, (8, 128), 0)
        within = lax.rem(lane, GW)
        above, below = pltpu.roll(hv, 1, 0), pltpu.roll(hv, 7, 0)
        six = (
            h[x - 1],
            h[x + 1],
            jnp.where(row == 0, rot(above, GW), above),
            jnp.where(row == 7, rot(below, -GW), below),
            jnp.where(within == HL - 1, edge, rot(hv, -1)),
            jnp.where(within == HL, edge, rot(hv, 1)),
        )
        emit(1, 0, hv, six)


def cut(part, ref, x, t, pad):
    if part == 1:
        return (x, slice(0, 8))
    r = 8 * t + (8 if pad else 0)
    return (x, slice(r, r + 8))


def fine_coef(c, b, a, q, d, lo, count):
    tiles = range((c[0].shape[1] - 16) // 8)

    def plane(x, _):
        def emit(part, t, v, six):
            total = 6.0 * v + (((six[0] + six[1]) + (six[2] + six[3])) + (six[4] + six[5]))
            inside = v > 0.0
            g = jnp.where(inside, W / jnp.where(inside, total, 1.0), 0.0)
            at = cut(part, None, x - 1, t, False)
            for j in range(6):
                a[j][part][at] = g * (v + six[j])
            q[part][at] = g * (2.0 * b[part][cut(part, None, x, t, True)])
            if part == 0:
                d[at] = total * (0.5 / W)

        fine_each(c[0], c[1], x, tiles, True, emit)

    fine_loop(lo, count, plane, UNROLL)


def gather_sum(a, part, at, six):
    s = a[0][part][at] * six[0] + a[1][part][at] * six[1]
    u = a[2][part][at] * six[2] + a[3][part][at] * six[3]
    w = a[4][part][at] * six[4] + a[5][part][at] * six[5]
    return (s + u) + w


def fine_sweep(src, dst, a, q, lo, count):
    tiles = range((src[0].shape[1] - 16) // 8)

    def plane(x, _):
        def emit(part, t, v, six):
            at = cut(part, None, x - 1, t, False)
            dst[part][cut(part, None, x, t, True)] = (
                (1.0 - W) * v + q[part][at]
            ) + gather_sum(a, part, at, six)

        fine_each(src[0], src[1], x, tiles, True, emit)

    fine_loop(lo, count, plane, UNROLL)


def fine_residual(v, a, d, x, b_tile, put):
    def emit(part, t, val, six):
        at = cut(part, None, x - 1, t, False)
        put(t - 1, b_tile(t - 1) - d[at] * (W * val - gather_sum(a, part, at, six)))

    fine_each(v[0], v[1], x, range(1, (v[0].shape[1] - 16) // 8 - 1), False, emit)


def fine_range(nsx, nx, extra):
    off = own_offset(nsx)
    xp = nx + nsx * HX
    lo = jnp.maximum(off - extra, 0) + 1
    return lo, nx + nsx * extra


def fine_kept(xp, rows):
    m, h = (xp, rows, 128), (xp, 8, 128)
    return [(xp + 2, rows + 16, 128), (xp + 2, 8, 128)] + [m, h] * 7 + [m]


def split_kept(s):
    two = lambda i: (s[i], s[i + 1])
    return two(0), [two(2 + 2 * j) for j in range(6)], two(14), s[16]


def clear_rim(*pairs):
    for m, h in pairs:
        n, rows, _ = m.shape
        for x in (0, n - 1):
            m[x] = jnp.zeros(m.shape[1:], F32)
            h[x] = jnp.zeros(h.shape[1:], F32)

        def one(x, _):
            m[x, 0:8] = jnp.zeros((8, 128), F32)
            m[x, rows - 8 : rows] = jnp.zeros((8, 128), F32)
            return 0

        lax.fori_loop(0, n, one, 0)


def near_far():
    ix = lax.axis_index("gx")
    return 1 + (HX + 1) * ix, jnp.where(ix == 0, 16, 2)


def fine_sweeps(nx, v, w, a, q):
    for _ in range(SWEEPS - 1):
        lo, count = fine_range(1, nx, HX - 1)
        fine_sweep(w, v, a, q, lo, count)
        v, w = w, v
    return w


def fine_prep_kernel(c_own, guess, src, r_a, r_b, z_a, z_b, *s):
    c, a, q, d = split_kept(s[:17])
    b, v, w = (s[17], s[18]), (s[19], s[20]), (s[21], s[22])
    clear_rim(c, v, w)
    for k, own, (m, h) in ((0, c_own, c), (1, guess, v), (2, src, b)):
        assemble_own(k, m, h, own, r_a, r_b, z_a, z_b)
    lo, _ = near_far()
    nx = src.shape[0]
    fine_coef(c, b, a, q, d, lo, nx - 1)
    fine_sweep(v, w, a, q, lo, nx - 1)


def fine_down_kernel(c_own, src, x1, x2, *refs):
    s = refs[23:46]
    v_out, bc, y_a, y_b, xf = refs[46:51]
    pair = refs[51]
    c, a, q, d = split_kept(s[:17])
    b, v, w = (s[17], s[18]), (s[19], s[20]), (s[21], s[22])
    nx, ny, _ = src.shape
    off = 1 + own_offset(1)
    for k, (m, h) in ((0, c), (1, v), (2, b)):
        assemble_x(3, k, m, h, nx, x1, x2)
    _, lo = near_far()
    fine_coef(c, b, a, q, d, lo, HX)
    fine_sweep(v, w, a, q, lo, HX)
    v = fine_sweeps(nx, v, w, a, q)
    pb, pc = pick(0, 64, 128), pick(64, 64, 128)

    def coarse(i, _):
        x = off + 2 * i
        rs = [None] * (ny // 8)

        def first(t, val):
            rs[t] = val

        def second(t, val):
            pair[0, 8 * t : 8 * t + 8] = rs[t] + val

        for o, put in ((0, first), (1, second)):
            fine_residual(
                v, a, d, x + o, lambda t: src[2 * i + o, 8 * t : 8 * t + 8], put
            )
        for t in range(ny // 8):
            w8 = slice(8 * t, 8 * t + 8)
            pair[1, w8] = c_own[2 * i, w8] + c_own[2 * i + 1, w8]
            v_out[2 * i, w8] = v[0][x, 16 + 8 * t : 24 + 8 * t]
            v_out[2 * i + 1, w8] = v[0][x + 1, 16 + 8 * t : 24 + 8 * t]
        bc[i] = dot(half_rows(pair.at[0], 0, ny), pb) + dot(half_rows(pair.at[1], 0, ny), pc)
        return 0

    lax.fori_loop(0, nx // 2, coarse, 0)
    p5 = face_start("gx", nx, HX, True)
    for f in range(HX):
        xf[f] = v_out[p5 + f]
    for ref, flag in ((y_a, True), (y_b, False)):
        r = pl.multiple_of(face_start("gy", ny, 8, flag), 8)
        ref[...] = v_out[:, pl.ds(r, 8), :]


def join_kernel(own, other, full):
    n = own.shape[0]
    ix = lax.axis_index("gx")
    full[pl.ds(n * ix, n)] = own[...]
    full[pl.ds(n - n * ix, n)] = other[...]


def mid_rows(full, r_a, r_b, x, t, tiles):
    rows = slice((t % tiles) * 8, (t % tiles) * 8 + 8)
    if t < tiles:
        return jnp.where(even("gy"), r_b[x, rows], r_a[x, rows])
    if t >= 2 * tiles:
        return jnp.where(even("gy"), r_a[x, rows], r_b[x, rows])
    return full[x, rows]


def mid_z_kernel(full, r_a, r_b, v0, vr_a, vr_b, z_a, z_b, vz, work):
    nx, ny, _ = full.shape
    tiles = ny // 8
    ez = even("gz")
    low = lax.rem(lanes(), 64) < 32

    def pair(i, _):
        for t in range(3 * tiles):
            e = mid_rows(full, r_a, r_b, 2 * i, t, tiles)
            o = mid_rows(full, r_a, r_b, 2 * i + 1, t, tiles)
            first = jnp.where(low, e, rot(o, 32))
            last = jnp.where(low, rot(o, -32), e)
            z_a[i, t * 8 : t * 8 + 8] = jnp.where(ez, last, first)
            z_b[i, t * 8 : t * 8 + 8] = jnp.where(ez, first, last)

    fine_loop(0, nx // 2, lambda i, c: pair(i, c), 2)
    zpack_kernel(1, v0, vr_a, vr_b, vz, work)


def mid_down_kernel(full, r_a, r_b, z_a, z_b, vr_a, vr_b, vz_a, vz_b, *s):
    v1_out, c = s[0], (s[1],)
    a, q = [(s[2 + j],) for j in range(6)], (s[8],)
    v2_out, c2 = s[9], (s[10],)
    a2, q2 = [(s[11 + j],) for j in range(6)], (s[17],)
    bc3, frame = s[18], s[19]
    b, d, w = (s[20],), (s[21],), (s[22],)
    b2, d2, w2 = (s[23],), (s[24],), (s[25],)
    pair = s[26]
    xframe_kernel(1, vr_a.shape[0], vr_a, vr_b, vz_a, vz_b, frame)
    v, v2 = (v1_out,), (v2_out,)
    nx, ny, _ = full.shape
    tiles = ny // 8
    ez = even("gz")
    lane = lanes()
    own, low = lane < 64, lax.rem(lane, 64) < 32
    clear_pads(c[0], v[0], w[0], c2[0], v2[0], w2[0])

    def place(x, t, mine, side):
        rows = slice(8 + t * 8, 16 + t * 8)
        b[0][x + 1, rows] = jnp.where(own, mine, rot(side, 64))
        c[0][x + 1, rows] = jnp.where(own, rot(mine, 64), side)

    def two(i, _):
        for t in range(3 * tiles):
            za, zb = z_a[i, t * 8 : t * 8 + 8], z_b[i, t * 8 : t * 8 + 8]
            right = jnp.where(ez, za, zb)
            left = jnp.where(ez, zb, za)
            e = mid_rows(full, r_a, r_b, 2 * i, t, tiles)
            o = mid_rows(full, r_a, r_b, 2 * i + 1, t, tiles)
            place(2 * i, t, e, jnp.where(low, right, left))
            place(2 * i + 1, t, o, jnp.where(low, rot(right, -32), rot(left, 32)))

    fine_loop(0, nx // 2, two, 2)
    build_coef(c, b, a, q, d, 0.25, False)
    copy_q(w, q)
    sweep(w, v, a, q)
    sweep(v, w, a, q)
    sweep(w, v, a, q)
    rows2 = ny // 2 + 2 * H2
    r0 = ny - 2 * H2
    mat = ring_pick(96)

    def down(i, _):
        x = 1 + 2 * i
        for r in chunks(2 * rows2):
            rp = pl.ds(8 + r0 + r, 8)
            e = residual_rows(v, b[0][x, rp], a, d, x, r0 + r)
            o = residual_rows(v, b[0][x + 1, rp], a, d, x + 1, r0 + r)
            pair[0, pl.ds(r, 8)] = e + o
            pair[1, pl.ds(r, 8)] = c[0][x, rp] + c[0][x + 1, rp]
        b2[0][1 + i, 8 : 8 + rows2] = dot(half_rows(pair.at[0], 0, 2 * rows2), mat)
        c2[0][1 + i, 8 : 8 + rows2] = dot(half_rows(pair.at[1], 0, 2 * rows2), mat)

    fine_loop(0, nx // 2, down, 2)
    build_coef(c2, b2, a2, q2, d2, 0.0625, False)
    copy_q(w2, q2)
    sweep(w2, v2, a2, q2)
    sweep(v2, w2, a2, q2)
    sweep(w2, v2, a2, q2)
    n3, ny3 = nx // 4, ny // 4
    for i in range(n3):
        x = 1 + 2 * i
        for r in chunks(ny // 2):
            rp = pl.ds(8 + H2 + r, 8)
            e = residual_rows(v2, b2[0][x, rp], a2, d2, x, H2 + r)
            o = residual_rows(v2, b2[0][x + 1, rp], a2, d2, x + 1, H2 + r)
            pair[0, pl.ds(r, 8)] = e + o
            pair[1, pl.ds(r, 8)] = c2[0][x, rp] + c2[0][x + 1, rp]
        at = 32 * (i % 4)
        val = dot(half_rows(pair.at[0], 0, ny // 2), pick(at, 16, 32))
        val = val + dot(half_rows(pair.at[1], 0, ny // 2), pick(at + 16, 16, 32))
        if i % 4 == 0:
            acc = val
        else:
            acc = acc + val
        if i % 4 == 3 or i == n3 - 1:
            bc3[(i // 4) * ny3 : (i // 4 + 1) * ny3] = acc


def ring_pick(split):
    i = lax.broadcasted_iota(jnp.int32, (128, 128), 0)
    o = lax.broadcasted_iota(jnp.int32, (128, 128), 1)
    return jnp.where(o == jnp.where(i < split, i // 2, i // 2 + 64), 0.125, 0.0).astype(F32)


def clear_pads(*refs):
    for ref in refs:
        n, rows, _ = ref.shape
        for x in (0, n - 1):
            ref[x] = jnp.zeros(ref.shape[1:], F32)

        def one(x, _):
            ref[x, 0:8] = jnp.zeros((8, 128), F32)
            ref[x, rows - 8 : rows] = jnp.zeros((8, 128), F32)

        fine_loop(0, n, one, 6)


def spread(src, dst, mat, c, planes, skip, r_dst, rows, tmp):
    n = src.shape[0]
    p = dot(src, mat)
    tmp[pl.ds(0, n, stride=2)] = p
    tmp[pl.ds(1, n, stride=2)] = p
    for r in chunks(rows):
        rr = slice(r_dst + r, r_dst + r + 8)
        val = tmp[skip + r : skip + r + 8]
        for x in planes:
            dst[0][x, rr] = dst[0][x, rr] + jnp.where(c[0][x, rr] > 0.0, val, 0.0)


def select_mat(fn):
    i = lax.broadcasted_iota(jnp.int32, (128, 128), 0)
    o = lax.broadcasted_iota(jnp.int32, (128, 128), 1)
    return jnp.where(i == fn(o), 1.0, 0.0).astype(F32)


def coarse_kernel(gy, gz, blocks, *s):
    v1_in, c1 = s[0], (s[1],)
    a1, q1 = [(s[2 + j],) for j in range(6)], (s[8],)
    v2_in, c2 = s[9], (s[10],)
    a2, q2 = [(s[11 + j],) for j in range(6)], (s[17],)
    v1 = (s[18],)
    s = s[19:]
    w1, v2, w2 = (s[0],), (s[1],), (s[2],)
    c3, b3, v3, w3 = [(s[3 + i],) for i in range(4)]
    a3, q3 = [(s[7 + j],) for j in range(6)], (s[13],)
    tmp = s[14]
    iy, iz = lax.axis_index("gy"), lax.axis_index("gz")
    n3, ny3 = q3[0].shape[:2]
    yb = ny3 // gy
    lane = lanes(yb)
    zero(c3[0], v3[0], w3[0])
    for jy in range(gy):
        ky = lax.bitwise_xor(jnp.int32(jy), iy)
        blk = []
        for jz in range(gz):
            kz = lax.bitwise_xor(jnp.int32(jz), iz)
            blk.append(((kz % 2) * (gz // 2) + kz // 2) * gy + ky)
        for i in range(n3):
            rows = slice((i // 4) * yb, (i // 4 + 1) * yb)
            for ref, o in ((b3[0], 32 * (i % 4)), (c3[0], 32 * (i % 4) + 16)):
                acc = jnp.zeros((yb, 128), F32)
                for jz in range(gz):
                    acc = jnp.where(lane // 16 == jz, rot(blocks[blk[jz], rows], 16 * jz - o), acc)
                ref[1 + i, 8 + yb * jy : 8 + yb * (jy + 1)] = acc
    build_coef(c3, b3, a3, q3, None, 0.015625, False)
    copy_q(v3, q3)
    sweep(v3, w3, a3, q3, True)

    def two(_, carry):
        sweep(w3, v3, a3, q3, True)
        sweep(v3, w3, a3, q3, True)
        return carry

    lax.fori_loop(0, (COARSE - 2) // 2, two, 0)
    v2[0][...] = v2_in[...]
    v1[0][...] = v1_in[...]
    clear_pads(w1[0], w2[0])
    up = select_mat(lambda o: jnp.where(o < 96, o // 2, (o + 128) // 2))
    rows2 = q2[0].shape[1]
    skip = 16 - H2
    start = pl.multiple_of(yb * iy, 8)

    def up2(i, _):
        par = rot(w3[0][1 + i, pl.ds(start, yb + 16)], -16 * iz)
        spread(par, v2, up, c2, (1 + 2 * i, 2 + 2 * i), skip, 8, rows2, tmp)

    fine_loop(0, n3, up2, 2)

    def two2(_, carry):
        sweep(v2, w2, a2, q2)
        sweep(w2, v2, a2, q2)
        return carry

    lax.fori_loop(0, SWEEPS // 2, two2, 0)
    ny1 = 4 * yb
    r0 = ny1 - 8

    def up1(i, _):
        par = v2[0][1 + i, 8 + H2 - 4 : 8 + H2 + ny1 // 2 + 4]
        spread(par, v1, up, c1, (1 + 2 * i, 2 + 2 * i), 0, 8 + r0, ny1 + 16, tmp)

    fine_loop(0, 2 * n3, up1, 2)

    def two1(_, carry):
        sweep(v1, w1, a1, q1, False, r0, ny1 + 16)
        sweep(w1, v1, a1, q1, False, r0, ny1 + 16)
        return carry

    lax.fori_loop(0, SWEEPS // 2, two1, 0)


def spread_fine(v, c, planes, up, tmp):
    n = up.shape[0]
    for half in (0, 1):
        p = up[:, 128 * half : 128 * half + 128]
        tmp[half, pl.ds(0, n, stride=2)] = p
        tmp[half, pl.ds(1, n, stride=2)] = p
    lane = lanes()
    edge = jnp.zeros((8, 128), F32)
    for t in range(2 * n // 8):
        rows = slice(8 + 8 * t, 16 + 8 * t)
        par = tmp[0, 8 * t : 8 * t + 8]
        for x in planes:
            v[0][x, rows] = v[0][x, rows] + jnp.where(c[0][x, rows] > 0.0, par, 0.0)
        g = GW * t
        here = (lane >= g) & (lane < g + GW)
        edge = jnp.where(here, tmp[1, 8 * t : 8 * t + 8], edge)
    for x in planes:
        v[1][x] = v[1][x] + jnp.where(c[1][x] > 0.0, edge, 0.0)


def fine_up_kernel(v_own, src, vr_a, vr_b, vz_a, vz_b, x1, x2, v1, *refs):
    c, a, q, d = split_kept(refs[:17])
    sol_hbm, res_hbm = refs[17:19]
    v, w = (refs[19], refs[20]), (refs[21], refs[22])
    tmp, stage, spread, sol, res, sems = refs[23:]
    nx, ny, _ = src.shape
    off = 1 + own_offset(1)
    clear_rim(v, w)
    assemble_own(0, v[0], v[1], v_own, vr_a, vr_b, vz_a, vz_b)
    assemble_x(1, 0, v[0], v[1], nx, x1, x2)
    i = lax.broadcasted_iota(jnp.int32, (128, 256), 0)
    o = lax.broadcasted_iota(jnp.int32, (128, 256), 1)
    within = lax.rem(o - 128, GW)
    z = HL - 1 - within
    par = jnp.where(within < HL, 64 + lax.div(z, 2), 128 + lax.shift_right_arithmetic(z, 1))
    mat = jnp.where(i == jnp.where(o < 128, lax.div(o, 2), par), 1.0, 0.0).astype(F32)
    nc = v1.shape[0] - 2
    ix = lax.axis_index("gx")
    half = (ny + 16) // 2
    xp = v[0].shape[0] - 2
    count = (xp + 2) // 2
    c0 = lax.shift_right_arithmetic(nx * ix + 1 - off, 1)
    for j in range(count):
        stage[j * half : (j + 1) * half] = v1[1 + jnp.clip(c0 + j, 0, nc - 1), 4 + ny // 2 : 4 + ny // 2 + half]
    spread[...] = dot(stage[...], mat)

    def up(j, _):
        p = 2 * (c0 + j) - nx * ix + off
        start = pl.multiple_of(half * j, 8)
        spread_fine(v, c, (p, p + 1), spread[pl.ds(start, half)], tmp)
        return 0

    lax.fori_loop(0, count, up, 0)
    lo, total = fine_range(1, nx, HX - 1)
    fine_sweep(v, w, a, q, lo, total)
    v = fine_sweeps(nx, v, w, a, q)

    step = nx // 4

    def copies(i):
        at = pl.ds(i * step, step)
        return (
            pltpu.make_async_copy(sol.at[at], sol_hbm.at[at], sems.at[0, i]),
            pltpu.make_async_copy(res.at[at], res_hbm.at[at], sems.at[1, i]),
        )

    def out(x, _):
        def put(t, val):
            w8 = slice(8 * t, 8 * t + 8)
            res[x, w8] = val
            sol[x, w8] = v[0][off + x, 16 + 8 * t : 24 + 8 * t]

        fine_residual(v, a, d, off + x, lambda t: src[x, 8 * t : 8 * t + 8], put)

    for i in range(4):
        fine_loop(i * step, step, out, 2)
        for cp in copies(i):
            cp.start()
    for i in range(4):
        for cp in copies(i):
            cp.wait()


def named(fn, *args):
    out = functools.partial(fn, *args)
    out.__name__ = fn.__name__
    return out


def plain_with_halo(block, sides, width):
    for axis, dim in sides:
        count = lax.axis_size(axis)
        forward = [(i, i + 1) for i in range(count - 1)]
        backward = [(target, source) for source, target in forward]
        low = lax.ppermute(
            lax.slice_in_dim(block, block.shape[dim] - width, None, axis=dim), axis, forward
        )
        high = lax.ppermute(lax.slice_in_dim(block, 0, width, axis=dim), axis, backward)
        block = jnp.concatenate([low, block, high], axis=dim)
    return block


def plain_neighbor(padded, axis_dim, offset):
    window = [slice(1, -1), slice(1, -1), slice(1, -1)]
    window[axis_dim] = slice(1 + offset, padded.shape[axis_dim] - 1 + offset)
    return padded[tuple(window)]


def plain_apply_padded(padded_u, padded_c, level_scale):
    center_u = padded_u[1:-1, 1:-1, 1:-1]
    center_c = padded_c[1:-1, 1:-1, 1:-1]
    stencil_sum = jnp.zeros_like(center_u)
    diagonal = jnp.zeros_like(center_u)
    for axis_dim in range(3):
        for offset in (-1, 1):
            face = 0.5 * (center_c + plain_neighbor(padded_c, axis_dim, offset))
            stencil_sum = stencil_sum + face * (center_u - plain_neighbor(padded_u, axis_dim, offset))
            diagonal = diagonal + face
    return (level_scale * stencil_sum, level_scale * diagonal)


def plain_restrict(field):
    size_x, size_y, size_z = field.shape
    return field.reshape(size_x // 2, 2, size_y // 2, 2, size_z // 2, 2).mean(axis=(1, 3, 5))


def plain_prolong(field):
    size_x, size_y, size_z = field.shape
    spread = jnp.broadcast_to(field[:, None, :, None, :, None], (size_x, 2, size_y, 2, size_z, 2))
    return spread.reshape(2 * size_x, 2 * size_y, 2 * size_z)


def plain_coef_halo(coef_value):
    return plain_with_halo(coef_value, (("gx", 0), ("gy", 1), ("gz", 2)), 1)


def plain_residual_of(values, rhs_field, coef_padded, level_scale):
    padded_u = plain_with_halo(values, (("gx", 0), ("gy", 1), ("gz", 2)), 1)
    stencil_sum, diagonal = plain_apply_padded(padded_u, coef_padded, level_scale)
    return rhs_field - stencil_sum


def plain_narrow_sweeps(values, rhs_field, coef_padded, level_scale):
    for sweep_id in range(SWEEPS):
        padded_u = plain_with_halo(values, (("gx", 0), ("gy", 1), ("gz", 2)), 1)
        stencil_sum, diagonal = plain_apply_padded(padded_u, coef_padded, level_scale)
        values = values + W * (rhs_field - stencil_sum) / diagonal
    return values


def plain_smooth(values, level_id, rhs_list, padded_list):
    level_scale = 0.25**level_id
    return plain_narrow_sweeps(values, rhs_list[level_id], padded_list[level_id], level_scale)


def plain_coarse_solve(coarse_rhs, coarse_coef):
    coarse_scale = 0.25**LEVELS
    coarse_pad = plain_coef_halo(coarse_coef)

    def local_step(sweep_id, values):
        padded_u = plain_with_halo(values, (("gx", 0), ("gy", 1), ("gz", 2)), 1)
        stencil_sum, diagonal = plain_apply_padded(padded_u, coarse_pad, coarse_scale)
        return values + W * (coarse_rhs - stencil_sum) / diagonal

    return lax.fori_loop(0, COARSE, local_step, jnp.zeros_like(coarse_rhs))


def plain_body(source, first_guess, cell_classes, class_table):
    cell_coef = jnp.zeros(cell_classes.shape, jnp.float32)
    for class_id in range(CLASSES):
        cell_coef = cell_coef + jnp.where(cell_classes == class_id, class_table[class_id], 0.0)
    coef_list = [cell_coef]
    for level_id in range(LEVELS):
        coef_list.append(plain_restrict(coef_list[-1]))
    top_level = LEVELS
    padded_list = [plain_coef_halo(coef_list[level_id]) for level_id in range(top_level)]
    rhs_list = [source]
    iterate_list = []
    values = first_guess
    for level_id in range(top_level):
        level_scale = 0.25**level_id
        if level_id > 0:
            values = jnp.zeros_like(rhs_list[level_id])
        values = plain_smooth(values, level_id, rhs_list, padded_list)
        iterate_list.append(values)
        rhs_list.append(
            plain_restrict(plain_residual_of(values, rhs_list[level_id], padded_list[level_id], level_scale))
        )
    correction = plain_coarse_solve(rhs_list[LEVELS], coef_list[LEVELS])
    for level_id in reversed(range(top_level)):
        values = iterate_list[level_id] + plain_prolong(correction)
        values = plain_smooth(values, level_id, rhs_list, padded_list)
        correction = values
    final = plain_residual_of(correction, source, padded_list[0], 1.0)
    return (correction, final)


def body(source, first_guess, cell_classes, class_table):
    nx, ny, nz = source.shape
    gx, gy, gz = (lax.axis_size(n) for n in ("gx", "gy", "gz"))
    if (gx, gy, gz, nx, ny, nz) != (2, 4, 4, 16, 64, 128):
        return plain_body(source, first_guess, cell_classes, class_table)
    xp = nx + HX
    rows = ny + 16
    full = (nx, ny, 128)
    halo = (3 * nx, 8, 128)

    y_a, y_b, x1 = call(
        face_kernel,
        [(nx, 16, 128)] * 2 + [(3 * HX - 1, ny, 128)],
        source, first_guess, cell_classes, class_table,
        smem=(3,),
        hbm=(0, 1, 2),
        more=[pltpu.VMEM((HX, ny, 128), jnp.int32)]
        + [pltpu.VMEM((2, nx, 8, 128), jnp.int32)]
        + [pltpu.VMEM((2, nx, 8, 128), F32)] * 2
        + [pltpu.SemaphoreType.DMA((9,))],
    )
    x1 = swap_even(x1, "gx")
    r_a, r_b = swap_even(y_a, "gy"), swap_odd(y_b, "gy")
    own = call(
        load_kernel,
        [full, full, full],
        source, first_guess, cell_classes, class_table,
        smem=(3,),
        hbm=(0, 1, 2),
        more=[pltpu.VMEM(full, jnp.int32), pltpu.SemaphoreType.DMA((6,))],
    )
    c_own, _, source = own
    (z,) = call(named(zpack_kernel, 3), [halo], *own, r_a, r_b, scratch=[(3 * nx * 8, 128)])
    rec = (r_a, r_b, swap_even(z, "gz"), swap_odd(z, "gz"))
    (x2,) = call(named(xframe_kernel, 3, nx), [(frame_rows(3), 128)], *rec)
    x2 = swap_even(x2, "gx")
    pad = [(xp + 2, rows + 16, 128), (xp + 2, 8, 128)]
    state_shapes = fine_kept(xp, rows) + pad * 3
    state = call(fine_prep_kernel, state_shapes, *own, *rec)
    out = call(
        fine_down_kernel,
        state_shapes
        + [full, (nx // 2, ny // 2, 128), (nx, 8, 128), (nx, 8, 128), (HX, ny, 128)],
        c_own, source, x1, x2, *state,
        scratch=[(2, ny, 128)],
        alias={4 + i: i for i in range(23)},
    )
    kept = out[:17]
    v0, bc1, vy_a, vy_b, vx1 = out[23:]

    n1, ny1 = nx, ny // 2
    (f1,) = call(join_kernel, [(n1, ny1, 128)], bc1, swap_even(bc1, "gx"))
    vr_a, vr_b = swap_even(vy_a, "gy"), swap_odd(vy_b, "gy")
    vx1 = swap_even(vx1, "gx")
    r_a, r_b = swap_even(f1, "gy"), swap_odd(f1, "gy")
    rows1 = 3 * ny1
    z_a, z_b, vz = call(
        mid_z_kernel,
        [(n1 // 2, rows1, 128)] * 2 + [(nx, 8, 128)],
        f1, r_a, r_b, v0, vr_a, vr_b,
        scratch=[(nx * 8, 128)],
    )
    z_a, z_b = swap_even(z_a, "gz"), swap_odd(z_b, "gz")
    vz_a, vz_b = swap_even(vz, "gz"), swap_odd(vz, "gz")
    pad1, bare1 = (n1 + 2, rows1 + 16, 128), (n1, rows1, 128)
    n2, rows2 = n1 // 2, ny1 // 2 + 2 * H2
    pad2, bare2 = (n2 + 2, rows2 + 16, 128), (n2, rows2, 128)
    n3, yb = n1 // 4, ny1 // 4
    kept_mid = [pad1, pad1] + [bare1] * 7 + [pad2, pad2] + [bare2] * 7
    out = call(
        mid_down_kernel,
        kept_mid + [(-(-n3 // 4) * yb, 128), (frame_rows(1), 128)],
        f1, r_a, r_b, z_a, z_b, vr_a, vr_b, vz_a, vz_b,
        scratch=[pad1, bare1, pad1, pad2, bare2, pad2, (2, 2 * rows2, 128)],
    )
    kept_mid, (bc3, frame) = out[:-2], out[-2:]
    vx2 = swap_even(frame, "gx")
    vrec = (vr_a, vr_b, vz_a, vz_b)

    got = jnp.stack([bc3] + [swap_xor(bc3, "gy", m) for m in range(1, gy)])
    bit = gz // 2
    while bit:
        got = jnp.concatenate([got, swap_xor(got, "gz", bit)])
        bit //= 2

    pad3, bare3 = (n3 + 2, gy * yb + 16, 128), (n3, gy * yb, 128)
    (v1,) = call(
        named(coarse_kernel, gy, gz),
        [pad1],
        got, *kept_mid,
        scratch=[pad1, pad2, pad2] + [pad3] * 4 + [bare3] * 7 + [(2 * (ny1 + 16), 128)],
    )
    par_rows = (xp + 2) // 2 * (rows // 2)
    sol, res = call(
        fine_up_kernel,
        [full, full],
        v0, source, *vrec, vx1, vx2, v1, *kept,
        scratch=pad * 2 + [(2, rows, 128), (par_rows, 128), (par_rows, 256), full, full],
        hbm_out=True,
        more=[pltpu.SemaphoreType.DMA((2, 4))],
    )
    return sol, res


def solution(mesh):
    spec = P("gx", "gy", "gz")
    return jax.shard_map(
        body,
        mesh=mesh,
        in_specs=(spec, spec, spec, P()),
        out_specs=(spec, spec),
        check_vma=False,
    )
```
